32 devices in a mesh: row: 8 (over y, x, core), col: 4 (over z).
Axes of the slice: x: 2, y: 2, z: 4, core: 2. Of those that a mesh axis runs over, the one named last changes fastest.
Arguments:
- density: bfloat16 [4096, 4096], P('row', 'col'), as said below
- pattern: int32 [32, 32], P('row', 'col'), may hold values from 0 to 1, as said below
Outputs:
- purified: float32 [4096, 4096], P('row', 'col')
- occupation: float32 [], replicated
The draws below stay inside these ranges and needn't reach their ends.
Inputs may be any that keep to these rules, and one draw needn't show every extreme that they name: density is symmetric. pattern is symmetric, 0 or 1, with every diagonal block kept.
All inputs are finite; a program needn't handle non-finite values.
Results may differ from the reference program's by a relative error of at most 0.0047.
Values may be sent and summed in bfloat16 or wider, within the bound.
No kernel may reach another device: no remote copies, remote signals or barrier semaphores. Data moves between devices by JAX's collectives and lax.ppermute only.
A program may use at most 64 MiB of HBM per device.

```python
import math
import jax
import jax.numpy as jnp

B = 128
NB = 32
ORDER = 4096


def block_centres(key):
    spot = jax.random.fold_in(key, 7)
    return jax.random.randint(spot, (NB, 3), 0, 32)


def draw_density(key, part):
    first, second, third = jax.random.split(jax.random.fold_in(key, 11), 3)
    indices = jnp.arange(ORDER)
    position = indices.astype(jnp.float32) / ORDER
    block_ids = jnp.arange(NB)
    raw = jax.random.normal(first, (ORDER, ORDER), jnp.float32)
    level = jax.random.uniform(third, (NB, NB), jnp.float32, 0.6, 1.0)
    rough = 0.85 + 0.3 * jax.random.uniform(second, (ORDER,), jnp.float32)
    level = jnp.where(block_ids[:, None] <= block_ids[None, :], level, level.T)
    noise = (raw + raw.T) * (0.7071 / math.sqrt(ORDER))
    noise = (noise.reshape(NB, B, NB, B) * level[:, None, :, None]).reshape(ORDER, ORDER)
    diagonal = 0.05 * jnp.exp(2.302585 * position) * rough
    return jnp.where(indices[:, None] == indices[None, :], diagonal[:, None], noise).astype(jnp.bfloat16)


def draw_pattern(key, part):
    centres = block_centres(key)
    apart = jnp.abs(centres[:, None, :] - centres[None, :, :])
    apart = jnp.minimum(apart, 32 - apart)
    distance = jnp.sum(apart * apart, axis=2)
    indices = jnp.arange(NB)
    kept = (indices[:, None] == indices[None, :]) | (distance <= 196)
    return jnp.where(kept, 1, 0).astype(jnp.int32)


def setup_inputs(seed: int = 0) -> dict:
    keys = jax.random.split(jax.random.key(seed), 3)
    return {
        "density": draw_density(jax.random.fold_in(keys[2], 71), 0),
        "pattern": draw_pattern(jax.random.fold_in(keys[2], 71), 0),
    }


def filtered(values, pattern):
    blocks = values.reshape(NB, B, NB, B) * pattern.astype(jnp.float32)[:, None, :, None]
    return blocks.reshape(ORDER, ORDER)


def reference(density, pattern):
    masked = filtered(density.astype(jnp.float32), pattern).astype(jnp.bfloat16)
    squared = filtered(jnp.dot(masked, masked, preferred_element_type=jnp.float32), pattern).astype(jnp.bfloat16)
    cubic_term = filtered(jnp.dot(squared, masked, preferred_element_type=jnp.float32), pattern)
    purified = 3.0 * squared.astype(jnp.float32) - 2.0 * cubic_term
    occupation = jnp.trace(purified) / ORDER
    return purified, occupation
```

```python
import functools

import jax
import jax.numpy as jnp
from jax import lax
from jax.experimental import pallas as pl
from jax.experimental.pallas import tpu as pltpu
from jax.sharding import PartitionSpec as P

B = 128


def filtered(values, pattern):
    block_rows, block_cols = pattern.shape
    blocked = (
        values.reshape(block_rows, B, block_cols, B) * pattern.astype(jnp.float32)[:, None, :, None]
    )
    return blocked.reshape(block_rows * B, block_cols * B)


def general(density, pattern):
    masked = filtered(density.astype(jnp.float32), pattern).astype(jnp.bfloat16)
    row_count = masked.shape[0]
    col_count = masked.shape[1]
    column = lax.all_gather(masked, "row", axis=0, tiled=True)

    def multiply(factor):
        return jnp.dot(
            lax.all_gather(factor, "col", axis=1, tiled=True),
            column,
            preferred_element_type=jnp.float32,
        )

    squared = filtered(multiply(masked), pattern).astype(jnp.bfloat16)
    cubic_term = filtered(multiply(squared), pattern)
    purified = 3.0 * squared.astype(jnp.float32) - 2.0 * cubic_term
    row_index = lax.axis_index("row") * row_count + jnp.arange(row_count, dtype=jnp.int32)
    col_index = lax.axis_index("col") * col_count + jnp.arange(col_count, dtype=jnp.int32)
    diagonal_sum = jnp.sum(jnp.where(row_index[:, None] == col_index[None, :], purified, 0.0))
    total_trace = lax.psum(diagonal_sum, ("row", "col"))
    occupation = total_trace / (row_count * lax.axis_size("row"))
    return (purified, occupation)


TILE = 256


def product(refs, left, right, acc, left_sem, right_sem, where):
    lefts, rights = refs[:7], refs[7:15]
    row, col = where[0], where[1]
    for k in range(8):
        slot = row ^ k
        pltpu.make_async_copy(rights[k], right.at[slot], right_sem.at[slot]).start()
    for d in range(7):
        source = col + (0, -1, -2, -3, 1, 2, 3)[d]

        @pl.when((source >= 0) & (source < 4))
        def _():
            pltpu.make_async_copy(lefts[d], left.at[source], left_sem.at[source]).start()

    columns = right.shape[2]
    for c in range(4):
        pltpu.make_async_copy(lefts[0], left.at[c], left_sem.at[c]).wait()
        for t in range(2):
            slot = 2 * c + t
            pltpu.make_async_copy(rights[0], right.at[slot], right_sem.at[slot]).wait()

        @pl.loop(0, columns // TILE)
        def _(n):
            lanes = pl.ds(pl.multiple_of(n * TILE, TILE), TILE)
            depth = right.shape[1]
            part = jnp.dot(
                left[c, :, :depth], right[2 * c, :, lanes], preferred_element_type=jnp.float32
            ) + jnp.dot(
                left[c, :, depth:], right[2 * c + 1, :, lanes], preferred_element_type=jnp.float32
            )
            if c == 0:
                acc[:, lanes] = part
            else:
                acc[:, lanes] += part


def square_kernel(where, pattern, *refs):
    own = refs[0]
    squared_ref, sum_ref = refs[15:17]
    left, right, acc, left_sem, right_sem = refs[17:]
    product(refs, left, right, acc, left_sem, right_sem, where)
    row, col = where[0], where[1]
    rows, columns = acc.shape
    sum_ref[...] = jnp.zeros_like(sum_ref)

    @pl.loop(0, (rows // B) * (columns // B))
    def _(block):
        a = block // (columns // B)
        b = block % (columns // B)
        part = (
            pl.ds(pl.multiple_of(a * B, B), B),
            pl.ds(pl.multiple_of(b * B, B), B),
        )
        kept = pattern[a, b].astype(jnp.float32)
        squared = (acc[part] * kept).astype(jnp.bfloat16)
        squared_ref[part] = squared
        wide = squared.astype(jnp.float32)
        masked = left[col, part[0], part[1]].astype(jnp.float32)
        offset = row * rows + a * B - (col * columns + b * B)
        diagonal = (
            lax.broadcasted_iota(jnp.int32, (B, B), 0) + offset
            == lax.broadcasted_iota(jnp.int32, (B, B), 1)
        )
        term = jnp.where(diagonal, 3.0 * wide, 0.0) - 2.0 * wide * masked
        sum_ref[...] += jnp.sum(term.reshape(B // 8, 8, B), axis=0)


def cubic_kernel(where, pattern, *refs):
    purified_ref = refs[15]
    left, right, acc, left_sem, right_sem = refs[16:]
    product(refs, left, right, acc, left_sem, right_sem, where)
    col = where[1]
    rows, columns = acc.shape

    @pl.loop(0, (rows // B) * (columns // B))
    def _(block):
        a = block // (columns // B)
        b = block % (columns // B)
        part = (
            pl.ds(pl.multiple_of(a * B, B), B),
            pl.ds(pl.multiple_of(b * B, B), B),
        )
        kept = pattern[a, b].astype(jnp.float32)
        squared = left[col, part[0], part[1]].astype(jnp.float32)
        purified_ref[part] = 3.0 * squared - 2.0 * (acc[part] * kept)


def call(kernel, where, pattern, lefts, rights, outs):
    rows, columns = rights[0].shape
    anywhere = pl.BlockSpec(memory_space=pl.ANY)
    scalars = pl.BlockSpec(memory_space=pltpu.SMEM)
    whole = pl.BlockSpec(memory_space=pltpu.VMEM)
    return pl.pallas_call(
        kernel,
        out_shape=outs,
        in_specs=[scalars, scalars] + [anywhere] * 15,
        out_specs=jax.tree.map(lambda _: whole, outs),
        scratch_shapes=[
            pltpu.VMEM((4, rows, columns), jnp.bfloat16),
            pltpu.VMEM((8, rows, columns), jnp.bfloat16),
            pltpu.VMEM((rows, columns), jnp.float32),
            pltpu.SemaphoreType.DMA((4,)),
            pltpu.SemaphoreType.DMA((8,)),
        ],
        compiler_params=pltpu.CompilerParams(vmem_limit_bytes=40 << 20),
        cost_estimate=pl.CostEstimate(
            flops=2 * 8 * rows * rows * columns,
            bytes_accessed=2 * 13 * rows * columns,
            transcendentals=0,
        ),
    )(where, pattern, *lefts, *rights)


def swap(x, k):
    return lax.ppermute(x, "row", [(i, i ^ k) for i in range(8)])


def line_gather(x):
    up1 = lax.ppermute(x, "col", [(0, 1), (1, 2), (2, 3)])
    down1 = lax.ppermute(x, "col", [(3, 2), (2, 1), (1, 0)])
    up2 = lax.ppermute(up1, "col", [(1, 2), (2, 3)])
    down2 = lax.ppermute(down1, "col", [(2, 1), (1, 0)])
    up3 = lax.ppermute(up2, "col", [(2, 3)])
    down3 = lax.ppermute(down2, "col", [(1, 0)])
    return [x, up1, up2, up3, down1, down2, down3]


def column_gather(x):
    by_x = swap(x, 2)
    by_y = swap(x, 4)
    core = swap(x, 1)
    by_x_core = swap(by_x, 1)
    by_y_core = swap(by_y, 1)
    diagonal = swap(by_x, 4)
    return [x, core, by_x, by_x_core, by_y, by_y_core, diagonal, swap(diagonal, 1)]


def local(density, pattern):
    masked = filtered(density.astype(jnp.float32), pattern).astype(jnp.bfloat16)
    rows, columns = masked.shape
    where = jnp.stack([lax.axis_index("row"), lax.axis_index("col")]).astype(jnp.int32)
    lefts = line_gather(masked)
    rights = column_gather(masked)
    squared, sums = call(
        square_kernel,
        where,
        pattern,
        lefts,
        rights,
        (
            jax.ShapeDtypeStruct((rows, columns), jnp.bfloat16),
            jax.ShapeDtypeStruct((8, B), jnp.float32),
        ),
    )
    purified = call(
        cubic_kernel,
        where,
        pattern,
        line_gather(squared),
        rights,
        jax.ShapeDtypeStruct((rows, columns), jnp.float32),
    )
    total = jnp.sum(sums)
    for k in (1, 2, 4):
        total = total + swap(total, k)
    for k in (1, 2):
        total = total + lax.ppermute(total, "col", [(i, i ^ k) for i in range(4)])
    return (purified, total / (rows * lax.axis_size("row")))


def solution(mesh):
    placed = (P("row", "col"), P("row", "col"))
    body = local if (mesh.shape["row"], mesh.shape["col"]) == (8, 4) else general
    return jax.shard_map(
        body, mesh=mesh, in_specs=placed, out_specs=(P("row", "col"), P()), check_vma=False
    )
```

```python
import functools

import jax
import jax.numpy as jnp
from jax import lax
from jax.experimental import pallas as pl
from jax.experimental.pallas import tpu as pltpu
from jax.sharding import PartitionSpec as P

B = 128


def filtered(values, pattern):
    block_rows, block_cols = pattern.shape
    blocked = (
        values.reshape(block_rows, B, block_cols, B) * pattern.astype(jnp.float32)[:, None, :, None]
    )
    return blocked.reshape(block_rows * B, block_cols * B)


def general(density, pattern):
    masked = filtered(density.astype(jnp.float32), pattern).astype(jnp.bfloat16)
    row_count = masked.shape[0]
    col_count = masked.shape[1]
    column = lax.all_gather(masked, "row", axis=0, tiled=True)

    def multiply(factor):
        return jnp.dot(
            lax.all_gather(factor, "col", axis=1, tiled=True),
            column,
            preferred_element_type=jnp.float32,
        )

    squared = filtered(multiply(masked), pattern).astype(jnp.bfloat16)
    cubic_term = filtered(multiply(squared), pattern)
    purified = 3.0 * squared.astype(jnp.float32) - 2.0 * cubic_term
    row_index = lax.axis_index("row") * row_count + jnp.arange(row_count, dtype=jnp.int32)
    col_index = lax.axis_index("col") * col_count + jnp.arange(col_count, dtype=jnp.int32)
    diagonal_sum = jnp.sum(jnp.where(row_index[:, None] == col_index[None, :], purified, 0.0))
    total_trace = lax.psum(diagonal_sum, ("row", "col"))
    occupation = total_trace / (row_count * lax.axis_size("row"))
    return (purified, occupation)


TILE = 256
EXTRA = 16


def fetch_right(rights, right, sem, row):
    for k in range(8):
        slot = row ^ k
        pltpu.make_async_copy(rights[k], right.at[slot], sem.at[slot]).start()


def product(left, right, acc, left_sem, right_sem):
    rows, columns = acc.shape
    depth = right.shape[1]
    for c in range(4):
        pltpu.make_async_copy(left.at[c], left.at[c], left_sem.at[c]).wait()
        for t in range(2):
            slot = 2 * c + t
            pltpu.make_async_copy(right.at[slot], right.at[slot], right_sem.at[slot]).wait()

        @pl.loop(0, columns // TILE)
        def _(n):
            lanes = pl.ds(pl.multiple_of(n * TILE, TILE), TILE)
            part = jnp.dot(
                left[c, :rows, :depth], right[2 * c, :, lanes], preferred_element_type=jnp.float32
            ) + jnp.dot(
                left[c, :rows, depth:],
                right[2 * c + 1, :, lanes],
                preferred_element_type=jnp.float32,
            )
            if c == 0:
                acc[:, lanes] = part
            else:
                acc[:, lanes] += part


def blocks(rows, columns, body):
    @pl.loop(0, (rows // B) * (columns // B))
    def _(block):
        a = block // (columns // B)
        b = block % (columns // B)
        body(
            a,
            b,
            (pl.ds(pl.multiple_of(a * B, B), B), pl.ds(pl.multiple_of(b * B, B), B)),
        )


def square_kernel(where, pattern, *refs):
    lefts, rights = refs[:7], refs[7:15]
    squared_ref, sum_ref, left = refs[15:18]
    right, acc, left_sem, right_sem = refs[18:]
    row, col = where[0], where[1]
    rows, columns = acc.shape
    fetch_right(rights, right, right_sem, row)
    for d in range(7):
        source = col + (0, -1, -2, -3, 1, 2, 3)[d]

        @pl.when((source >= 0) & (source < 4))
        def _():
            pltpu.make_async_copy(lefts[d], left.at[source], left_sem.at[source]).start()

    product(left, right, acc, left_sem, right_sem)
    sum_ref[...] = jnp.zeros_like(sum_ref)

    def body(a, b, part):
        kept = pattern[a, b].astype(jnp.float32)
        squared = (acc[part] * kept).astype(jnp.bfloat16)
        squared_ref[part] = squared
        wide = squared.astype(jnp.float32)
        masked = left[col, part[0], part[1]].astype(jnp.float32)
        offset = row * rows + a * B - (col * columns + b * B)
        diagonal = (
            lax.broadcasted_iota(jnp.int32, (B, B), 0) + offset
            == lax.broadcasted_iota(jnp.int32, (B, B), 1)
        )
        term = jnp.where(diagonal, 3.0 * wide, 0.0) - 2.0 * wide * masked
        sum_ref[...] += jnp.sum(term.reshape(B // 8, 8, B), axis=0)

    blocks(rows, columns, body)


def turn_kernel(where, squared, same_ref, cross_ref):
    core = where[0] % 2
    half = same_ref.shape[0]

    def body(a, b, part):
        for out, h in ((same_ref, core), (cross_ref, 1 - core)):
            lanes = pl.ds(pl.multiple_of(h * half + b * B, B), B)
            out[part[1], part[0]] = squared[part[0], lanes].T

    blocks(half, half, body)


def own_square_kernel(where, panel, other, out):
    row = where[0]
    core, chip = row % 2, row // 2
    rows = out.shape[0]
    for source, h in ((panel, core), (other, 1 - core)):
        total = None
        for c in range(4):
            part = lax.dot_general(
                panel[c, :rows, :],
                source[c, :rows, :],
                (((1,), (1,)), ((), ())),
                preferred_element_type=jnp.float32,
            )
            total = part if total is None else total + part
        lanes = pl.ds(pl.multiple_of(h * rows, rows), rows)
        kept = panel[chip, rows : rows + EXTRA, lanes].astype(jnp.float32)
        for a in range(rows // B):
            out[a * B : (a + 1) * B, lanes] = (
                total[a * B : (a + 1) * B] * kept[a : a + 1]
            ).astype(jnp.bfloat16)


def cubic_kernel(where, pattern, *refs):
    own, local_square, turn1, turn2 = refs[:4]
    sides, rights = refs[4:10], refs[10:18]
    purified_ref = refs[18]
    left, right, acc, left_sem, right_sem = refs[19:]
    row, col = where[0], where[1]
    core, chip = row % 2, row // 2
    rows, columns = acc.shape
    fetch_right(rights, right, right_sem, row)
    pltpu.make_async_copy(own, left.at[col], left_sem.at[col]).start()

    @pl.when(chip != col)
    def _():
        pltpu.make_async_copy(local_square, left.at[chip], left_sem.at[chip]).start()
        place = col - (col > chip).astype(jnp.int32)
        for ref, back in ((turn1, 2), (turn2, 1)):
            index = (place + back) % 3
            source = index + (index >= chip).astype(jnp.int32)
            pltpu.make_async_copy(ref, left.at[source], left_sem.at[source]).start()

    @pl.when(chip == col)
    def _():
        for j in range(1, 4):
            source = col ^ j
            for u in range(2):
                t = core ^ u
                lanes = pl.ds(pl.multiple_of(t * rows, rows), rows)
                pltpu.make_async_copy(
                    sides[2 * (j - 1) + u], left.at[source, :, lanes], left_sem.at[source]
                ).start()

    product(left, right, acc, left_sem, right_sem)

    def body(a, b, part):
        kept = pattern[a, b].astype(jnp.float32)
        squared = left[col, part[0], part[1]].astype(jnp.float32)
        purified_ref[part] = 3.0 * squared - 2.0 * (acc[part] * kept)

    blocks(rows, columns, body)


ANYWHERE = pl.BlockSpec(memory_space=pl.ANY)
SCALARS = pl.BlockSpec(memory_space=pltpu.SMEM)
WHOLE = pl.BlockSpec(memory_space=pltpu.VMEM)


def call(kernel, specs, args, outs, scratch, flops, moved):
    return pl.pallas_call(
        kernel,
        out_shape=outs,
        in_specs=specs,
        out_specs=jax.tree.map(lambda _: WHOLE, outs),
        scratch_shapes=scratch,
        compiler_params=pltpu.CompilerParams(vmem_limit_bytes=60 << 20),
        cost_estimate=pl.CostEstimate(flops=flops, bytes_accessed=moved, transcendentals=0),
    )(*args)


def swap(x, k):
    return lax.ppermute(x, "row", [(i, i ^ k) for i in range(8)])


def line_gather(x):
    up1 = lax.ppermute(x, "col", [(0, 1), (1, 2), (2, 3)])
    down1 = lax.ppermute(x, "col", [(3, 2), (2, 1), (1, 0)])
    up2 = lax.ppermute(up1, "col", [(1, 2), (2, 3)])
    down2 = lax.ppermute(down1, "col", [(2, 1), (1, 0)])
    up3 = lax.ppermute(up2, "col", [(2, 3)])
    down3 = lax.ppermute(down2, "col", [(1, 0)])
    return [x, up1, up2, up3, down1, down2, down3]


def column_gather(x):
    by_x = swap(x, 2)
    by_y = swap(x, 4)
    core = swap(x, 1)
    by_x_core = swap(by_x, 1)
    by_y_core = swap(by_y, 1)
    diagonal = swap(by_x, 4)
    return [x, core, by_x, by_x_core, by_y, by_y_core, diagonal, swap(diagonal, 1)]


def rotate(x, step):
    pairs = []
    for row in range(8):
        planes = [c for c in range(4) if c != row // 2]
        for i in range(3):
            pairs.append((row * 4 + planes[i], row * 4 + planes[(i + step) % 3]))
    return lax.ppermute(x, ("row", "col"), pairs)


def to_corner(x, j, u):
    pairs = []
    for col in range(4):
        for core in range(2):
            source = (col ^ j) * 2 + core
            target = col * 2 + (core ^ u)
            pairs.append((source * 4 + col, target * 4 + col))
    return lax.ppermute(x, ("row", "col"), pairs)


def local(density, pattern):
    masked = filtered(density.astype(jnp.float32), pattern).astype(jnp.bfloat16)
    rows, columns = masked.shape
    row, col = lax.axis_index("row"), lax.axis_index("col")
    where = jnp.stack([row, col]).astype(jnp.int32)
    kept = jnp.repeat(pattern.astype(jnp.bfloat16), B, axis=1)
    kept = jnp.pad(kept, ((0, EXTRA - kept.shape[0]), (0, 0)))
    lefts = line_gather(jnp.concatenate([masked, kept], axis=0))
    rights = column_gather(masked)
    flops = 2 * 8 * rows * rows * columns
    moved = 2 * 13 * rows * columns
    tile = jax.ShapeDtypeStruct((rows, columns), jnp.bfloat16)
    scratch = [
        pltpu.VMEM((8, rows, columns), jnp.bfloat16),
        pltpu.VMEM((rows, columns), jnp.float32),
        pltpu.SemaphoreType.DMA((4,)),
        pltpu.SemaphoreType.DMA((8,)),
    ]
    squared, sums, panel = call(
        square_kernel,
        [SCALARS, SCALARS] + [ANYWHERE] * 15,
        (where, pattern, *lefts, *rights),
        (
            tile,
            jax.ShapeDtypeStruct((8, B), jnp.float32),
            jax.ShapeDtypeStruct((4, rows + EXTRA, columns), jnp.bfloat16),
        ),
        scratch,
        flops,
        moved,
    )
    turns = [rotate(squared, 1), rotate(squared, 2)]
    quarter = jax.ShapeDtypeStruct((rows, rows), jnp.bfloat16)
    turned = call(
        turn_kernel,
        [SCALARS, WHOLE],
        (where, squared),
        (quarter, quarter),
        [],
        0,
        4 * rows * columns,
    )
    sides = [to_corner(turned[u], j, u) for j in (1, 2, 3) for u in (0, 1)]
    local_square = call(
        own_square_kernel,
        [SCALARS, WHOLE, WHOLE],
        (where, panel, swap(panel, 1)),
        tile,
        [],
        flops,
        moved,
    )
    purified = call(
        cubic_kernel,
        [SCALARS, SCALARS] + [ANYWHERE] * 18,
        (where, pattern, squared, local_square, *turns, *sides, *rights),
        jax.ShapeDtypeStruct((rows, columns), jnp.float32),
        [pltpu.VMEM((4, rows, columns), jnp.bfloat16)] + scratch,
        flops,
        moved,
    )
    total = jnp.sum(sums)
    for k in (1, 2, 4):
        total = total + swap(total, k)
    for k in (1, 2):
        total = total + lax.ppermute(total, "col", [(i, i ^ k) for i in range(4)])
    return (purified, total / (rows * lax.axis_size("row")))


def solution(mesh):
    placed = (P("row", "col"), P("row", "col"))
    body = local if (mesh.shape["row"], mesh.shape["col"]) == (8, 4) else general
    return jax.shard_map(
        body, mesh=mesh, in_specs=placed, out_specs=(P("row", "col"), P()), check_vma=False
    )
```

```python
import jax
import jax.numpy as jnp
from jax import lax
from jax.experimental import pallas as pl
from jax.experimental.pallas import tpu as pltpu
from jax.sharding import PartitionSpec as P


B = 128


def filtered(values, pattern):
    block_rows, block_cols = pattern.shape
    blocked = (
        values.reshape(block_rows, B, block_cols, B) * pattern.astype(jnp.float32)[:, None, :, None]
    )
    return blocked.reshape(block_rows * B, block_cols * B)


def general(density, pattern):
    masked = filtered(density.astype(jnp.float32), pattern).astype(jnp.bfloat16)
    row_count = masked.shape[0]
    col_count = masked.shape[1]
    column = lax.all_gather(masked, "row", axis=0, tiled=True)

    def multiply(factor):
        return jnp.dot(
            lax.all_gather(factor, "col", axis=1, tiled=True),
            column,
            preferred_element_type=jnp.float32,
        )

    squared = filtered(multiply(masked), pattern).astype(jnp.bfloat16)
    cubic_term = filtered(multiply(squared), pattern)
    purified = 3.0 * squared.astype(jnp.float32) - 2.0 * cubic_term
    row_index = lax.axis_index("row") * row_count + jnp.arange(row_count, dtype=jnp.int32)
    col_index = lax.axis_index("col") * col_count + jnp.arange(col_count, dtype=jnp.int32)
    diagonal_sum = jnp.sum(jnp.where(row_index[:, None] == col_index[None, :], purified, 0.0))
    total_trace = lax.psum(diagonal_sum, ("row", "col"))
    occupation = total_trace / (row_count * lax.axis_size("row"))
    return (purified, occupation)


TILE = 256
EXTRA = 16


def multiply(acc, left, right, fresh):
    rows, columns = acc.shape

    @pl.loop(0, columns // TILE)
    def _(n):
        lanes = pl.ds(pl.multiple_of(n * TILE, TILE), TILE)
        part = jnp.dot(
            left[:rows, :rows], right[0, :, lanes], preferred_element_type=jnp.float32
        ) + jnp.dot(left[:rows, rows:], right[1, :, lanes], preferred_element_type=jnp.float32)
        if fresh:
            acc[:, lanes] = part
        else:
            acc[:, lanes] += part


def blocks(rows, columns, body):
    @pl.loop(0, (rows // B) * (columns // B))
    def _(block):
        a = block // (columns // B)
        b = block % (columns // B)
        body(
            a,
            b,
            (pl.ds(pl.multiple_of(a * B, B), B), pl.ds(pl.multiple_of(b * B, B), B)),
        )


def square_early_kernel(where, own, pair, middle2, outer2, *refs):
    rights = refs[:8]
    acc, panel, right, left_sem, right_sem = refs[8:]
    row, col = where[0], where[1]
    pltpu.make_async_copy(own, panel.at[0], left_sem.at[0]).start()
    pltpu.make_async_copy(pair, panel.at[1], left_sem.at[1]).start()
    inner = (col == 1) | (col == 2)

    @pl.when(inner)
    def _():
        pltpu.make_async_copy(middle2, panel.at[2], left_sem.at[2]).start()

    @pl.when(jnp.logical_not(inner))
    def _():
        pltpu.make_async_copy(outer2, panel.at[2], left_sem.at[2]).start()

    for k in range(8):
        slot = row ^ k
        pltpu.make_async_copy(rights[k], right.at[slot], right_sem.at[slot]).start()
    for d in range(3):
        slot = 2 * (col ^ d)
        pltpu.make_async_copy(panel.at[d], panel.at[d], left_sem.at[d]).wait()
        for t in range(2):
            there = right.at[slot + t]
            pltpu.make_async_copy(there, there, right_sem.at[slot + t]).wait()
        multiply(acc, panel.at[d], right.at[pl.ds(slot, 2)], d == 0)
    slot = 2 * (col ^ 3)
    for t in range(2):
        there = right.at[slot + t]
        pltpu.make_async_copy(there, there, right_sem.at[slot + t]).wait()


def square_late_kernel(where, pattern, own, acc_in, middle1, outer3, right_all, *refs):
    squared_ref, sum_ref, far, right, acc, left_sem, right_sem = refs
    row, col = where[0], where[1]
    rows, columns = acc.shape
    inner = (col == 1) | (col == 2)

    @pl.when(inner)
    def _():
        pltpu.make_async_copy(middle1, far, left_sem).start()

    @pl.when(jnp.logical_not(inner))
    def _():
        pltpu.make_async_copy(outer3, far, left_sem).start()

    fetch = pltpu.make_async_copy(right_all.at[pl.ds(2 * (col ^ 3), 2)], right, right_sem)
    fetch.start()
    pltpu.make_async_copy(far, far, left_sem).wait()
    fetch.wait()
    multiply(acc, far, right, True)
    sum_ref[...] = jnp.zeros_like(sum_ref)

    def body(a, b, part):
        kept = pattern[a, b].astype(jnp.float32)
        squared = ((acc_in[part] + acc[part]) * kept).astype(jnp.bfloat16)
        squared_ref[part] = squared
        wide = squared.astype(jnp.float32)
        masked = own[part].astype(jnp.float32)
        offset = row * rows + a * B - (col * columns + b * B)
        diagonal = (
            lax.broadcasted_iota(jnp.int32, (B, B), 0) + offset
            == lax.broadcasted_iota(jnp.int32, (B, B), 1)
        )
        term = jnp.where(diagonal, 3.0 * wide, 0.0) - 2.0 * wide * masked
        sum_ref[...] += jnp.sum(term.reshape(B // 8, 8, B), axis=0)

    blocks(rows, columns, body)


def turn_kernel(where, squared, same_ref, cross_ref):
    core = where[0] % 2
    half = same_ref.shape[0]

    def body(a, b, part):
        for out, h in ((same_ref, core), (cross_ref, 1 - core)):
            lanes = pl.ds(pl.multiple_of(h * half + b * B, B), B)
            out[part[1], part[0]] = squared[part[0], lanes].T

    blocks(half, half, body)


def own_square_kernel(where, panel, other, far, far_other, out):
    row, col = where[0], where[1]
    core, chip = row % 2, row // 2
    rows = out.shape[0]
    d = col ^ chip
    for source, last, h in ((panel, far, core), (other, far_other, 1 - core)):
        total = None
        for left, right in [(panel.at[d], source.at[d]) for d in range(3)] + [(far, last)]:
            part = lax.dot_general(
                left[:rows, :],
                right[:rows, :],
                (((1,), (1,)), ((), ())),
                preferred_element_type=jnp.float32,
            )
            total = part if total is None else total + part
        lanes = pl.ds(pl.multiple_of(h * rows, rows), rows)
        near = panel[jnp.minimum(d, 2), rows : rows + EXTRA, lanes].astype(jnp.float32)
        kept = jnp.where(d == 3, far[rows : rows + EXTRA, lanes].astype(jnp.float32), near)
        for a in range(rows // B):
            out[a * B : (a + 1) * B, lanes] = (
                total[a * B : (a + 1) * B] * kept[a : a + 1]
            ).astype(jnp.bfloat16)


def cubic_early_kernel(where, squared, local_square, right_all, acc, right, sem):
    row, col = where[0], where[1]
    chip = row // 2
    first = pltpu.make_async_copy(right_all.at[pl.ds(2 * col, 2)], right.at[0], sem.at[0])
    second = pltpu.make_async_copy(right_all.at[pl.ds(2 * chip, 2)], right.at[1], sem.at[1])
    first.start()
    second.start()
    first.wait()
    second.wait()
    multiply(acc, squared, right.at[0], True)

    @pl.when(chip != col)
    def _():
        multiply(acc, local_square, right.at[1], False)


def cubic_late_kernel(where, pattern, squared, acc_in, turn1, turn2, *refs):
    sides, right_all, purified_ref = refs[:6], refs[6], refs[7]
    left, right, acc, left_sem, right_sem = refs[8:]
    row, col = where[0], where[1]
    core, chip = row % 2, row // 2
    rows, columns = acc.shape
    corner = chip == col
    place = col - (col > chip).astype(jnp.int32)
    sources = []
    for i in range(3):
        index = (place + 2 - i) % 3
        source = jnp.where(corner, col ^ (i + 1), index + (index >= chip).astype(jnp.int32))
        sources.append(source)

    def fetch(i):
        return pltpu.make_async_copy(
            right_all.at[pl.ds(2 * sources[i], 2)], right.at[i], right_sem.at[i]
        )

    fetch(0).start()
    fetch(1).start()

    @pl.when(jnp.logical_not(corner))
    def _():
        pltpu.make_async_copy(turn1, left.at[0], left_sem.at[0]).start()
        pltpu.make_async_copy(turn2, left.at[1], left_sem.at[1]).start()

    @pl.when(corner)
    def _():
        for i in range(3):
            for u in range(2):
                lanes = pl.ds(pl.multiple_of((core ^ u) * rows, rows), rows)
                pltpu.make_async_copy(
                    sides[2 * i + u], left.at[i, :, lanes], left_sem.at[i]
                ).start()
        fetch(2).start()

    for i in range(2):
        pltpu.make_async_copy(left.at[i], left.at[i], left_sem.at[i]).wait()
        fetch(i).wait()
        multiply(acc, left.at[i], right.at[i], i == 0)

    @pl.when(corner)
    def _():
        pltpu.make_async_copy(left.at[2], left.at[2], left_sem.at[2]).wait()
        fetch(2).wait()
        multiply(acc, left.at[2], right.at[2], False)

    def body(a, b, part):
        kept = pattern[a, b].astype(jnp.float32)
        wide = squared[part].astype(jnp.float32)
        purified_ref[part] = 3.0 * wide - 2.0 * ((acc_in[part] + acc[part]) * kept)

    blocks(rows, columns, body)


ANYWHERE = pl.BlockSpec(memory_space=pl.ANY)
SCALARS = pl.BlockSpec(memory_space=pltpu.SMEM)
WHOLE = pl.BlockSpec(memory_space=pltpu.VMEM)
DMA = pltpu.SemaphoreType.DMA


def call(kernel, specs, args, outs, scratch, flops, moved):
    return pl.pallas_call(
        kernel,
        out_shape=outs,
        in_specs=specs,
        out_specs=jax.tree.map(lambda _: WHOLE, outs),
        scratch_shapes=scratch,
        compiler_params=pltpu.CompilerParams(vmem_limit_bytes=24 << 20),
        cost_estimate=pl.CostEstimate(flops=flops, bytes_accessed=moved, transcendentals=0),
    )(*args)


def swap(x, k):
    return lax.ppermute(x, "row", [(i, i ^ k) for i in range(8)])


def column_gather(x):
    by_x = swap(x, 2)
    by_y = swap(x, 4)
    core = swap(x, 1)
    by_x_core = swap(by_x, 1)
    by_y_core = swap(by_y, 1)
    diagonal = swap(by_x, 4)
    return [x, core, by_x, by_x_core, by_y, by_y_core, diagonal, swap(diagonal, 1)]


def rotate(x, step):
    pairs = []
    for row in range(8):
        planes = [c for c in range(4) if c != row // 2]
        for i in range(3):
            pairs.append((row * 4 + planes[i], row * 4 + planes[(i + step) % 3]))
    return lax.ppermute(x, ("row", "col"), pairs)


def to_corner(x, j, u):
    pairs = []
    for col in range(4):
        for core in range(2):
            source = (col ^ j) * 2 + core
            target = col * 2 + (core ^ u)
            pairs.append((source * 4 + col, target * 4 + col))
    return lax.ppermute(x, ("row", "col"), pairs)


def local(density, pattern):
    masked = filtered(density.astype(jnp.float32), pattern).astype(jnp.bfloat16)
    rows, columns = masked.shape
    row, col = lax.axis_index("row"), lax.axis_index("col")
    where = jnp.stack([row, col]).astype(jnp.int32)
    kept = jnp.repeat(pattern.astype(jnp.bfloat16), B, axis=1)
    kept = jnp.pad(kept, ((0, EXTRA - kept.shape[0]), (0, 0)))
    own = jnp.concatenate([masked, kept], axis=0)
    pair = lax.ppermute(own, "col", [(0, 1), (1, 0), (2, 3), (3, 2)])
    middle1 = lax.ppermute(own, "col", [(1, 2), (2, 1)])
    outer2 = lax.ppermute(middle1, "col", [(2, 3), (1, 0)])
    middle2 = lax.ppermute(pair, "col", [(1, 2), (2, 1)])
    outer3 = lax.ppermute(middle2, "col", [(2, 3), (1, 0)])
    rights = column_gather(masked)

    flops = 2 * 2 * rows * rows * columns
    size = 2 * rows * columns
    tile = jax.ShapeDtypeStruct((rows, columns), jnp.bfloat16)
    wide = jax.ShapeDtypeStruct((rows, columns), jnp.float32)
    extended = jax.ShapeDtypeStruct((rows + EXTRA, columns), jnp.bfloat16)
    acc = pltpu.VMEM((rows, columns), jnp.float32)
    partial, panel, right = call(
        square_early_kernel,
        [SCALARS] + [ANYWHERE] * 12,
        (where, own, pair, middle2, outer2, *rights),
        (
            wide,
            jax.ShapeDtypeStruct((3, rows + EXTRA, columns), jnp.bfloat16),
            jax.ShapeDtypeStruct((8, rows, columns), jnp.bfloat16),
        ),
        [DMA((3,)), DMA((8,))],
        3 * flops,
        24 * size,
    )
    other = swap(panel, 1)
    squared, sums, far = call(
        square_late_kernel,
        [SCALARS, SCALARS, WHOLE, WHOLE] + [ANYWHERE] * 3,
        (where, pattern, own, partial, middle1, outer3, right),
        (tile, jax.ShapeDtypeStruct((8, B), jnp.float32), extended),
        [pltpu.VMEM((2, rows, columns), jnp.bfloat16), acc, DMA(()), DMA(())],
        flops,
        8 * size,
    )
    turns = [rotate(squared, 1), rotate(squared, 2)]
    total = jnp.sum(sums)
    for k in (1, 2, 4):
        total = total + swap(total, k)
    quarter = jax.ShapeDtypeStruct((rows, rows), jnp.bfloat16)
    turned = call(
        turn_kernel,
        [SCALARS, WHOLE],
        (where, squared),
        (quarter, quarter),
        [],
        0,
        2 * size,
    )
    same, cross, total = lax.optimization_barrier((*turned, total))
    sides = [to_corner((same, cross)[u], j, u) for j in (1, 2, 3) for u in (0, 1)]
    local_square = call(
        own_square_kernel,
        [SCALARS] + [WHOLE] * 4,
        (where, panel, other, far, swap(far, 1)),
        tile,
        [],
        4 * flops,
        9 * size,
    )
    cubic = call(
        cubic_early_kernel,
        [SCALARS, WHOLE, WHOLE, ANYWHERE],
        (where, squared, local_square, right),
        wide,
        [pltpu.VMEM((2, 2, rows, columns), jnp.bfloat16), DMA((2,))],
        2 * flops,
        8 * size,
    )
    turns[0], turns[1], total = lax.optimization_barrier((*turns, total))
    for k in (1, 2):
        total = total + lax.ppermute(total, "col", [(i, i ^ k) for i in range(4)])
    purified = call(
        cubic_late_kernel,
        [SCALARS, SCALARS, WHOLE, WHOLE] + [ANYWHERE] * 9,
        (where, pattern, squared, cubic, *turns, *sides, right),
        wide,
        [
            pltpu.VMEM((3, rows, columns), jnp.bfloat16),
            pltpu.VMEM((3, 2, rows, columns), jnp.bfloat16),
            acc,
            DMA((3,)),
            DMA((3,)),
        ],
        3 * flops,
        16 * size,
    )
    return (purified, total / (rows * lax.axis_size("row")))


def solution(mesh):
    placed = (P("row", "col"), P("row", "col"))
    body = local if (mesh.shape["row"], mesh.shape["col"]) == (8, 4) else general
    return jax.shard_map(
        body, mesh=mesh, in_specs=placed, out_specs=(P("row", "col"), P()), check_vma=False
    )
```

```python
import jax
import jax.numpy as jnp
from jax import lax
from jax.experimental import pallas as pl
from jax.experimental.pallas import tpu as pltpu
from jax.sharding import PartitionSpec as P


B = 128


def filtered(values, pattern):
    block_rows, block_cols = pattern.shape
    blocked = (
        values.reshape(block_rows, B, block_cols, B) * pattern.astype(jnp.float32)[:, None, :, None]
    )
    return blocked.reshape(block_rows * B, block_cols * B)


def general(density, pattern):
    masked = filtered(density.astype(jnp.float32), pattern).astype(jnp.bfloat16)
    row_count = masked.shape[0]
    col_count = masked.shape[1]
    column = lax.all_gather(masked, "row", axis=0, tiled=True)

    def multiply(factor):
        return jnp.dot(
            lax.all_gather(factor, "col", axis=1, tiled=True),
            column,
            preferred_element_type=jnp.float32,
        )

    squared = filtered(multiply(masked), pattern).astype(jnp.bfloat16)
    cubic_term = filtered(multiply(squared), pattern)
    purified = 3.0 * squared.astype(jnp.float32) - 2.0 * cubic_term
    row_index = lax.axis_index("row") * row_count + jnp.arange(row_count, dtype=jnp.int32)
    col_index = lax.axis_index("col") * col_count + jnp.arange(col_count, dtype=jnp.int32)
    diagonal_sum = jnp.sum(jnp.where(row_index[:, None] == col_index[None, :], purified, 0.0))
    total_trace = lax.psum(diagonal_sum, ("row", "col"))
    occupation = total_trace / (row_count * lax.axis_size("row"))
    return (purified, occupation)


TILE = 256
EXTRA = 16


def multiply(acc, left, right, fresh):
    rows, columns = acc.shape

    @pl.loop(0, columns // TILE)
    def _(n):
        lanes = pl.ds(pl.multiple_of(n * TILE, TILE), TILE)
        part = jnp.dot(
            left[:rows, :rows], right[0, :, lanes], preferred_element_type=jnp.float32
        ) + jnp.dot(left[:rows, rows:], right[1, :, lanes], preferred_element_type=jnp.float32)
        if fresh:
            acc[:, lanes] = part
        else:
            acc[:, lanes] += part


def blocks(rows, columns, body):
    @pl.loop(0, (rows // B) * (columns // B))
    def _(block):
        a = block // (columns // B)
        b = block % (columns // B)
        body(
            a,
            b,
            (pl.ds(pl.multiple_of(a * B, B), B), pl.ds(pl.multiple_of(b * B, B), B)),
        )


def square_early_kernel(where, own, pair, middle2, outer2, *refs):
    rights = refs[:8]
    acc, panel, right, ahead, left_sem, right_sem, ahead_sem = refs[8:]
    row, col = where[0], where[1]
    pltpu.make_async_copy(own, panel.at[0], left_sem.at[0]).start()
    pltpu.make_async_copy(pair, panel.at[1], left_sem.at[1]).start()
    inner = (col == 1) | (col == 2)

    @pl.when(inner)
    def _():
        pltpu.make_async_copy(middle2, panel.at[2], left_sem.at[2]).start()

    @pl.when(jnp.logical_not(inner))
    def _():
        pltpu.make_async_copy(outer2, panel.at[2], left_sem.at[2]).start()

    for k in range(8):
        slot = row ^ k
        pltpu.make_async_copy(rights[k], right.at[slot], right_sem.at[slot]).start()
    slot = 2 * (col ^ 3)
    for t in range(2):
        there = right.at[slot + t]
        pltpu.make_async_copy(there, there, right_sem.at[slot + t]).wait()
    hand_over = pltpu.make_async_copy(right.at[pl.ds(slot, 2)], ahead, ahead_sem)
    hand_over.start()
    for d in range(3):
        slot = 2 * (col ^ d)
        pltpu.make_async_copy(panel.at[d], panel.at[d], left_sem.at[d]).wait()
        for t in range(2):
            there = right.at[slot + t]
            pltpu.make_async_copy(there, there, right_sem.at[slot + t]).wait()
        multiply(acc, panel.at[d], right.at[pl.ds(slot, 2)], d == 0)
    hand_over.wait()


def piece(left, right, lanes):
    rows = right.shape[1]
    return jnp.dot(
        left[:rows, :rows], right[0, :, lanes], preferred_element_type=jnp.float32
    ) + jnp.dot(left[:rows, rows:], right[1, :, lanes], preferred_element_type=jnp.float32)


def square_late_kernel(where, own, acc_in, right, middle1, outer3, *refs):
    squared_ref, sum_ref, far, left_sem = refs
    row, col = where[0], where[1]
    rows, columns = squared_ref.shape
    inner = (col == 1) | (col == 2)

    @pl.when(inner)
    def _():
        pltpu.make_async_copy(middle1, far, left_sem).start()

    @pl.when(jnp.logical_not(inner))
    def _():
        pltpu.make_async_copy(outer3, far, left_sem).start()

    pltpu.make_async_copy(far, far, left_sem).wait()
    sums = jnp.zeros((8, TILE), jnp.float32)
    for n in range(columns // TILE):
        lanes = slice(n * TILE, (n + 1) * TILE)
        total = acc_in[:, lanes] + piece(far, right, lanes)
        kept = own[rows : rows + EXTRA, lanes].astype(jnp.float32)
        for a in range(rows // B):
            part = slice(a * B, (a + 1) * B)
            squared = (total[part] * kept[a : a + 1]).astype(jnp.bfloat16)
            squared_ref[part, lanes] = squared
            term = squared.astype(jnp.float32) * own[part, lanes].astype(jnp.float32)
            sums -= 2.0 * jnp.sum(term.reshape(B // 8, 8, TILE), axis=0)
    sum_ref[...] = sums[:, :B]
    for n in range(1, TILE // B):
        sum_ref[...] += sums[:, n * B : (n + 1) * B]

    @pl.when(row // 2 == col)
    def _():
        same = lax.broadcasted_iota(jnp.int32, (B, B), 0) == lax.broadcasted_iota(
            jnp.int32, (B, B), 1
        )
        for a in range(rows // B):
            lanes = pl.ds(pl.multiple_of(row * rows - col * columns + a * B, B), B)
            squared = squared_ref[a * B : (a + 1) * B, lanes].astype(jnp.float32)
            term = jnp.where(same, 3.0 * squared, 0.0)
            sum_ref[...] += jnp.sum(term.reshape(B // 8, 8, B), axis=0)


def turn_kernel(where, squared, same_ref, cross_ref):
    core = where[0] % 2
    half = same_ref.shape[0]

    def body(a, b, part):
        for out, h in ((same_ref, core), (cross_ref, 1 - core)):
            lanes = pl.ds(pl.multiple_of(h * half + b * B, B), B)
            out[part[1], part[0]] = squared[part[0], lanes].T

    blocks(half, half, body)


def own_square_kernel(where, panel, other, far, far_other, out):
    row, col = where[0], where[1]
    core, chip = row % 2, row // 2
    rows = out.shape[0]
    d = col ^ chip
    for source, last, h in ((panel, far, core), (other, far_other, 1 - core)):
        total = None
        for left, right in [(panel.at[d], source.at[d]) for d in range(3)] + [(far, last)]:
            part = lax.dot_general(
                left[:rows, :],
                right[:rows, :],
                (((1,), (1,)), ((), ())),
                preferred_element_type=jnp.float32,
            )
            total = part if total is None else total + part
        lanes = pl.ds(pl.multiple_of(h * rows, rows), rows)
        near = panel[jnp.minimum(d, 2), rows : rows + EXTRA, lanes].astype(jnp.float32)
        kept = jnp.where(d == 3, far[rows : rows + EXTRA, lanes].astype(jnp.float32), near)
        for a in range(rows // B):
            out[a * B : (a + 1) * B, lanes] = (
                total[a * B : (a + 1) * B] * kept[a : a + 1]
            ).astype(jnp.bfloat16)


def late_sources(row, col):
    chip = row // 2
    place = col - (col > chip).astype(jnp.int32)
    sources = []
    for i in range(3):
        index = (place + 2 - i) % 3
        other = index + (index >= chip).astype(jnp.int32)
        sources.append(jnp.where(chip == col, col ^ (i + 1), other))
    return sources


def cubic_early_kernel(where, squared, local_square, right_all, acc, right, sem):
    row, col = where[0], where[1]
    chip = row // 2
    first = pltpu.make_async_copy(right_all.at[pl.ds(2 * col, 2)], right.at[0], sem.at[0])
    second = pltpu.make_async_copy(right_all.at[pl.ds(2 * chip, 2)], right.at[1], sem.at[1])
    first.start()
    second.start()
    first.wait()
    multiply(acc, squared, right.at[0], True)
    second.wait()

    @pl.when(chip != col)
    def _():
        multiply(acc, local_square, right.at[1], False)


def cubic_late_kernel(where, own, squared, acc_in, turn1, turn2, *refs):
    sides, right_all, purified_ref, left, right, sem, right_sem = (
        refs[:6],
        *refs[6:],
    )
    row, col = where[0], where[1]
    core, chip = row % 2, row // 2
    rows, columns = squared.shape
    corner = chip == col
    fetches = [
        pltpu.make_async_copy(right_all.at[pl.ds(2 * source, 2)], right.at[i], right_sem.at[i])
        for i, source in enumerate(late_sources(row, col))
    ]
    for fetch in fetches:
        fetch.start()

    def finish(lefts):
        for n in range(columns // TILE):
            lanes = slice(n * TILE, (n + 1) * TILE)
            total = acc_in[:, lanes]
            for i, ref in enumerate(lefts):
                if n == 0:
                    fetches[i].wait()
                total = total + piece(ref, right.at[i], lanes)
            kept = own[rows : rows + EXTRA, lanes].astype(jnp.float32)
            for a in range(rows // B):
                part = slice(a * B, (a + 1) * B)
                wide = squared[part, lanes].astype(jnp.float32)
                purified_ref[part, lanes] = 3.0 * wide - 2.0 * (total[part] * kept[a : a + 1])

    @pl.when(jnp.logical_not(corner))
    def _():
        finish([turn1, turn2])
        fetches[2].wait()

    @pl.when(corner)
    def _():
        for i in range(3):
            for u in range(2):
                lanes = pl.ds(pl.multiple_of((core ^ u) * rows, rows), rows)
                pltpu.make_async_copy(sides[2 * i + u], left.at[i, :, lanes], sem.at[i]).start()
        for i in range(3):
            pltpu.make_async_copy(left.at[i], left.at[i], sem.at[i]).wait()
        finish([left.at[i] for i in range(3)])


ANYWHERE = pl.BlockSpec(memory_space=pl.ANY)
AWAY = pl.BlockSpec(memory_space=pltpu.HBM)
SCALARS = pl.BlockSpec(memory_space=pltpu.SMEM)
WHOLE = pl.BlockSpec(memory_space=pltpu.VMEM)
DMA = pltpu.SemaphoreType.DMA


def call(kernel, specs, args, outs, scratch, flops, moved, grant=24):
    return pl.pallas_call(
        kernel,
        out_shape=outs,
        in_specs=specs,
        out_specs=jax.tree.map(lambda _: WHOLE, outs),
        scratch_shapes=scratch,
        compiler_params=pltpu.CompilerParams(vmem_limit_bytes=grant << 20),
        cost_estimate=pl.CostEstimate(flops=flops, bytes_accessed=moved, transcendentals=0),
    )(*args)


def swap(x, k):
    return lax.ppermute(x, "row", [(i, i ^ k) for i in range(8)])


def column_gather(x):
    by_x = swap(x, 2)
    by_y = swap(x, 4)
    core = swap(x, 1)
    by_x_core = swap(by_x, 1)
    by_y_core = swap(by_y, 1)
    diagonal = swap(by_x, 4)
    return [x, core, by_x, by_x_core, by_y, by_y_core, diagonal, swap(diagonal, 1)]


def rotate(x, step):
    pairs = []
    for row in range(8):
        planes = [c for c in range(4) if c != row // 2]
        for i in range(3):
            pairs.append((row * 4 + planes[i], row * 4 + planes[(i + step) % 3]))
    return lax.ppermute(x, ("row", "col"), pairs)


def to_corner(x, j, u):
    pairs = []
    for col in range(4):
        for core in range(2):
            source = (col ^ j) * 2 + core
            target = col * 2 + (core ^ u)
            pairs.append((source * 4 + col, target * 4 + col))
    return lax.ppermute(x, ("row", "col"), pairs)


def local(density, pattern):
    masked = filtered(density.astype(jnp.float32), pattern).astype(jnp.bfloat16)
    rows, columns = masked.shape
    row, col = lax.axis_index("row"), lax.axis_index("col")
    where = jnp.stack([row, col]).astype(jnp.int32)
    kept = jnp.repeat(pattern.astype(jnp.bfloat16), B, axis=1)
    kept = jnp.pad(kept, ((0, EXTRA - kept.shape[0]), (0, 0)))
    own = jnp.concatenate([masked, kept], axis=0)
    pair = lax.ppermute(own, "col", [(0, 1), (1, 0), (2, 3), (3, 2)])
    middle1 = lax.ppermute(own, "col", [(1, 2), (2, 1)])
    outer2 = lax.ppermute(middle1, "col", [(2, 3), (1, 0)])
    middle2 = lax.ppermute(pair, "col", [(1, 2), (2, 1)])
    outer3 = lax.ppermute(middle2, "col", [(2, 3), (1, 0)])
    rights = column_gather(masked)

    flops = 2 * 2 * rows * rows * columns
    size = 2 * rows * columns
    tile = jax.ShapeDtypeStruct((rows, columns), jnp.bfloat16)
    wide = jax.ShapeDtypeStruct((rows, columns), jnp.float32)
    extended = jax.ShapeDtypeStruct((rows + EXTRA, columns), jnp.bfloat16)
    acc = pltpu.VMEM((rows, columns), jnp.float32)
    partial, panel, right, ahead = call(
        square_early_kernel,
        [SCALARS] + [ANYWHERE] * 12,
        (where, own, pair, middle2, outer2, *rights),
        (
            wide,
            jax.ShapeDtypeStruct((3, rows + EXTRA, columns), jnp.bfloat16),
            jax.ShapeDtypeStruct((8, rows, columns), jnp.bfloat16),
            jax.ShapeDtypeStruct((2, rows, columns), jnp.bfloat16),
        ),
        [DMA((3,)), DMA((8,)), DMA(())],
        3 * flops,
        24 * size,
    )
    other = swap(panel, 1)
    squared, sums, far = call(
        square_late_kernel,
        [SCALARS, WHOLE, WHOLE, WHOLE] + [ANYWHERE] * 2,
        (where, own, partial, ahead, middle1, outer3),
        (tile, jax.ShapeDtypeStruct((8, B), jnp.float32), extended),
        [DMA(())],
        flops,
        8 * size,
    )
    turns = [rotate(squared, 1), rotate(squared, 2)]
    total = jnp.sum(sums)
    for k in (1, 2, 4):
        total = total + swap(total, k)
    quarter = jax.ShapeDtypeStruct((rows, rows), jnp.bfloat16)
    turned = call(
        turn_kernel,
        [SCALARS, WHOLE],
        (where, squared),
        (quarter, quarter),
        [],
        0,
        2 * size,
    )
    sides = [to_corner(turned[u], j, u) for j in (1, 2, 3) for u in (0, 1)]
    local_square = call(
        own_square_kernel,
        [SCALARS] + [WHOLE] * 4,
        (where, panel, other, far, swap(far, 1)),
        tile,
        [],
        4 * flops,
        9 * size,
        48,
    )
    cubic = call(
        cubic_early_kernel,
        [SCALARS, WHOLE, WHOLE, AWAY],
        (where, squared, local_square, right),
        wide,
        [pltpu.VMEM((2, 2, rows, columns), jnp.bfloat16), DMA((2,))],
        2 * flops,
        8 * size,
        48,
    )
    for k in (2, 1):
        total = total + lax.ppermute(total, "col", [(i, i ^ k) for i in range(4)])
    purified = call(
        cubic_late_kernel,
        [SCALARS] + [WHOLE] * 5 + [ANYWHERE] * 6 + [AWAY],
        (where, own, squared, cubic, *turns, *sides, right),
        wide,
        [
            pltpu.VMEM((3, rows, columns), jnp.bfloat16),
            pltpu.VMEM((3, 2, rows, columns), jnp.bfloat16),
            DMA((3,)),
            DMA((3,)),
        ],
        3 * flops,
        16 * size,
        48,
    )
    return (purified, total / (rows * lax.axis_size("row")))


def solution(mesh):
    placed = (P("row", "col"), P("row", "col"))
    body = local if (mesh.shape["row"], mesh.shape["col"]) == (8, 4) else general
    return jax.shard_map(
        body, mesh=mesh, in_specs=placed, out_specs=(P("row", "col"), P()), check_vma=False
    )
```

```python
import jax
import jax.numpy as jnp
from jax import lax
from jax.experimental import pallas as pl
from jax.experimental.pallas import tpu as pltpu
from jax.sharding import PartitionSpec as P


B = 128


def filtered(values, pattern):
    block_rows, block_cols = pattern.shape
    blocked = (
        values.reshape(block_rows, B, block_cols, B) * pattern.astype(jnp.float32)[:, None, :, None]
    )
    return blocked.reshape(block_rows * B, block_cols * B)


def general(density, pattern):
    masked = filtered(density.astype(jnp.float32), pattern).astype(jnp.bfloat16)
    row_count = masked.shape[0]
    col_count = masked.shape[1]
    column = lax.all_gather(masked, "row", axis=0, tiled=True)

    def multiply(factor):
        return jnp.dot(
            lax.all_gather(factor, "col", axis=1, tiled=True),
            column,
            preferred_element_type=jnp.float32,
        )

    squared = filtered(multiply(masked), pattern).astype(jnp.bfloat16)
    cubic_term = filtered(multiply(squared), pattern)
    purified = 3.0 * squared.astype(jnp.float32) - 2.0 * cubic_term
    row_index = lax.axis_index("row") * row_count + jnp.arange(row_count, dtype=jnp.int32)
    col_index = lax.axis_index("col") * col_count + jnp.arange(col_count, dtype=jnp.int32)
    diagonal_sum = jnp.sum(jnp.where(row_index[:, None] == col_index[None, :], purified, 0.0))
    total_trace = lax.psum(diagonal_sum, ("row", "col"))
    occupation = total_trace / (row_count * lax.axis_size("row"))
    return (purified, occupation)


NEAR = (0, 1, 3)
LAST = 2
TILE = 256
EXTRA = 16


def multiply(acc, left, right, fresh):
    rows, columns = acc.shape

    @pl.loop(0, columns // TILE)
    def _(n):
        lanes = pl.ds(pl.multiple_of(n * TILE, TILE), TILE)
        part = jnp.dot(
            left[:rows, :rows], right[0, :, lanes], preferred_element_type=jnp.float32
        ) + jnp.dot(left[:rows, rows:], right[1, :, lanes], preferred_element_type=jnp.float32)
        if fresh:
            acc[:, lanes] = part
        else:
            acc[:, lanes] += part


def blocks(rows, columns, body):
    @pl.loop(0, (rows // B) * (columns // B))
    def _(block):
        a = block // (columns // B)
        b = block % (columns // B)
        body(
            a,
            b,
            (pl.ds(pl.multiple_of(a * B, B), B), pl.ds(pl.multiple_of(b * B, B), B)),
        )


def square_early_kernel(where, own, pair, cross, *refs):
    rights = refs[:8]
    acc, panel, right, ahead, left_sem, right_sem, ahead_sem = refs[8:]
    row, col = where[0], where[1]
    for i, ref in enumerate((own, pair, cross)):
        pltpu.make_async_copy(ref, panel.at[i], left_sem.at[i]).start()

    for k in range(8):
        slot = row ^ k
        pltpu.make_async_copy(rights[k], right.at[slot], right_sem.at[slot]).start()
    slot = 2 * (col ^ LAST)
    for t in range(2):
        there = right.at[slot + t]
        pltpu.make_async_copy(there, there, right_sem.at[slot + t]).wait()
    hand_over = pltpu.make_async_copy(right.at[pl.ds(slot, 2)], ahead, ahead_sem)
    hand_over.start()
    for i, d in enumerate(NEAR):
        slot = 2 * (col ^ d)
        pltpu.make_async_copy(panel.at[i], panel.at[i], left_sem.at[i]).wait()
        for t in range(2):
            there = right.at[slot + t]
            pltpu.make_async_copy(there, there, right_sem.at[slot + t]).wait()
        multiply(acc, panel.at[i], right.at[pl.ds(slot, 2)], i == 0)
    hand_over.wait()


def piece(left, right, lanes):
    rows = right.shape[1]
    return jnp.dot(
        left[:rows, :rows], right[0, :, lanes], preferred_element_type=jnp.float32
    ) + jnp.dot(left[:rows, rows:], right[1, :, lanes], preferred_element_type=jnp.float32)


def square_late_kernel(where, own, acc_in, right, middle2, outer2, *refs):
    squared_ref, sum_ref, far, left_sem = refs
    row, col = where[0], where[1]
    rows, columns = squared_ref.shape
    inner = (col == 1) | (col == 2)

    @pl.when(inner)
    def _():
        pltpu.make_async_copy(middle2, far, left_sem).start()

    @pl.when(jnp.logical_not(inner))
    def _():
        pltpu.make_async_copy(outer2, far, left_sem).start()

    pltpu.make_async_copy(far, far, left_sem).wait()
    sums = jnp.zeros((8, TILE), jnp.float32)
    for n in range(columns // TILE):
        lanes = slice(n * TILE, (n + 1) * TILE)
        total = acc_in[:, lanes] + piece(far, right, lanes)
        kept = own[rows : rows + EXTRA, lanes].astype(jnp.float32)
        for a in range(rows // B):
            part = slice(a * B, (a + 1) * B)
            squared = (total[part] * kept[a : a + 1]).astype(jnp.bfloat16)
            squared_ref[part, lanes] = squared
            term = squared.astype(jnp.float32) * own[part, lanes].astype(jnp.float32)
            sums -= 2.0 * jnp.sum(term.reshape(B // 8, 8, TILE), axis=0)
    sum_ref[...] = sums[:, :B]
    for n in range(1, TILE // B):
        sum_ref[...] += sums[:, n * B : (n + 1) * B]

    @pl.when(row // 2 == col)
    def _():
        same = lax.broadcasted_iota(jnp.int32, (B, B), 0) == lax.broadcasted_iota(
            jnp.int32, (B, B), 1
        )
        for a in range(rows // B):
            lanes = pl.ds(pl.multiple_of(row * rows - col * columns + a * B, B), B)
            squared = squared_ref[a * B : (a + 1) * B, lanes].astype(jnp.float32)
            term = jnp.where(same, 3.0 * squared, 0.0)
            sum_ref[...] += jnp.sum(term.reshape(B // 8, 8, B), axis=0)


def turn_kernel(where, squared, same_ref, cross_ref):
    core = where[0] % 2
    half = same_ref.shape[0]

    def body(a, b, part):
        for out, h in ((same_ref, core), (cross_ref, 1 - core)):
            lanes = pl.ds(pl.multiple_of(h * half + b * B, B), B)
            out[part[1], part[0]] = squared[part[0], lanes].T

    blocks(half, half, body)


def own_square_kernel(where, panel, other, far, far_other, out):
    row, col = where[0], where[1]
    core, chip = row % 2, row // 2
    rows = out.shape[0]
    d = col ^ chip
    for source, last, h in ((panel, far, core), (other, far_other, 1 - core)):
        total = None
        for left, right in [(panel.at[i], source.at[i]) for i in range(3)] + [(far, last)]:
            part = lax.dot_general(
                left[:rows, :],
                right[:rows, :],
                (((1,), (1,)), ((), ())),
                preferred_element_type=jnp.float32,
            )
            total = part if total is None else total + part
        lanes = pl.ds(pl.multiple_of(h * rows, rows), rows)
        near = panel[jnp.minimum(d, 2), rows : rows + EXTRA, lanes].astype(jnp.float32)
        kept = jnp.where(d == LAST, far[rows : rows + EXTRA, lanes].astype(jnp.float32), near)
        for a in range(rows // B):
            out[a * B : (a + 1) * B, lanes] = (
                total[a * B : (a + 1) * B] * kept[a : a + 1]
            ).astype(jnp.bfloat16)


def late_sources(row, col):
    chip = row // 2
    place = col - (col > chip).astype(jnp.int32)
    sources = []
    for i in range(3):
        index = (place + 2 - i) % 3
        other = index + (index >= chip).astype(jnp.int32)
        sources.append(jnp.where(chip == col, col ^ (i + 1), other))
    return sources


def cubic_early_kernel(where, squared, local_square, right_all, acc, right, sem):
    row, col = where[0], where[1]
    chip = row // 2
    first = pltpu.make_async_copy(right_all.at[pl.ds(2 * col, 2)], right.at[0], sem.at[0])
    second = pltpu.make_async_copy(right_all.at[pl.ds(2 * chip, 2)], right.at[1], sem.at[1])
    first.start()
    second.start()
    first.wait()
    multiply(acc, squared, right.at[0], True)
    second.wait()

    @pl.when(chip != col)
    def _():
        multiply(acc, local_square, right.at[1], False)


def cubic_late_kernel(where, own, squared, acc_in, turn1, turn2, *refs):
    sides = refs[:6]
    right_all, purified_ref, left, right, acc, sem, right_sem = refs[6:]
    row, col = where[0], where[1]
    core, chip = row % 2, row // 2
    rows, columns = squared.shape
    corner = chip == col
    fetches = [
        pltpu.make_async_copy(right_all.at[pl.ds(2 * source, 2)], right.at[i], right_sem.at[i])
        for i, source in enumerate(late_sources(row, col))
    ]
    fetches[0].start()
    fetches[1].start()

    def finish(last):
        for n in range(columns // TILE):
            lanes = slice(n * TILE, (n + 1) * TILE)
            total = acc_in[:, lanes] + acc[:, lanes] + piece(last, right.at[1], lanes)
            kept = own[rows : rows + EXTRA, lanes].astype(jnp.float32)
            for a in range(rows // B):
                part = slice(a * B, (a + 1) * B)
                wide = squared[part, lanes].astype(jnp.float32)
                purified_ref[part, lanes] = 3.0 * wide - 2.0 * (total[part] * kept[a : a + 1])

    @pl.when(jnp.logical_not(corner))
    def _():
        fetches[0].wait()
        multiply(acc, turn1, right.at[0], True)
        fetches[1].wait()
        finish(turn2)

    @pl.when(corner)
    def _():
        fetches[2].start()
        for i in range(3):
            for u in range(2):
                lanes = pl.ds(pl.multiple_of((core ^ u) * rows, rows), rows)
                pltpu.make_async_copy(sides[2 * i + u], left.at[i, :, lanes], sem.at[i]).start()
        for i in (0, 2, 1):
            pltpu.make_async_copy(left.at[i], left.at[i], sem.at[i]).wait()
            fetches[i].wait()
            if i != 1:
                multiply(acc, left.at[i], right.at[i], i == 0)
        finish(left.at[1])


ANYWHERE = pl.BlockSpec(memory_space=pl.ANY)
AWAY = pl.BlockSpec(memory_space=pltpu.HBM)
SCALARS = pl.BlockSpec(memory_space=pltpu.SMEM)
WHOLE = pl.BlockSpec(memory_space=pltpu.VMEM)
DMA = pltpu.SemaphoreType.DMA


def call(kernel, specs, args, outs, scratch, flops, moved, grant=24):
    return pl.pallas_call(
        kernel,
        out_shape=outs,
        in_specs=specs,
        out_specs=jax.tree.map(lambda _: WHOLE, outs),
        scratch_shapes=scratch,
        compiler_params=pltpu.CompilerParams(vmem_limit_bytes=grant << 20),
        cost_estimate=pl.CostEstimate(flops=flops, bytes_accessed=moved, transcendentals=0),
    )(*args)


def swap(x, k):
    return lax.ppermute(x, "row", [(i, i ^ k) for i in range(8)])


def column_gather(x):
    by_x = swap(x, 2)
    by_y = swap(x, 4)
    core = swap(x, 1)
    by_x_core = swap(by_x, 1)
    by_y_core = swap(by_y, 1)
    diagonal = swap(by_x, 4)
    return [x, core, by_x, by_x_core, by_y, by_y_core, diagonal, swap(diagonal, 1)]


def rotate(x, step):
    pairs = []
    for row in range(8):
        planes = [c for c in range(4) if c != row // 2]
        for i in range(3):
            pairs.append((row * 4 + planes[i], row * 4 + planes[(i + step) % 3]))
    return lax.ppermute(x, ("row", "col"), pairs)


def in_plane(x, source, target, u):
    pairs = []
    for col in range(4):
        for core in range(2):
            here = (col ^ source) * 2 + core
            there = (col ^ target) * 2 + (core ^ u)
            pairs.append((here * 4 + col, there * 4 + col))
    return lax.ppermute(x, ("row", "col"), pairs)


def to_corner(same, cross):
    by_y = [in_plane(same, 2, 0, 0), in_plane(cross, 2, 0, 1)]
    half_way = in_plane(cross, 3, 1, 0)
    by_x = [in_plane(same, 1, 0, 0), in_plane(cross, 1, 0, 1)]
    direct = in_plane(same, 3, 0, 0)
    return [*by_x, *by_y, direct, in_plane(half_way, 1, 0, 1)]


def local(density, pattern):
    masked = filtered(density.astype(jnp.float32), pattern).astype(jnp.bfloat16)
    rows, columns = masked.shape
    row, col = lax.axis_index("row"), lax.axis_index("col")
    where = jnp.stack([row, col]).astype(jnp.int32)
    kept = jnp.repeat(pattern.astype(jnp.bfloat16), B, axis=1)
    kept = jnp.pad(kept, ((0, EXTRA - kept.shape[0]), (0, 0)))
    own = jnp.concatenate([masked, kept], axis=0)
    pair = lax.ppermute(own, "col", [(i, i ^ 1) for i in range(4)])
    cross = lax.ppermute(own, "col", [(i, i ^ 3) for i in range(4)])
    middle2 = lax.ppermute(pair, "col", [(1, 2), (2, 1)])
    outer2 = lax.ppermute(cross, "col", [(2, 3), (1, 0)])
    rights = column_gather(masked)

    flops = 2 * 2 * rows * rows * columns
    size = 2 * rows * columns
    tile = jax.ShapeDtypeStruct((rows, columns), jnp.bfloat16)
    wide = jax.ShapeDtypeStruct((rows, columns), jnp.float32)
    extended = jax.ShapeDtypeStruct((rows + EXTRA, columns), jnp.bfloat16)
    acc = pltpu.VMEM((rows, columns), jnp.float32)
    partial, panel, right, ahead = call(
        square_early_kernel,
        [SCALARS] + [ANYWHERE] * 11,
        (where, own, pair, cross, *rights),
        (
            wide,
            jax.ShapeDtypeStruct((3, rows + EXTRA, columns), jnp.bfloat16),
            jax.ShapeDtypeStruct((8, rows, columns), jnp.bfloat16),
            jax.ShapeDtypeStruct((2, rows, columns), jnp.bfloat16),
        ),
        [DMA((3,)), DMA((8,)), DMA(())],
        3 * flops,
        24 * size,
    )
    other = swap(panel, 1)
    squared, sums, far = call(
        square_late_kernel,
        [SCALARS, WHOLE, WHOLE, WHOLE] + [ANYWHERE] * 2,
        (where, own, partial, ahead, middle2, outer2),
        (tile, jax.ShapeDtypeStruct((8, B), jnp.float32), extended),
        [DMA(())],
        flops,
        8 * size,
    )
    turns = [rotate(squared, 1), rotate(squared, 2)]
    total = jnp.sum(sums)
    for k in (1, 4, 2):
        total = total + swap(total, k)
    quarter = jax.ShapeDtypeStruct((rows, rows), jnp.bfloat16)
    turned = call(
        turn_kernel,
        [SCALARS, WHOLE],
        (where, squared),
        (quarter, quarter),
        [],
        0,
        2 * size,
    )
    sides = to_corner(*turned)
    local_square = call(
        own_square_kernel,
        [SCALARS] + [WHOLE] * 4,
        (where, panel, other, far, swap(far, 1)),
        tile,
        [],
        4 * flops,
        9 * size,
        48,
    )
    cubic = call(
        cubic_early_kernel,
        [SCALARS, WHOLE, WHOLE, AWAY],
        (where, squared, local_square, right),
        wide,
        [pltpu.VMEM((2, 2, rows, columns), jnp.bfloat16), DMA((2,))],
        2 * flops,
        8 * size,
        48,
    )
    for k in (2, 1):
        total = total + lax.ppermute(total, "col", [(i, i ^ k) for i in range(4)])
    purified = call(
        cubic_late_kernel,
        [SCALARS] + [WHOLE] * 5 + [ANYWHERE] * 6 + [AWAY],
        (where, own, squared, cubic, *turns, *sides, right),
        wide,
        [
            pltpu.VMEM((3, rows, columns), jnp.bfloat16),
            pltpu.VMEM((3, 2, rows, columns), jnp.bfloat16),
            acc,
            DMA((3,)),
            DMA((3,)),
        ],
        3 * flops,
        16 * size,
        48,
    )
    return (purified, total / (rows * lax.axis_size("row")))


def solution(mesh):
    placed = (P("row", "col"), P("row", "col"))
    body = local if (mesh.shape["row"], mesh.shape["col"]) == (8, 4) else general
    return jax.shard_map(
        body, mesh=mesh, in_specs=placed, out_specs=(P("row", "col"), P()), check_vma=False
    )
```

```python
import jax
import jax.numpy as jnp
from jax import lax
from jax.experimental import pallas as pl
from jax.experimental.pallas import tpu as pltpu
from jax.sharding import PartitionSpec as P


B = 128


def filtered(values, pattern):
    block_rows, block_cols = pattern.shape
    blocked = (
        values.reshape(block_rows, B, block_cols, B) * pattern.astype(jnp.float32)[:, None, :, None]
    )
    return blocked.reshape(block_rows * B, block_cols * B)


def general(density, pattern):
    masked = filtered(density.astype(jnp.float32), pattern).astype(jnp.bfloat16)
    row_count = masked.shape[0]
    col_count = masked.shape[1]
    column = lax.all_gather(masked, "row", axis=0, tiled=True)

    def multiply(factor):
        return jnp.dot(
            lax.all_gather(factor, "col", axis=1, tiled=True),
            column,
            preferred_element_type=jnp.float32,
        )

    squared = filtered(multiply(masked), pattern).astype(jnp.bfloat16)
    cubic_term = filtered(multiply(squared), pattern)
    purified = 3.0 * squared.astype(jnp.float32) - 2.0 * cubic_term
    row_index = lax.axis_index("row") * row_count + jnp.arange(row_count, dtype=jnp.int32)
    col_index = lax.axis_index("col") * col_count + jnp.arange(col_count, dtype=jnp.int32)
    diagonal_sum = jnp.sum(jnp.where(row_index[:, None] == col_index[None, :], purified, 0.0))
    total_trace = lax.psum(diagonal_sum, ("row", "col"))
    occupation = total_trace / (row_count * lax.axis_size("row"))
    return (purified, occupation)


NEAR = (0, 1, 3)
LAST = 2
TILE = 256
EXTRA = 16


def multiply(acc, left, right, fresh):
    rows, columns = acc.shape

    @pl.loop(0, columns // TILE)
    def _(n):
        lanes = pl.ds(pl.multiple_of(n * TILE, TILE), TILE)
        part = jnp.dot(
            left[:rows, :rows], right[0, :, lanes], preferred_element_type=jnp.float32
        ) + jnp.dot(left[:rows, rows:], right[1, :, lanes], preferred_element_type=jnp.float32)
        if fresh:
            acc[:, lanes] = part
        else:
            acc[:, lanes] += part


def blocks(rows, columns, body):
    @pl.loop(0, (rows // B) * (columns // B))
    def _(block):
        a = block // (columns // B)
        b = block % (columns // B)
        body(
            a,
            b,
            (pl.ds(pl.multiple_of(a * B, B), B), pl.ds(pl.multiple_of(b * B, B), B)),
        )


def square_early_kernel(where, own, pair, cross, *refs):
    rights = refs[:8]
    acc, panel, right, ahead, left_sem, right_sem, ahead_sem = refs[8:]
    row, col = where[0], where[1]
    for i, ref in enumerate((own, pair, cross)):
        pltpu.make_async_copy(ref, panel.at[i], left_sem.at[i]).start()

    for k in range(8):
        slot = row ^ k
        pltpu.make_async_copy(rights[k], right.at[slot], right_sem.at[slot]).start()
    slot = 2 * (col ^ LAST)
    for t in range(2):
        there = right.at[slot + t]
        pltpu.make_async_copy(there, there, right_sem.at[slot + t]).wait()
    hand_over = pltpu.make_async_copy(right.at[pl.ds(slot, 2)], ahead, ahead_sem)
    hand_over.start()
    for i, d in enumerate(NEAR):
        slot = 2 * (col ^ d)
        pltpu.make_async_copy(panel.at[i], panel.at[i], left_sem.at[i]).wait()
        for t in range(2):
            there = right.at[slot + t]
            pltpu.make_async_copy(there, there, right_sem.at[slot + t]).wait()
        multiply(acc, panel.at[i], right.at[pl.ds(slot, 2)], i == 0)
    hand_over.wait()


def piece(left, right, lanes):
    rows = right.shape[1]
    return jnp.dot(
        left[:rows, :rows], right[0, :, lanes], preferred_element_type=jnp.float32
    ) + jnp.dot(left[:rows, rows:], right[1, :, lanes], preferred_element_type=jnp.float32)


def square_late_kernel(where, own, acc_in, right, middle2, outer2, *refs):
    squared_ref, sum_ref, far, left_sem = refs
    row, col = where[0], where[1]
    rows, columns = squared_ref.shape
    inner = (col == 1) | (col == 2)

    @pl.when(inner)
    def _():
        pltpu.make_async_copy(middle2, far, left_sem).start()

    @pl.when(jnp.logical_not(inner))
    def _():
        pltpu.make_async_copy(outer2, far, left_sem).start()

    pltpu.make_async_copy(far, far, left_sem).wait()
    sums = jnp.zeros((8, TILE), jnp.float32)
    for n in range(columns // TILE):
        lanes = slice(n * TILE, (n + 1) * TILE)
        total = acc_in[:, lanes] + piece(far, right, lanes)
        kept = own[rows : rows + EXTRA, lanes].astype(jnp.float32)
        for a in range(rows // B):
            part = slice(a * B, (a + 1) * B)
            squared = (total[part] * kept[a : a + 1]).astype(jnp.bfloat16)
            squared_ref[part, lanes] = squared
            term = squared.astype(jnp.float32) * own[part, lanes].astype(jnp.float32)
            sums -= 2.0 * jnp.sum(term.reshape(B // 8, 8, TILE), axis=0)
    sum_ref[...] = sums[:, :B]
    for n in range(1, TILE // B):
        sum_ref[...] += sums[:, n * B : (n + 1) * B]

    @pl.when(row // 2 == col)
    def _():
        same = lax.broadcasted_iota(jnp.int32, (B, B), 0) == lax.broadcasted_iota(
            jnp.int32, (B, B), 1
        )
        for a in range(rows // B):
            lanes = pl.ds(pl.multiple_of(row * rows - col * columns + a * B, B), B)
            squared = squared_ref[a * B : (a + 1) * B, lanes].astype(jnp.float32)
            term = jnp.where(same, 3.0 * squared, 0.0)
            sum_ref[...] += jnp.sum(term.reshape(B // 8, 8, B), axis=0)


def turn_kernel(where, squared, same_ref, cross_ref):
    core = where[0] % 2
    half = same_ref.shape[0]

    def body(a, b, part):
        for out, h in ((same_ref, core), (cross_ref, 1 - core)):
            lanes = pl.ds(pl.multiple_of(h * half + b * B, B), B)
            out[part[1], part[0]] = squared[part[0], lanes].T

    blocks(half, half, body)


def own_square_kernel(where, panel, other, far, far_other, out):
    row, col = where[0], where[1]
    core, chip = row % 2, row // 2
    rows = out.shape[0]
    d = col ^ chip
    for source, last, h in ((panel, far, core), (other, far_other, 1 - core)):
        total = None
        for left, right in [(panel.at[i], source.at[i]) for i in range(3)] + [(far, last)]:
            part = lax.dot_general(
                left[:rows, :],
                right[:rows, :],
                (((1,), (1,)), ((), ())),
                preferred_element_type=jnp.float32,
            )
            total = part if total is None else total + part
        lanes = pl.ds(pl.multiple_of(h * rows, rows), rows)
        near = panel[jnp.minimum(d, 2), rows : rows + EXTRA, lanes].astype(jnp.float32)
        kept = jnp.where(d == LAST, far[rows : rows + EXTRA, lanes].astype(jnp.float32), near)
        for a in range(rows // B):
            out[a * B : (a + 1) * B, lanes] = (
                total[a * B : (a + 1) * B] * kept[a : a + 1]
            ).astype(jnp.bfloat16)


def late_sources(row, col):
    chip = row // 2
    place = col - (col > chip).astype(jnp.int32)
    sources = []
    for i in range(3):
        index = (place + 2 - i) % 3
        other = index + (index >= chip).astype(jnp.int32)
        sources.append(jnp.where(chip == col, col ^ (i + 1), other))
    return sources


def cubic_early_kernel(where, squared, local_square, right_all, acc, right, sem):
    row, col = where[0], where[1]
    chip = row // 2
    first = pltpu.make_async_copy(right_all.at[pl.ds(2 * col, 2)], right.at[0], sem.at[0])
    second = pltpu.make_async_copy(right_all.at[pl.ds(2 * chip, 2)], right.at[1], sem.at[1])
    first.start()
    second.start()
    first.wait()
    multiply(acc, squared, right.at[0], True)
    second.wait()

    @pl.when(chip != col)
    def _():
        multiply(acc, local_square, right.at[1], False)


def load_side(pieces, left, sem, core):
    for u, ref in enumerate(pieces):
        half = ref.shape[0]
        lanes = pl.ds(pl.multiple_of((core ^ u) * half, half), half)
        pltpu.make_async_copy(ref, left.at[:, lanes], sem).start()


def fetch_right(right_all, source, right, sem):
    return pltpu.make_async_copy(right_all.at[pl.ds(2 * source, 2)], right, sem)


def cubic_middle_kernel(where, acc_in, turn, *refs):
    sides, right_all, acc, left, right, sem, right_sem = refs[:4], *refs[4:]
    row, col = where[0], where[1]
    corner = row // 2 == col
    sources = late_sources(row, col)
    first = fetch_right(right_all, sources[0], right.at[0], right_sem.at[0])
    second = fetch_right(right_all, sources[1], right.at[1], right_sem.at[1])
    first.start()
    acc[...] = acc_in[...]

    @pl.when(jnp.logical_not(corner))
    def _():
        first.wait()
        multiply(acc, turn, right.at[0], False)

    @pl.when(corner)
    def _():
        second.start()
        for i in range(2):
            load_side(sides[2 * i : 2 * i + 2], left.at[i], sem.at[i], row % 2)
        for i, fetch in enumerate((first, second)):
            pltpu.make_async_copy(left.at[i], left.at[i], sem.at[i]).wait()
            fetch.wait()
            multiply(acc, left.at[i], right.at[i], False)


def cubic_late_kernel(where, own, squared, acc, turn, *refs):
    sides, right_all, purified_ref, left, right, sem, right_sem = refs[:2], *refs[2:]
    row, col = where[0], where[1]
    rows, columns = squared.shape
    corner = row // 2 == col
    sources = late_sources(row, col)
    fetch = fetch_right(
        right_all, jnp.where(corner, sources[2], sources[1]), right, right_sem
    )
    fetch.start()

    def finish(last):
        for n in range(columns // TILE):
            lanes = slice(n * TILE, (n + 1) * TILE)
            total = acc[:, lanes] + piece(last, right, lanes)
            kept = own[rows : rows + EXTRA, lanes].astype(jnp.float32)
            for a in range(rows // B):
                part = slice(a * B, (a + 1) * B)
                wide = squared[part, lanes].astype(jnp.float32)
                purified_ref[part, lanes] = 3.0 * wide - 2.0 * (total[part] * kept[a : a + 1])

    @pl.when(jnp.logical_not(corner))
    def _():
        fetch.wait()
        finish(turn)

    @pl.when(corner)
    def _():
        load_side(sides, left, sem, row % 2)
        pltpu.make_async_copy(left, left, sem).wait()
        fetch.wait()
        finish(left)


ANYWHERE = pl.BlockSpec(memory_space=pl.ANY)
AWAY = pl.BlockSpec(memory_space=pltpu.HBM)
SCALARS = pl.BlockSpec(memory_space=pltpu.SMEM)
WHOLE = pl.BlockSpec(memory_space=pltpu.VMEM)
DMA = pltpu.SemaphoreType.DMA


def call(kernel, specs, args, outs, scratch, flops, moved, grant=24):
    return pl.pallas_call(
        kernel,
        out_shape=outs,
        in_specs=specs,
        out_specs=jax.tree.map(lambda _: WHOLE, outs),
        scratch_shapes=scratch,
        compiler_params=pltpu.CompilerParams(vmem_limit_bytes=grant << 20),
        cost_estimate=pl.CostEstimate(flops=flops, bytes_accessed=moved, transcendentals=0),
    )(*args)


def swap(x, k):
    return lax.ppermute(x, "row", [(i, i ^ k) for i in range(8)])


def column_gather(x):
    by_x = swap(x, 2)
    by_y = swap(x, 4)
    core = swap(x, 1)
    by_x_core = swap(by_x, 1)
    by_y_core = swap(by_y, 1)
    diagonal = swap(by_x, 4)
    return [x, core, by_x, by_x_core, by_y, by_y_core, diagonal, swap(diagonal, 1)]


def rotate(x, step):
    pairs = []
    for row in range(8):
        planes = [c for c in range(4) if c != row // 2]
        for i in range(3):
            pairs.append((row * 4 + planes[i], row * 4 + planes[(i + step) % 3]))
    return lax.ppermute(x, ("row", "col"), pairs)


def in_plane(x, source, target, u):
    pairs = []
    for col in range(4):
        for core in range(2):
            here = (col ^ source) * 2 + core
            there = (col ^ target) * 2 + (core ^ u)
            pairs.append((here * 4 + col, there * 4 + col))
    return lax.ppermute(x, ("row", "col"), pairs)


def to_corner(same, cross):
    by_y = [in_plane(same, 2, 0, 0), in_plane(cross, 2, 0, 1)]
    half_way = in_plane(cross, 3, 1, 0)
    by_x = [in_plane(same, 1, 0, 0), in_plane(cross, 1, 0, 1)]
    direct = in_plane(same, 3, 0, 0)
    return [*by_x, *by_y, direct, in_plane(half_way, 1, 0, 1)]


def local(density, pattern):
    masked = filtered(density.astype(jnp.float32), pattern).astype(jnp.bfloat16)
    rows, columns = masked.shape
    row, col = lax.axis_index("row"), lax.axis_index("col")
    where = jnp.stack([row, col]).astype(jnp.int32)
    kept = jnp.repeat(pattern.astype(jnp.bfloat16), B, axis=1)
    kept = jnp.pad(kept, ((0, EXTRA - kept.shape[0]), (0, 0)))
    own = jnp.concatenate([masked, kept], axis=0)
    pair = lax.ppermute(own, "col", [(i, i ^ 1) for i in range(4)])
    cross = lax.ppermute(own, "col", [(i, i ^ 3) for i in range(4)])
    middle2 = lax.ppermute(pair, "col", [(1, 2), (2, 1)])
    outer2 = lax.ppermute(cross, "col", [(2, 3), (1, 0)])
    rights = column_gather(masked)

    flops = 2 * 2 * rows * rows * columns
    size = 2 * rows * columns
    tile = jax.ShapeDtypeStruct((rows, columns), jnp.bfloat16)
    wide = jax.ShapeDtypeStruct((rows, columns), jnp.float32)
    extended = jax.ShapeDtypeStruct((rows + EXTRA, columns), jnp.bfloat16)
    partial, panel, right, ahead = call(
        square_early_kernel,
        [SCALARS] + [ANYWHERE] * 11,
        (where, own, pair, cross, *rights),
        (
            wide,
            jax.ShapeDtypeStruct((3, rows + EXTRA, columns), jnp.bfloat16),
            jax.ShapeDtypeStruct((8, rows, columns), jnp.bfloat16),
            jax.ShapeDtypeStruct((2, rows, columns), jnp.bfloat16),
        ),
        [DMA((3,)), DMA((8,)), DMA(())],
        3 * flops,
        24 * size,
    )
    other = swap(panel, 1)
    squared, sums, far = call(
        square_late_kernel,
        [SCALARS, WHOLE, WHOLE, WHOLE] + [ANYWHERE] * 2,
        (where, own, partial, ahead, middle2, outer2),
        (tile, jax.ShapeDtypeStruct((8, B), jnp.float32), extended),
        [DMA(())],
        flops,
        8 * size,
    )
    turns = [rotate(squared, 1), rotate(squared, 2)]
    total = jnp.sum(sums)
    for k in (1, 4, 2):
        total = total + swap(total, k)
    quarter = jax.ShapeDtypeStruct((rows, rows), jnp.bfloat16)
    turned = call(
        turn_kernel,
        [SCALARS, WHOLE],
        (where, squared),
        (quarter, quarter),
        [],
        0,
        2 * size,
    )
    sides = to_corner(*turned)
    local_square = call(
        own_square_kernel,
        [SCALARS] + [WHOLE] * 4,
        (where, panel, other, far, swap(far, 1)),
        tile,
        [],
        4 * flops,
        9 * size,
        48,
    )
    cubic = call(
        cubic_early_kernel,
        [SCALARS, WHOLE, WHOLE, AWAY],
        (where, squared, local_square, right),
        wide,
        [pltpu.VMEM((2, 2, rows, columns), jnp.bfloat16), DMA((2,))],
        2 * flops,
        8 * size,
        48,
    )
    for k in (2, 1):
        total = total + lax.ppermute(total, "col", [(i, i ^ k) for i in range(4)])
    cubic = call(
        cubic_middle_kernel,
        [SCALARS] + [WHOLE] * 2 + [ANYWHERE] * 4 + [AWAY],
        (where, cubic, turns[0], *sides[:4], right),
        wide,
        [
            pltpu.VMEM((2, rows, columns), jnp.bfloat16),
            pltpu.VMEM((2, 2, rows, columns), jnp.bfloat16),
            DMA((2,)),
            DMA((2,)),
        ],
        2 * flops,
        10 * size,
        48,
    )
    purified = call(
        cubic_late_kernel,
        [SCALARS] + [WHOLE] * 4 + [ANYWHERE] * 2 + [AWAY],
        (where, own, squared, cubic, turns[1], *sides[4:], right),
        wide,
        [
            pltpu.VMEM((rows, columns), jnp.bfloat16),
            pltpu.VMEM((2, rows, columns), jnp.bfloat16),
            DMA(()),
            DMA(()),
        ],
        flops,
        9 * size,
        48,
    )
    return (purified, total / (rows * lax.axis_size("row")))


def solution(mesh):
    placed = (P("row", "col"), P("row", "col"))
    body = local if (mesh.shape["row"], mesh.shape["col"]) == (8, 4) else general
    return jax.shard_map(
        body, mesh=mesh, in_specs=placed, out_specs=(P("row", "col"), P()), check_vma=False
    )
```

```python
import jax
import jax.numpy as jnp
from jax import lax
from jax.experimental import pallas as pl
from jax.experimental.pallas import tpu as pltpu
from jax.sharding import PartitionSpec as P


B = 128


def filtered(values, pattern):
    block_rows, block_cols = pattern.shape
    blocked = (
        values.reshape(block_rows, B, block_cols, B) * pattern.astype(jnp.float32)[:, None, :, None]
    )
    return blocked.reshape(block_rows * B, block_cols * B)


def general(density, pattern):
    masked = filtered(density.astype(jnp.float32), pattern).astype(jnp.bfloat16)
    row_count = masked.shape[0]
    col_count = masked.shape[1]
    column = lax.all_gather(masked, "row", axis=0, tiled=True)

    def multiply(factor):
        return jnp.dot(
            lax.all_gather(factor, "col", axis=1, tiled=True),
            column,
            preferred_element_type=jnp.float32,
        )

    squared = filtered(multiply(masked), pattern).astype(jnp.bfloat16)
    cubic_term = filtered(multiply(squared), pattern)
    purified = 3.0 * squared.astype(jnp.float32) - 2.0 * cubic_term
    row_index = lax.axis_index("row") * row_count + jnp.arange(row_count, dtype=jnp.int32)
    col_index = lax.axis_index("col") * col_count + jnp.arange(col_count, dtype=jnp.int32)
    diagonal_sum = jnp.sum(jnp.where(row_index[:, None] == col_index[None, :], purified, 0.0))
    total_trace = lax.psum(diagonal_sum, ("row", "col"))
    occupation = total_trace / (row_count * lax.axis_size("row"))
    return (purified, occupation)


NEAR = (0, 1, 3)
LAST = 2
EXTRA = 16


def piece(left, right):
    rows = right.shape[1]
    return jnp.dot(left[:rows, :rows], right[0], preferred_element_type=jnp.float32) + jnp.dot(
        left[:rows, rows:], right[1], preferred_element_type=jnp.float32
    )


def multiply(acc, left, right, fresh):
    if fresh:
        acc[...] = piece(left, right)
    else:
        acc[...] += piece(left, right)


def blocks(rows, columns, body):
    @pl.loop(0, (rows // B) * (columns // B))
    def _(block):
        a = block // (columns // B)
        b = block % (columns // B)
        body(
            a,
            b,
            (pl.ds(pl.multiple_of(a * B, B), B), pl.ds(pl.multiple_of(b * B, B), B)),
        )


def square_early_kernel(where, own, pair, cross, *refs):
    rights = refs[:8]
    acc, panel, right, left_sem, right_sem = refs[8:]
    row, col = where[0], where[1]
    for i, ref in enumerate((own, pair, cross)):
        pltpu.make_async_copy(ref, panel.at[i], left_sem.at[i]).start()

    for k in range(8):
        slot = row ^ k
        pltpu.make_async_copy(rights[k], right.at[slot], right_sem.at[slot]).start()
    for i, d in enumerate(NEAR):
        slot = 2 * (col ^ d)
        pltpu.make_async_copy(panel.at[i], panel.at[i], left_sem.at[i]).wait()
        for t in range(2):
            there = right.at[slot + t]
            pltpu.make_async_copy(there, there, right_sem.at[slot + t]).wait()
        multiply(acc, panel.at[i], right.at[pl.ds(slot, 2)], i == 0)
    slot = 2 * (col ^ LAST)
    for t in range(2):
        there = right.at[slot + t]
        pltpu.make_async_copy(there, there, right_sem.at[slot + t]).wait()


def square_late_kernel(where, own, acc_in, right, middle2, outer2, *refs):
    squared_ref, sum_ref, far, left_sem = refs
    row, col = where[0], where[1]
    rows, columns = squared_ref.shape
    inner = (col == 1) | (col == 2)

    @pl.when(inner)
    def _():
        pltpu.make_async_copy(middle2, far, left_sem).start()

    @pl.when(jnp.logical_not(inner))
    def _():
        pltpu.make_async_copy(outer2, far, left_sem).start()

    pltpu.make_async_copy(far, far, left_sem).wait()
    total = acc_in[...] + piece(far, right.at[pl.ds(2 * (col ^ LAST), 2)])
    kept = own[rows : rows + EXTRA, :].astype(jnp.float32)
    sums = jnp.zeros((8, columns), jnp.float32)
    for a in range(rows // B):
        part = slice(a * B, (a + 1) * B)
        squared = (total[part] * kept[a : a + 1]).astype(jnp.bfloat16)
        squared_ref[part, :] = squared
        term = squared.astype(jnp.float32) * own[part, :].astype(jnp.float32)
        sums -= 2.0 * jnp.sum(term.reshape(B // 8, 8, columns), axis=0)
    sum_ref[...] = sums[:, :B]
    for n in range(1, columns // B):
        sum_ref[...] += sums[:, n * B : (n + 1) * B]

    @pl.when(row // 2 == col)
    def _():
        same = lax.broadcasted_iota(jnp.int32, (B, B), 0) == lax.broadcasted_iota(
            jnp.int32, (B, B), 1
        )
        for a in range(rows // B):
            lanes = pl.ds(pl.multiple_of(row * rows - col * columns + a * B, B), B)
            squared = squared_ref[a * B : (a + 1) * B, lanes].astype(jnp.float32)
            term = jnp.where(same, 3.0 * squared, 0.0)
            sum_ref[...] += jnp.sum(term.reshape(B // 8, 8, B), axis=0)

    sum_ref[...] = jnp.broadcast_to(jnp.sum(sum_ref[...], keepdims=True), sum_ref.shape)


def add_kernel(left, right, out):
    out[...] = left[...] + right[...]


def turn_kernel(where, squared, same_ref, cross_ref):
    core = where[0] % 2
    half = same_ref.shape[0]

    def body(a, b, part):
        for out, h in ((same_ref, core), (cross_ref, 1 - core)):
            lanes = pl.ds(pl.multiple_of(h * half + b * B, B), B)
            out[part[1], part[0]] = squared[part[0], lanes].T

    blocks(half, half, body)


def own_square_kernel(where, panel, other, far, far_other, out):
    row, col = where[0], where[1]
    core, chip = row % 2, row // 2
    rows = out.shape[0]
    d = col ^ chip
    for source, last, h in ((panel, far, core), (other, far_other, 1 - core)):
        total = None
        for left, right in [(panel.at[i], source.at[i]) for i in range(3)] + [(far, last)]:
            part = lax.dot_general(
                left[:rows, :],
                right[:rows, :],
                (((1,), (1,)), ((), ())),
                preferred_element_type=jnp.float32,
            )
            total = part if total is None else total + part
        lanes = pl.ds(pl.multiple_of(h * rows, rows), rows)
        near = panel[jnp.minimum(d, 2), rows : rows + EXTRA, lanes].astype(jnp.float32)
        kept = jnp.where(d == LAST, far[rows : rows + EXTRA, lanes].astype(jnp.float32), near)
        for a in range(rows // B):
            out[a * B : (a + 1) * B, lanes] = (
                total[a * B : (a + 1) * B] * kept[a : a + 1]
            ).astype(jnp.bfloat16)


def late_sources(row, col):
    chip = row // 2
    place = col - (col > chip).astype(jnp.int32)
    sources = []
    for i in range(3):
        index = (place + 2 - i) % 3
        other = index + (index >= chip).astype(jnp.int32)
        sources.append(jnp.where(chip == col, col ^ (i + 1), other))
    return sources


def cubic_early_kernel(where, squared, local_square, right, acc):
    row, col = where[0], where[1]
    chip = row // 2
    multiply(acc, squared, right.at[pl.ds(2 * col, 2)], True)

    @pl.when(chip != col)
    def _():
        multiply(acc, local_square, right.at[pl.ds(2 * chip, 2)], False)


def cubic_late_kernel(where, own, squared, acc_in, turn1, turn2, right_all, *refs):
    sides = refs[:6]
    purified_ref, left, acc, sem = refs[6:]
    row, col = where[0], where[1]
    core, chip = row % 2, row // 2
    rows, _ = squared.shape
    corner = chip == col
    rights = [right_all.at[pl.ds(2 * source, 2)] for source in late_sources(row, col)]

    def finish(last):
        total = acc_in[...] + acc[...] + piece(last, rights[1])
        kept = own[rows : rows + EXTRA, :].astype(jnp.float32)
        for a in range(rows // B):
            part = slice(a * B, (a + 1) * B)
            wide = squared[part, :].astype(jnp.float32)
            purified_ref[part, :] = 3.0 * wide - 2.0 * (total[part] * kept[a : a + 1])

    @pl.when(jnp.logical_not(corner))
    def _():
        multiply(acc, turn1, rights[0], True)
        finish(turn2)

    @pl.when(corner)
    def _():
        for i in range(3):
            for u in range(2):
                lanes = pl.ds(pl.multiple_of((core ^ u) * rows, rows), rows)
                pltpu.make_async_copy(sides[2 * i + u], left.at[i, :, lanes], sem.at[i]).start()
        for i in (0, 2, 1):
            pltpu.make_async_copy(left.at[i], left.at[i], sem.at[i]).wait()
            if i != 1:
                multiply(acc, left.at[i], rights[i], i == 0)
        finish(left.at[1])


ANYWHERE = pl.BlockSpec(memory_space=pl.ANY)
SCALARS = pl.BlockSpec(memory_space=pltpu.SMEM)
WHOLE = pl.BlockSpec(memory_space=pltpu.VMEM)
DMA = pltpu.SemaphoreType.DMA


def call(kernel, specs, args, outs, scratch, flops, moved, grant=16):
    return pl.pallas_call(
        kernel,
        out_shape=outs,
        in_specs=specs,
        out_specs=jax.tree.map(lambda _: WHOLE, outs),
        scratch_shapes=scratch,
        compiler_params=pltpu.CompilerParams(vmem_limit_bytes=grant << 20),
        cost_estimate=pl.CostEstimate(flops=flops, bytes_accessed=moved, transcendentals=0),
    )(*args)


def swap(x, k):
    return lax.ppermute(x, "row", [(i, i ^ k) for i in range(8)])


def column_gather(x):
    by_x = swap(x, 2)
    by_y = swap(x, 4)
    core = swap(x, 1)
    by_x_core = swap(by_x, 1)
    by_y_core = swap(by_y, 1)
    diagonal = swap(by_x, 4)
    return [x, core, by_x, by_x_core, by_y, by_y_core, diagonal, swap(diagonal, 1)]


def rotate(x, step):
    pairs = []
    for row in range(8):
        planes = [c for c in range(4) if c != row // 2]
        for i in range(3):
            pairs.append((row * 4 + planes[i], row * 4 + planes[(i + step) % 3]))
    return lax.ppermute(x, ("row", "col"), pairs)


def in_plane(x, source, target, u):
    pairs = []
    for col in range(4):
        for core in range(2):
            here = (col ^ source) * 2 + core
            there = (col ^ target) * 2 + (core ^ u)
            pairs.append((here * 4 + col, there * 4 + col))
    return lax.ppermute(x, ("row", "col"), pairs)


def to_corner(same, cross):
    by_y = [in_plane(same, 2, 0, 0), in_plane(cross, 2, 0, 1)]
    half_way = in_plane(cross, 3, 1, 0)
    by_x = [in_plane(same, 1, 0, 0), in_plane(cross, 1, 0, 1)]
    direct = in_plane(same, 3, 0, 0)
    return [*by_x, *by_y, direct, in_plane(half_way, 1, 0, 1)]


def local(density, pattern):
    masked = filtered(density.astype(jnp.float32), pattern).astype(jnp.bfloat16)
    rows, columns = masked.shape
    row, col = lax.axis_index("row"), lax.axis_index("col")
    where = jnp.stack([row, col]).astype(jnp.int32)
    kept = jnp.repeat(pattern.astype(jnp.bfloat16), B, axis=1)
    kept = jnp.pad(kept, ((0, EXTRA - kept.shape[0]), (0, 0)))
    own = jnp.concatenate([masked, kept], axis=0)
    pair = lax.ppermute(own, "col", [(i, i ^ 1) for i in range(4)])
    cross = lax.ppermute(own, "col", [(i, i ^ 3) for i in range(4)])
    middle2 = lax.ppermute(pair, "col", [(1, 2), (2, 1)])
    outer2 = lax.ppermute(cross, "col", [(2, 3), (1, 0)])
    rights = column_gather(masked)

    flops = 2 * 2 * rows * rows * columns
    size = 2 * rows * columns
    tile = jax.ShapeDtypeStruct((rows, columns), jnp.bfloat16)
    wide = jax.ShapeDtypeStruct((rows, columns), jnp.float32)
    extended = jax.ShapeDtypeStruct((rows + EXTRA, columns), jnp.bfloat16)
    acc = pltpu.VMEM((rows, columns), jnp.float32)
    partial, panel, right = call(
        square_early_kernel,
        [SCALARS] + [ANYWHERE] * 11,
        (where, own, pair, cross, *rights),
        (
            wide,
            jax.ShapeDtypeStruct((3, rows + EXTRA, columns), jnp.bfloat16),
            jax.ShapeDtypeStruct((8, rows, columns), jnp.bfloat16),
        ),
        [DMA((3,)), DMA((8,))],
        3 * flops,
        24 * size,
    )
    other = swap(panel, 1)
    squared, sums, far = call(
        square_late_kernel,
        [SCALARS, WHOLE, WHOLE, WHOLE] + [ANYWHERE] * 2,
        (where, own, partial, right, middle2, outer2),
        (tile, jax.ShapeDtypeStruct((8, B), jnp.float32), extended),
        [DMA(())],
        flops,
        8 * size,
    )
    turns = [rotate(squared, 1), rotate(squared, 2)]
    total = sums

    def add(left, right):
        return call(
            add_kernel,
            [WHOLE] * 2,
            (left, right),
            jax.ShapeDtypeStruct(left.shape, left.dtype),
            [],
            left.size,
            12 * left.size,
            1,
        )

    for k in (1, 4, 2):
        total = add(total, swap(total, k))
    quarter = jax.ShapeDtypeStruct((rows, rows), jnp.bfloat16)
    turned = call(
        turn_kernel,
        [SCALARS, WHOLE],
        (where, squared),
        (quarter, quarter),
        [],
        0,
        2 * size,
    )
    sides = to_corner(*turned)
    local_square = call(
        own_square_kernel,
        [SCALARS] + [WHOLE] * 4,
        (where, panel, other, far, swap(far, 1)),
        tile,
        [],
        4 * flops,
        9 * size,
        16,
    )
    cubic = call(
        cubic_early_kernel,
        [SCALARS] + [WHOLE] * 3,
        (where, squared, local_square, right),
        wide,
        [],
        2 * flops,
        8 * size,
        16,
    )
    for k in (2, 1):
        total = add(total, lax.ppermute(total, "col", [(i, i ^ k) for i in range(4)]))
    purified = call(
        cubic_late_kernel,
        [SCALARS] + [WHOLE] * 6 + [ANYWHERE] * 6,
        (where, own, squared, cubic, *turns, right, *sides),
        wide,
        [
            pltpu.VMEM((3, rows, columns), jnp.bfloat16),
            acc,
            DMA((3,)),
        ],
        3 * flops,
        16 * size,
        16,
    )
    return (purified, total[0, 0] / (rows * lax.axis_size("row")))


def solution(mesh):
    placed = (P("row", "col"), P("row", "col"))
    body = local if (mesh.shape["row"], mesh.shape["col"]) == (8, 4) else general
    return jax.shard_map(
        body, mesh=mesh, in_specs=placed, out_specs=(P("row", "col"), P()), check_vma=False
    )
```

```python
import jax
import jax.numpy as jnp
from jax import lax
from jax.experimental import pallas as pl
from jax.experimental.pallas import tpu as pltpu
from jax.sharding import PartitionSpec as P


B = 128


def filtered(values, pattern):
    block_rows, block_cols = pattern.shape
    blocked = (
        values.reshape(block_rows, B, block_cols, B) * pattern.astype(jnp.float32)[:, None, :, None]
    )
    return blocked.reshape(block_rows * B, block_cols * B)


def general(density, pattern):
    masked = filtered(density.astype(jnp.float32), pattern).astype(jnp.bfloat16)
    row_count = masked.shape[0]
    col_count = masked.shape[1]
    column = lax.all_gather(masked, "row", axis=0, tiled=True)

    def multiply(factor):
        return jnp.dot(
            lax.all_gather(factor, "col", axis=1, tiled=True),
            column,
            preferred_element_type=jnp.float32,
        )

    squared = filtered(multiply(masked), pattern).astype(jnp.bfloat16)
    cubic_term = filtered(multiply(squared), pattern)
    purified = 3.0 * squared.astype(jnp.float32) - 2.0 * cubic_term
    row_index = lax.axis_index("row") * row_count + jnp.arange(row_count, dtype=jnp.int32)
    col_index = lax.axis_index("col") * col_count + jnp.arange(col_count, dtype=jnp.int32)
    diagonal_sum = jnp.sum(jnp.where(row_index[:, None] == col_index[None, :], purified, 0.0))
    total_trace = lax.psum(diagonal_sum, ("row", "col"))
    occupation = total_trace / (row_count * lax.axis_size("row"))
    return (purified, occupation)


NEAR = (0, 1, 3)
LAST = 2
EXTRA = 16


def piece(left, right):
    rows = right.shape[1]
    return jnp.dot(left[:rows, :rows], right[0], preferred_element_type=jnp.float32) + jnp.dot(
        left[:rows, rows:], right[1], preferred_element_type=jnp.float32
    )


def multiply(acc, left, right, fresh):
    if fresh:
        acc[...] = piece(left, right)
    else:
        acc[...] += piece(left, right)


def blocks(rows, columns, body):
    @pl.loop(0, (rows // B) * (columns // B))
    def _(block):
        a = block // (columns // B)
        b = block % (columns // B)
        body(
            a,
            b,
            (pl.ds(pl.multiple_of(a * B, B), B), pl.ds(pl.multiple_of(b * B, B), B)),
        )


def square_early_kernel(where, own, pair, cross, *refs):
    rights = refs[:8]
    acc, panel, right, left_sem, right_sem = refs[8:]
    row, col = where[0], where[1]
    for i, ref in enumerate((own, pair, cross)):
        pltpu.make_async_copy(ref, panel.at[i], left_sem.at[i]).start()

    for k in range(8):
        slot = row ^ k
        pltpu.make_async_copy(rights[k], right.at[slot], right_sem.at[slot]).start()
    for i, d in enumerate(NEAR):
        slot = 2 * (col ^ d)
        pltpu.make_async_copy(panel.at[i], panel.at[i], left_sem.at[i]).wait()
        for t in range(2):
            there = right.at[slot + t]
            pltpu.make_async_copy(there, there, right_sem.at[slot + t]).wait()
        multiply(acc, panel.at[i], right.at[pl.ds(slot, 2)], i == 0)
    slot = 2 * (col ^ LAST)
    for t in range(2):
        there = right.at[slot + t]
        pltpu.make_async_copy(there, there, right_sem.at[slot + t]).wait()


def square_late_kernel(where, own, acc_in, right, far, squared_ref, sum_ref):
    row, col = where[0], where[1]
    rows, columns = squared_ref.shape
    total = acc_in[...] + piece(far, right.at[pl.ds(2 * (col ^ LAST), 2)])
    kept = own[rows : rows + EXTRA, :].astype(jnp.float32)
    sums = jnp.zeros((8, columns), jnp.float32)
    for a in range(rows // B):
        part = slice(a * B, (a + 1) * B)
        squared = (total[part] * kept[a : a + 1]).astype(jnp.bfloat16)
        squared_ref[part, :] = squared
        term = squared.astype(jnp.float32) * own[part, :].astype(jnp.float32)
        sums -= 2.0 * jnp.sum(term.reshape(B // 8, 8, columns), axis=0)
    sum_ref[...] = sums[:, :B]
    for n in range(1, columns // B):
        sum_ref[...] += sums[:, n * B : (n + 1) * B]

    @pl.when(row // 2 == col)
    def _():
        same = lax.broadcasted_iota(jnp.int32, (B, B), 0) == lax.broadcasted_iota(
            jnp.int32, (B, B), 1
        )
        for a in range(rows // B):
            lanes = pl.ds(pl.multiple_of(row * rows - col * columns + a * B, B), B)
            squared = squared_ref[a * B : (a + 1) * B, lanes].astype(jnp.float32)
            term = jnp.where(same, 3.0 * squared, 0.0)
            sum_ref[...] += jnp.sum(term.reshape(B // 8, 8, B), axis=0)

    sum_ref[...] = jnp.broadcast_to(jnp.sum(sum_ref[...], keepdims=True), sum_ref.shape)


def add_kernel(left, right, out):
    out[...] = left[...] + right[...]


def turn_kernel(where, squared, same_ref, cross_ref):
    core = where[0] % 2
    half = same_ref.shape[0]

    def body(a, b, part):
        for out, h in ((same_ref, core), (cross_ref, 1 - core)):
            lanes = pl.ds(pl.multiple_of(h * half + b * B, B), B)
            out[part[1], part[0]] = squared[part[0], lanes].T

    blocks(half, half, body)


def own_square_kernel(where, panel, other, far, far_other, out):
    row, col = where[0], where[1]
    core, chip = row % 2, row // 2
    rows = out.shape[0]
    d = col ^ chip
    for source, last, h in ((panel, far, core), (other, far_other, 1 - core)):
        total = None
        for left, right in [(panel.at[i], source.at[i]) for i in range(3)] + [(far, last)]:
            part = lax.dot_general(
                left[:rows, :],
                right[:rows, :],
                (((1,), (1,)), ((), ())),
                preferred_element_type=jnp.float32,
            )
            total = part if total is None else total + part
        lanes = pl.ds(pl.multiple_of(h * rows, rows), rows)
        near = panel[jnp.minimum(d, 2), rows : rows + EXTRA, lanes].astype(jnp.float32)
        kept = jnp.where(d == LAST, far[rows : rows + EXTRA, lanes].astype(jnp.float32), near)
        for a in range(rows // B):
            out[a * B : (a + 1) * B, lanes] = (
                total[a * B : (a + 1) * B] * kept[a : a + 1]
            ).astype(jnp.bfloat16)


def late_sources(row, col):
    chip = row // 2
    place = col - (col > chip).astype(jnp.int32)
    sources = []
    for i in range(3):
        index = (place + 2 - i) % 3
        other = index + (index >= chip).astype(jnp.int32)
        sources.append(jnp.where(chip == col, col ^ (i + 1), other))
    return sources


def cubic_early_kernel(where, squared, local_square, right, acc):
    row, col = where[0], where[1]
    chip = row // 2
    multiply(acc, squared, right.at[pl.ds(2 * col, 2)], True)

    @pl.when(chip != col)
    def _():
        multiply(acc, local_square, right.at[pl.ds(2 * chip, 2)], False)


def side_piece(sides, right_all, source, core):
    return sum(
        jnp.dot(ref[...], right_all[2 * source + (core ^ u)], preferred_element_type=jnp.float32)
        for u, ref in enumerate(sides)
    )


def cubic_middle_kernel(where, acc_in, right_all, same, cross, acc):
    row, col = where[0], where[1]

    @pl.when(row // 2 == col)
    def _():
        acc[...] = acc_in[...] + side_piece((same, cross), right_all, col ^ 2, row % 2)

    @pl.when(row // 2 != col)
    def _():
        acc[...] = acc_in[...]


def cubic_late_kernel(where, own, squared, acc, turn1, turn2, right_all, *refs):
    sides, purified_ref, scratch = refs[:4], refs[4], refs[5]
    row, col = where[0], where[1]
    core, chip = row % 2, row // 2
    rows, _ = squared.shape
    sources = late_sources(row, col)

    def finish(first, second):
        scratch[...] = acc[...] + first
        total = scratch[...] + second()
        kept = own[rows : rows + EXTRA, :].astype(jnp.float32)
        for a in range(rows // B):
            part = slice(a * B, (a + 1) * B)
            wide = squared[part, :].astype(jnp.float32)
            purified_ref[part, :] = 3.0 * wide - 2.0 * (total[part] * kept[a : a + 1])

    @pl.when(chip != col)
    def _():
        finish(
            piece(turn1, right_all.at[pl.ds(2 * sources[0], 2)]),
            lambda: piece(turn2, right_all.at[pl.ds(2 * sources[1], 2)]),
        )

    @pl.when(chip == col)
    def _():
        finish(
            side_piece(sides[:2], right_all, col ^ 1, core),
            lambda: side_piece(sides[2:], right_all, col ^ 3, core),
        )


ANYWHERE = pl.BlockSpec(memory_space=pl.ANY)
SCALARS = pl.BlockSpec(memory_space=pltpu.SMEM)
WHOLE = pl.BlockSpec(memory_space=pltpu.VMEM)
DMA = pltpu.SemaphoreType.DMA


def call(kernel, specs, args, outs, scratch, flops, moved, grant=16):
    return pl.pallas_call(
        kernel,
        out_shape=outs,
        in_specs=specs,
        out_specs=jax.tree.map(lambda _: WHOLE, outs),
        scratch_shapes=scratch,
        compiler_params=pltpu.CompilerParams(vmem_limit_bytes=grant << 20),
        cost_estimate=pl.CostEstimate(flops=flops, bytes_accessed=moved, transcendentals=0),
    )(*args)


def swap(x, k):
    return lax.ppermute(x, "row", [(i, i ^ k) for i in range(8)])


def column_gather(x):
    by_x = swap(x, 2)
    by_y = swap(x, 4)
    core = swap(x, 1)
    by_x_core = swap(by_x, 1)
    by_y_core = swap(by_y, 1)
    diagonal = swap(by_x, 4)
    return [x, core, by_x, by_x_core, by_y, by_y_core, diagonal, swap(diagonal, 1)]


def rotate(x, step):
    pairs = []
    for row in range(8):
        planes = [c for c in range(4) if c != row // 2]
        for i in range(3):
            pairs.append((row * 4 + planes[i], row * 4 + planes[(i + step) % 3]))
    return lax.ppermute(x, ("row", "col"), pairs)


def in_plane(x, source, target, u):
    pairs = []
    for col in range(4):
        for core in range(2):
            here = (col ^ source) * 2 + core
            there = (col ^ target) * 2 + (core ^ u)
            pairs.append((here * 4 + col, there * 4 + col))
    return lax.ppermute(x, ("row", "col"), pairs)


def to_corner(same, cross):
    by_y = [in_plane(same, 2, 0, 0), in_plane(cross, 2, 0, 1)]
    half_way = in_plane(cross, 3, 1, 0)
    by_x = [in_plane(same, 1, 0, 0), in_plane(cross, 1, 0, 1)]
    direct = in_plane(same, 3, 0, 0)
    return [*by_x, *by_y, direct, in_plane(half_way, 1, 0, 1)]


def local(density, pattern):
    masked = filtered(density.astype(jnp.float32), pattern).astype(jnp.bfloat16)
    rows, columns = masked.shape
    row, col = lax.axis_index("row"), lax.axis_index("col")
    where = jnp.stack([row, col]).astype(jnp.int32)
    kept = jnp.repeat(pattern.astype(jnp.bfloat16), B, axis=1)
    kept = jnp.pad(kept, ((0, EXTRA - kept.shape[0]), (0, 0)))
    own = jnp.concatenate([masked, kept], axis=0)
    cross = lax.ppermute(own, "col", [(i, i ^ 3) for i in range(4)])
    pair = lax.ppermute(own, "col", [(i, i ^ 1) for i in range(4)])
    far = lax.ppermute(cross, "col", [(i, i ^ 1) for i in range(4)])
    rights = column_gather(masked)

    flops = 2 * 2 * rows * rows * columns
    size = 2 * rows * columns
    tile = jax.ShapeDtypeStruct((rows, columns), jnp.bfloat16)
    wide = jax.ShapeDtypeStruct((rows, columns), jnp.float32)
    partial, panel, right = call(
        square_early_kernel,
        [SCALARS] + [ANYWHERE] * 11,
        (where, own, pair, cross, *rights),
        (
            wide,
            jax.ShapeDtypeStruct((3, rows + EXTRA, columns), jnp.bfloat16),
            jax.ShapeDtypeStruct((8, rows, columns), jnp.bfloat16),
        ),
        [DMA((3,)), DMA((8,))],
        3 * flops,
        24 * size,
    )
    other = swap(panel, 1)
    squared, sums = call(
        square_late_kernel,
        [SCALARS] + [WHOLE] * 4,
        (where, own, partial, right, far),
        (tile, jax.ShapeDtypeStruct((8, B), jnp.float32)),
        [],
        flops,
        8 * size,
    )
    turns = [rotate(squared, 1), rotate(squared, 2)]
    total = sums

    def add(left, right):
        return call(
            add_kernel,
            [WHOLE] * 2,
            (left, right),
            jax.ShapeDtypeStruct(left.shape, left.dtype),
            [],
            left.size,
            12 * left.size,
            1,
        )

    for k in (1, 2, 4):
        total = add(total, swap(total, k))
    quarter = jax.ShapeDtypeStruct((rows, rows), jnp.bfloat16)
    turned = call(
        turn_kernel,
        [SCALARS, WHOLE],
        (where, squared),
        (quarter, quarter),
        [],
        0,
        2 * size,
    )
    sides = to_corner(*turned)
    local_square = call(
        own_square_kernel,
        [SCALARS] + [WHOLE] * 4,
        (where, panel, other, far, swap(far, 1)),
        tile,
        [],
        4 * flops,
        9 * size,
        16,
    )
    cubic = call(
        cubic_early_kernel,
        [SCALARS] + [WHOLE] * 3,
        (where, squared, local_square, right),
        wide,
        [],
        2 * flops,
        8 * size,
        16,
    )
    cubic = call(
        cubic_middle_kernel,
        [SCALARS] + [WHOLE] * 4,
        (where, cubic, right, *sides[2:4]),
        wide,
        [],
        flops,
        9 * size,
    )
    for k in (2, 1):
        total = add(total, lax.ppermute(total, "col", [(i, i ^ k) for i in range(4)]))
    purified = call(
        cubic_late_kernel,
        [SCALARS] + [WHOLE] * 10,
        (where, own, squared, cubic, *turns, right, *sides[:2], *sides[4:]),
        wide,
        [pltpu.VMEM((rows, columns), jnp.float32)],
        2 * flops,
        16 * size,
    )
    return (purified, total[0, 0] / (rows * lax.axis_size("row")))


def solution(mesh):
    placed = (P("row", "col"), P("row", "col"))
    body = local if (mesh.shape["row"], mesh.shape["col"]) == (8, 4) else general
    return jax.shard_map(
        body, mesh=mesh, in_specs=placed, out_specs=(P("row", "col"), P()), check_vma=False
    )
```

```python
import jax
import jax.numpy as jnp
from jax import lax
from jax.experimental import pallas as pl
from jax.experimental.pallas import tpu as pltpu
from jax.sharding import PartitionSpec as P


B = 128


def filtered(values, pattern):
    block_rows, block_cols = pattern.shape
    blocked = (
        values.reshape(block_rows, B, block_cols, B) * pattern.astype(jnp.float32)[:, None, :, None]
    )
    return blocked.reshape(block_rows * B, block_cols * B)


def general(density, pattern):
    masked = filtered(density.astype(jnp.float32), pattern).astype(jnp.bfloat16)
    row_count = masked.shape[0]
    col_count = masked.shape[1]
    column = lax.all_gather(masked, "row", axis=0, tiled=True)

    def multiply(factor):
        return jnp.dot(
            lax.all_gather(factor, "col", axis=1, tiled=True),
            column,
            preferred_element_type=jnp.float32,
        )

    squared = filtered(multiply(masked), pattern).astype(jnp.bfloat16)
    cubic_term = filtered(multiply(squared), pattern)
    purified = 3.0 * squared.astype(jnp.float32) - 2.0 * cubic_term
    row_index = lax.axis_index("row") * row_count + jnp.arange(row_count, dtype=jnp.int32)
    col_index = lax.axis_index("col") * col_count + jnp.arange(col_count, dtype=jnp.int32)
    diagonal_sum = jnp.sum(jnp.where(row_index[:, None] == col_index[None, :], purified, 0.0))
    total_trace = lax.psum(diagonal_sum, ("row", "col"))
    occupation = total_trace / (row_count * lax.axis_size("row"))
    return (purified, occupation)


NEAR = (0, 1, 3)
LAST = 2
EXTRA = 16


def piece(left, right):
    rows = right.shape[1]
    return jnp.dot(left[:rows, :rows], right[0], preferred_element_type=jnp.float32) + jnp.dot(
        left[:rows, rows:], right[1], preferred_element_type=jnp.float32
    )


def multiply(acc, left, right, fresh):
    if fresh:
        acc[...] = piece(left, right)
    else:
        acc[...] += piece(left, right)


def blocks(rows, columns, body):
    @pl.loop(0, (rows // B) * (columns // B))
    def _(block):
        a = block // (columns // B)
        b = block % (columns // B)
        body(
            a,
            b,
            (pl.ds(pl.multiple_of(a * B, B), B), pl.ds(pl.multiple_of(b * B, B), B)),
        )


def square_early_kernel(where, own, pair, cross, *refs):
    rights = refs[:8]
    acc, panel, right, left_sem, right_sem = refs[8:]
    row, col = where[0], where[1]
    for i, ref in enumerate((own, pair, cross)):
        pltpu.make_async_copy(ref, panel.at[i], left_sem.at[i]).start()

    for k in range(8):
        slot = row ^ k
        pltpu.make_async_copy(rights[k], right.at[slot], right_sem.at[slot]).start()
    for i, d in enumerate(NEAR):
        slot = 2 * (col ^ d)
        pltpu.make_async_copy(panel.at[i], panel.at[i], left_sem.at[i]).wait()
        for t in range(2):
            there = right.at[slot + t]
            pltpu.make_async_copy(there, there, right_sem.at[slot + t]).wait()
        multiply(acc, panel.at[i], right.at[pl.ds(slot, 2)], i == 0)
    slot = 2 * (col ^ LAST)
    for t in range(2):
        there = right.at[slot + t]
        pltpu.make_async_copy(there, there, right_sem.at[slot + t]).wait()


def square_late_kernel(where, own, acc_in, right, far, squared_ref, sum_ref):
    row, col = where[0], where[1]
    rows, columns = squared_ref.shape
    total = acc_in[...] + piece(far, right.at[pl.ds(2 * (col ^ LAST), 2)])
    kept = own[rows : rows + EXTRA, :].astype(jnp.float32)
    sums = jnp.zeros((8, columns), jnp.float32)
    for a in range(rows // B):
        part = slice(a * B, (a + 1) * B)
        squared = (total[part] * kept[a : a + 1]).astype(jnp.bfloat16)
        squared_ref[part, :] = squared
        term = squared.astype(jnp.float32) * own[part, :].astype(jnp.float32)
        sums -= 2.0 * jnp.sum(term.reshape(B // 8, 8, columns), axis=0)
    sum_ref[...] = sums[:, :B]
    for n in range(1, columns // B):
        sum_ref[...] += sums[:, n * B : (n + 1) * B]

    @pl.when(row // 2 == col)
    def _():
        same = lax.broadcasted_iota(jnp.int32, (B, B), 0) == lax.broadcasted_iota(
            jnp.int32, (B, B), 1
        )
        for a in range(rows // B):
            lanes = pl.ds(pl.multiple_of(row * rows - col * columns + a * B, B), B)
            squared = squared_ref[a * B : (a + 1) * B, lanes].astype(jnp.float32)
            term = jnp.where(same, 3.0 * squared, 0.0)
            sum_ref[...] += jnp.sum(term.reshape(B // 8, 8, B), axis=0)

    sum_ref[...] = jnp.broadcast_to(jnp.sum(sum_ref[...], keepdims=True), sum_ref.shape)


def add_kernel(left, right, out):
    out[...] = left[...] + right[...]


def add_planes_kernel(own, first, second, third, out):
    out[...] = (own[...] + first[...]) + (second[...] + third[...])


def turn_kernel(where, squared, same_ref, cross_ref):
    core = where[0] % 2
    half = same_ref.shape[0]

    def body(a, b, part):
        for out, h in ((same_ref, core), (cross_ref, 1 - core)):
            lanes = pl.ds(pl.multiple_of(h * half + b * B, B), B)
            out[part[1], part[0]] = squared[part[0], lanes].T

    blocks(half, half, body)


def own_square_kernel(where, panel, other, far, far_other, out):
    row, col = where[0], where[1]
    core, chip = row % 2, row // 2
    rows = out.shape[0]
    d = col ^ chip
    for source, last, h in ((panel, far, core), (other, far_other, 1 - core)):
        total = None
        for left, right in [(panel.at[i], source.at[i]) for i in range(3)] + [(far, last)]:
            part = lax.dot_general(
                left[:rows, :],
                right[:rows, :],
                (((1,), (1,)), ((), ())),
                preferred_element_type=jnp.float32,
            )
            total = part if total is None else total + part
        lanes = pl.ds(pl.multiple_of(h * rows, rows), rows)
        near = panel[jnp.minimum(d, 2), rows : rows + EXTRA, lanes].astype(jnp.float32)
        kept = jnp.where(d == LAST, far[rows : rows + EXTRA, lanes].astype(jnp.float32), near)
        for a in range(rows // B):
            out[a * B : (a + 1) * B, lanes] = (
                total[a * B : (a + 1) * B] * kept[a : a + 1]
            ).astype(jnp.bfloat16)


def late_sources(row, col):
    chip = row // 2
    place = col - (col > chip).astype(jnp.int32)
    sources = []
    for i in range(3):
        index = (place + 2 - i) % 3
        other = index + (index >= chip).astype(jnp.int32)
        sources.append(jnp.where(chip == col, col ^ (i + 1), other))
    return sources


def cubic_early_kernel(where, squared, local_square, right, acc):
    row, col = where[0], where[1]
    chip = row // 2
    multiply(acc, squared, right.at[pl.ds(2 * col, 2)], True)

    @pl.when(chip != col)
    def _():
        multiply(acc, local_square, right.at[pl.ds(2 * chip, 2)], False)


def side_piece(sides, right_all, source, core):
    return sum(
        jnp.dot(ref[...], right_all[2 * source + (core ^ u)], preferred_element_type=jnp.float32)
        for u, ref in enumerate(sides)
    )


def cubic_middle_kernel(where, acc_in, right_all, same, cross, acc):
    row, col = where[0], where[1]

    @pl.when(row // 2 == col)
    def _():
        acc[...] = acc_in[...] + side_piece((same, cross), right_all, col ^ 1, row % 2)

    @pl.when(row // 2 != col)
    def _():
        acc[...] = acc_in[...]


def cubic_late_kernel(where, own, squared, acc, turn1, turn2, right_all, *refs):
    sides, purified_ref, scratch = refs[:4], refs[4], refs[5]
    row, col = where[0], where[1]
    core, chip = row % 2, row // 2
    rows, _ = squared.shape
    sources = late_sources(row, col)

    def finish(first, second):
        scratch[...] = acc[...] + first
        total = scratch[...] + second()
        kept = own[rows : rows + EXTRA, :].astype(jnp.float32)
        for a in range(rows // B):
            part = slice(a * B, (a + 1) * B)
            wide = squared[part, :].astype(jnp.float32)
            purified_ref[part, :] = 3.0 * wide - 2.0 * (total[part] * kept[a : a + 1])

    @pl.when(chip != col)
    def _():
        finish(
            piece(turn1, right_all.at[pl.ds(2 * sources[0], 2)]),
            lambda: piece(turn2, right_all.at[pl.ds(2 * sources[1], 2)]),
        )

    @pl.when(chip == col)
    def _():
        finish(
            side_piece(sides[:2], right_all, col ^ 2, core),
            lambda: side_piece(sides[2:], right_all, col ^ 3, core),
        )


ANYWHERE = pl.BlockSpec(memory_space=pl.ANY)
SCALARS = pl.BlockSpec(memory_space=pltpu.SMEM)
WHOLE = pl.BlockSpec(memory_space=pltpu.VMEM)
DMA = pltpu.SemaphoreType.DMA


def call(kernel, specs, args, outs, scratch, flops, moved, grant=16):
    return pl.pallas_call(
        kernel,
        out_shape=outs,
        in_specs=specs,
        out_specs=jax.tree.map(lambda _: WHOLE, outs),
        scratch_shapes=scratch,
        compiler_params=pltpu.CompilerParams(vmem_limit_bytes=grant << 20),
        cost_estimate=pl.CostEstimate(flops=flops, bytes_accessed=moved, transcendentals=0),
    )(*args)


def swap(x, k):
    return lax.ppermute(x, "row", [(i, i ^ k) for i in range(8)])


def column_gather(x):
    by_x = swap(x, 2)
    by_y = swap(x, 4)
    core = swap(x, 1)
    by_x_core = swap(by_x, 1)
    by_y_core = swap(by_y, 1)
    diagonal = swap(by_x, 4)
    return [x, core, by_x, by_x_core, by_y, by_y_core, diagonal, swap(diagonal, 1)]


def rotate(x, step):
    pairs = []
    for row in range(8):
        planes = [c for c in range(4) if c != row // 2]
        for i in range(3):
            pairs.append((row * 4 + planes[i], row * 4 + planes[(i + step) % 3]))
    return lax.ppermute(x, ("row", "col"), pairs)


def in_plane(x, source, target, u):
    pairs = []
    for col in range(4):
        for core in range(2):
            here = (col ^ source) * 2 + core
            there = (col ^ target) * 2 + (core ^ u)
            pairs.append((here * 4 + col, there * 4 + col))
    return lax.ppermute(x, ("row", "col"), pairs)


def to_corner(same, cross):
    by_y = [in_plane(same, 2, 0, 0), in_plane(cross, 2, 0, 1)]
    half_way = in_plane(cross, 3, 1, 0)
    by_x = [in_plane(same, 1, 0, 0), in_plane(cross, 1, 0, 1)]
    direct = in_plane(same, 3, 0, 0)
    return [*by_x, *by_y, direct, in_plane(half_way, 1, 0, 1)]


def local(density, pattern):
    masked = filtered(density.astype(jnp.float32), pattern).astype(jnp.bfloat16)
    rows, columns = masked.shape
    row, col = lax.axis_index("row"), lax.axis_index("col")
    where = jnp.stack([row, col]).astype(jnp.int32)
    kept = jnp.repeat(pattern.astype(jnp.bfloat16), B, axis=1)
    kept = jnp.pad(kept, ((0, EXTRA - kept.shape[0]), (0, 0)))
    own = jnp.concatenate([masked, kept], axis=0)
    cross = lax.ppermute(own, "col", [(i, i ^ 3) for i in range(4)])
    pair = lax.ppermute(own, "col", [(i, i ^ 1) for i in range(4)])
    far = lax.ppermute(cross, "col", [(i, i ^ 1) for i in range(4)])
    rights = column_gather(masked)

    flops = 2 * 2 * rows * rows * columns
    size = 2 * rows * columns
    tile = jax.ShapeDtypeStruct((rows, columns), jnp.bfloat16)
    wide = jax.ShapeDtypeStruct((rows, columns), jnp.float32)
    partial, panel, right = call(
        square_early_kernel,
        [SCALARS] + [ANYWHERE] * 11,
        (where, own, pair, cross, *rights),
        (
            wide,
            jax.ShapeDtypeStruct((3, rows + EXTRA, columns), jnp.bfloat16),
            jax.ShapeDtypeStruct((8, rows, columns), jnp.bfloat16),
        ),
        [DMA((3,)), DMA((8,))],
        3 * flops,
        24 * size,
    )
    other = swap(panel, 1)
    squared, sums = call(
        square_late_kernel,
        [SCALARS] + [WHOLE] * 4,
        (where, own, partial, right, far),
        (tile, jax.ShapeDtypeStruct((8, B), jnp.float32)),
        [],
        flops,
        8 * size,
    )
    turns = [rotate(squared, 1), rotate(squared, 2)]
    total = sums

    def add(left, right):
        return call(
            add_kernel,
            [WHOLE] * 2,
            (left, right),
            jax.ShapeDtypeStruct(left.shape, left.dtype),
            [],
            left.size,
            12 * left.size,
            1,
        )

    for k in (1, 2, 4):
        total = add(total, swap(total, k))
    quarter = jax.ShapeDtypeStruct((rows, rows), jnp.bfloat16)
    turned = call(
        turn_kernel,
        [SCALARS, WHOLE],
        (where, squared),
        (quarter, quarter),
        [],
        0,
        2 * size,
    )
    sides = to_corner(*turned)
    local_square = call(
        own_square_kernel,
        [SCALARS] + [WHOLE] * 4,
        (where, panel, other, far, swap(far, 1)),
        tile,
        [],
        4 * flops,
        9 * size,
        16,
    )
    cubic = call(
        cubic_early_kernel,
        [SCALARS] + [WHOLE] * 3,
        (where, squared, local_square, right),
        wide,
        [],
        2 * flops,
        8 * size,
        16,
    )
    cubic = call(
        cubic_middle_kernel,
        [SCALARS] + [WHOLE] * 4,
        (where, cubic, right, *sides[:2]),
        wide,
        [],
        flops,
        9 * size,
    )
    planes = [lax.ppermute(total, "col", [(i, i ^ k) for i in range(4)]) for k in (1, 2, 3)]
    total = call(
        add_planes_kernel,
        [WHOLE] * 4,
        (total, *planes),
        jax.ShapeDtypeStruct(total.shape, total.dtype),
        [],
        3 * total.size,
        20 * total.size,
        1,
    )
    purified = call(
        cubic_late_kernel,
        [SCALARS] + [WHOLE] * 10,
        (where, own, squared, cubic, *turns, right, *sides[2:]),
        wide,
        [pltpu.VMEM((rows, columns), jnp.float32)],
        2 * flops,
        16 * size,
    )
    return (purified, total[0, 0] / (rows * lax.axis_size("row")))


def solution(mesh):
    placed = (P("row", "col"), P("row", "col"))
    body = local if (mesh.shape["row"], mesh.shape["col"]) == (8, 4) else general
    return jax.shard_map(
        body, mesh=mesh, in_specs=placed, out_specs=(P("row", "col"), P()), check_vma=False
    )
```

```python
import jax
import jax.numpy as jnp
from jax import lax
from jax.experimental import pallas as pl
from jax.experimental.pallas import tpu as pltpu
from jax.sharding import PartitionSpec as P


B = 128


def filtered(values, pattern):
    block_rows, block_cols = pattern.shape
    blocked = (
        values.reshape(block_rows, B, block_cols, B) * pattern.astype(jnp.float32)[:, None, :, None]
    )
    return blocked.reshape(block_rows * B, block_cols * B)


def general(density, pattern):
    masked = filtered(density.astype(jnp.float32), pattern).astype(jnp.bfloat16)
    row_count = masked.shape[0]
    col_count = masked.shape[1]
    column = lax.all_gather(masked, "row", axis=0, tiled=True)

    def multiply(factor):
        return jnp.dot(
            lax.all_gather(factor, "col", axis=1, tiled=True),
            column,
            preferred_element_type=jnp.float32,
        )

    squared = filtered(multiply(masked), pattern).astype(jnp.bfloat16)
    cubic_term = filtered(multiply(squared), pattern)
    purified = 3.0 * squared.astype(jnp.float32) - 2.0 * cubic_term
    row_index = lax.axis_index("row") * row_count + jnp.arange(row_count, dtype=jnp.int32)
    col_index = lax.axis_index("col") * col_count + jnp.arange(col_count, dtype=jnp.int32)
    diagonal_sum = jnp.sum(jnp.where(row_index[:, None] == col_index[None, :], purified, 0.0))
    total_trace = lax.psum(diagonal_sum, ("row", "col"))
    occupation = total_trace / (row_count * lax.axis_size("row"))
    return (purified, occupation)


NEAR = (0, 1, 3)
LAST = 2
EXTRA = 16


def piece(left, right):
    rows = right.shape[1]
    return jnp.dot(left[:, :rows], right[0], preferred_element_type=jnp.float32) + jnp.dot(
        left[:, rows:], right[1], preferred_element_type=jnp.float32
    )


def multiply(acc, left, right, fresh):
    if fresh:
        acc[...] = piece(left, right)
    else:
        acc[...] += piece(left, right)


def blocks(rows, columns, body):
    @pl.loop(0, (rows // B) * (columns // B))
    def _(block):
        a = block // (columns // B)
        b = block % (columns // B)
        body(
            a,
            b,
            (pl.ds(pl.multiple_of(a * B, B), B), pl.ds(pl.multiple_of(b * B, B), B)),
        )


def square_early_kernel(where, own, pair, cross_a, cross_b, *refs):
    rights = refs[:8]
    acc, panel, right, left_sem, right_sem = refs[8:]
    row, col = where[0], where[1]
    half = cross_a.shape[0]
    pltpu.make_async_copy(own, panel.at[0], left_sem.at[0]).start()
    pltpu.make_async_copy(pair, panel.at[1], left_sem.at[1]).start()
    pltpu.make_async_copy(cross_a, panel.at[2, :half], left_sem.at[2]).start()
    pltpu.make_async_copy(cross_b, panel.at[2, half:], left_sem.at[2]).start()

    for k in range(8):
        slot = row ^ k
        pltpu.make_async_copy(rights[k], right.at[slot], right_sem.at[slot]).start()
    for i, d in enumerate(NEAR):
        slot = 2 * (col ^ d)
        pltpu.make_async_copy(panel.at[i], panel.at[i], left_sem.at[i]).wait()
        for t in range(2):
            there = right.at[slot + t]
            pltpu.make_async_copy(there, there, right_sem.at[slot + t]).wait()
        multiply(acc, panel.at[i, : acc.shape[0]], right.at[pl.ds(slot, 2)], i == 0)
    slot = 2 * (col ^ LAST)
    for t in range(2):
        there = right.at[slot + t]
        pltpu.make_async_copy(there, there, right_sem.at[slot + t]).wait()


def square_late_kernel(first, where, own, acc_in, right, far, sums_in, squared_ref, sum_ref):
    row, col = where[0], where[1]
    rows, columns = acc_in.shape
    count = squared_ref.shape[0]
    total = acc_in[first : first + count] + piece(
        far.at[:count], right.at[pl.ds(2 * (col ^ LAST), 2)]
    )
    kept = own[rows : rows + EXTRA, :].astype(jnp.float32)
    sums = jnp.zeros((8, columns), jnp.float32)
    for a in range(count // B):
        part = slice(a * B, (a + 1) * B)
        whole = slice(first + a * B, first + (a + 1) * B)
        line = first // B + a
        squared = (total[part] * kept[line : line + 1]).astype(jnp.bfloat16)
        squared_ref[part, :] = squared
        term = squared.astype(jnp.float32) * own[whole, :].astype(jnp.float32)
        sums -= 2.0 * jnp.sum(term.reshape(B // 8, 8, columns), axis=0)
    sum_ref[...] = sums[:, :B]
    for n in range(1, columns // B):
        sum_ref[...] += sums[:, n * B : (n + 1) * B]

    @pl.when(row // 2 == col)
    def _():
        same = lax.broadcasted_iota(jnp.int32, (B, B), 0) == lax.broadcasted_iota(
            jnp.int32, (B, B), 1
        )
        for a in range(count // B):
            start = row * rows - col * columns + first + a * B
            lanes = pl.ds(pl.multiple_of(start, B), B)
            squared = squared_ref[a * B : (a + 1) * B, lanes].astype(jnp.float32)
            term = jnp.where(same, 3.0 * squared, 0.0)
            sum_ref[...] += jnp.sum(term.reshape(B // 8, 8, B), axis=0)

    total_sum = jnp.sum(sum_ref[...], keepdims=True)
    sum_ref[...] = jnp.broadcast_to(total_sum, sum_ref.shape)
    if first:
        sum_ref[...] += sums_in[...]


def square_a_kernel(where, own, acc_in, right, far, squared_ref, sum_ref):
    square_late_kernel(0, where, own, acc_in, right, far, None, squared_ref, sum_ref)


def square_b_kernel(where, own, acc_in, right, far, sums_in, squared_ref, sum_ref):
    first = squared_ref.shape[0]
    square_late_kernel(first, where, own, acc_in, right, far, sums_in, squared_ref, sum_ref)


def add_kernel(left, right, out):
    out[...] = left[...] + right[...]


def tick_kernel(left, out):
    out[...] = left[...]


def add_planes_kernel(own, first, second, third, out):
    out[...] = (own[...] + first[...]) + (second[...] + third[...])


def turn_kernel(where, squared_a, squared_b, same_ref, cross_ref):
    core = where[0] % 2
    half = same_ref.shape[0]
    count = squared_a.shape[0]
    for i, squared in enumerate((squared_a, squared_b)):

        def body(a, b, part):
            for out, h in ((same_ref, core), (cross_ref, 1 - core)):
                lanes = pl.ds(pl.multiple_of(h * half + b * B, B), B)
                there = pl.ds(pl.multiple_of(i * count + a * B, B), B)
                out[part[1], there] = squared[part[0], lanes].T

        blocks(count, half, body)


def own_square_kernel(where, panel, other, far_a, far_b, far_other_a, far_other_b, *refs):
    out, far, far_other = refs
    half = far_a.shape[0]
    for whole, a_half, b_half in ((far, far_a, far_b), (far_other, far_other_a, far_other_b)):
        whole[:half] = a_half[...]
        whole[half:] = b_half[...]
    row, col = where[0], where[1]
    core, chip = row % 2, row // 2
    rows = out.shape[0]
    d = col ^ chip
    for source, last, h in ((panel, far, core), (other, far_other, 1 - core)):
        total = None
        for left, right in [(panel.at[i], source.at[i]) for i in range(3)] + [(far, last)]:
            part = lax.dot_general(
                left[:rows, :],
                right[:rows, :],
                (((1,), (1,)), ((), ())),
                preferred_element_type=jnp.float32,
            )
            total = part if total is None else total + part
        lanes = pl.ds(pl.multiple_of(h * rows, rows), rows)
        near = panel[jnp.minimum(d, 2), rows : rows + EXTRA, lanes].astype(jnp.float32)
        kept = jnp.where(d == LAST, far[rows : rows + EXTRA, lanes].astype(jnp.float32), near)
        for a in range(rows // B):
            out[a * B : (a + 1) * B, lanes] = (
                total[a * B : (a + 1) * B] * kept[a : a + 1]
            ).astype(jnp.bfloat16)


def late_sources(row, col):
    chip = row // 2
    place = col - (col > chip).astype(jnp.int32)
    sources = []
    for i in range(3):
        index = (place + 2 - i) % 3
        other = index + (index >= chip).astype(jnp.int32)
        sources.append(jnp.where(chip == col, col ^ (i + 1), other))
    return sources


def cubic_early_kernel(where, squared_a, squared_b, local_square, right, acc):
    row, col = where[0], where[1]
    chip = row // 2
    half = squared_a.shape[0]
    own_right = right.at[pl.ds(2 * col, 2)]
    acc[:half] = piece(squared_a, own_right)
    acc[half:] = piece(squared_b, own_right)

    @pl.when(chip != col)
    def _():
        multiply(acc, local_square, right.at[pl.ds(2 * chip, 2)], False)


def side_piece(sides, right_all, source, core):
    return sum(
        jnp.dot(ref[...], right_all[2 * source + (core ^ u)], preferred_element_type=jnp.float32)
        for u, ref in enumerate(sides)
    )


def cubic_middle_kernel(where, acc_in, turn1, turn2, right_all, same, cross, acc):
    row, col = where[0], where[1]
    half = turn1.shape[0]
    sources = late_sources(row, col)

    @pl.when(row // 2 == col)
    def _():
        acc[...] = acc_in[...] + side_piece((same, cross), right_all, col ^ 1, row % 2)

    @pl.when(row // 2 != col)
    def _():
        acc[:half] = (
            acc_in[:half]
            + piece(turn1, right_all.at[pl.ds(2 * sources[0], 2)])
            + piece(turn2, right_all.at[pl.ds(2 * sources[1], 2)])
        )
        acc[half:] = acc_in[half:]


def cubic_late_kernel(where, own, squared_a, squared_b, acc, turn1, turn2, right_all, *refs):
    sides, purified_ref, scratch = refs[:4], refs[4], refs[5]
    row, col = where[0], where[1]
    core, chip = row % 2, row // 2
    rows, _ = acc.shape
    half = squared_a.shape[0]
    sources = late_sources(row, col)

    def finish(total, first):
        kept = own[rows : rows + EXTRA, :].astype(jnp.float32)
        squared = squared_b if first else squared_a
        for a in range(half // B):
            part = slice(a * B, (a + 1) * B)
            whole = slice(first + a * B, first + (a + 1) * B)
            line = first // B + a
            wide = squared[part, :].astype(jnp.float32)
            purified_ref[whole, :] = 3.0 * wide - 2.0 * (total[part] * kept[line : line + 1])

    @pl.when(chip != col)
    def _():
        scratch[half:] = acc[half:] + piece(turn1, right_all.at[pl.ds(2 * sources[0], 2)])
        finish(acc, 0)
        finish(
            scratch[half:] + piece(turn2, right_all.at[pl.ds(2 * sources[1], 2)]),
            half,
        )

    @pl.when(chip == col)
    def _():
        scratch[...] = acc[...] + side_piece(sides[:2], right_all, col ^ 2, core)
        total = scratch[...] + side_piece(sides[2:], right_all, col ^ 3, core)
        finish(total[:half], 0)
        finish(total[half:], half)


ANYWHERE = pl.BlockSpec(memory_space=pl.ANY)
SCALARS = pl.BlockSpec(memory_space=pltpu.SMEM)
WHOLE = pl.BlockSpec(memory_space=pltpu.VMEM)
DMA = pltpu.SemaphoreType.DMA


def call(kernel, specs, args, outs, scratch, flops, moved, grant=16):
    return pl.pallas_call(
        kernel,
        out_shape=outs,
        in_specs=specs,
        out_specs=jax.tree.map(lambda _: WHOLE, outs),
        scratch_shapes=scratch,
        compiler_params=pltpu.CompilerParams(vmem_limit_bytes=grant << 20),
        cost_estimate=pl.CostEstimate(flops=flops, bytes_accessed=moved, transcendentals=0),
    )(*args)


def swap(x, k):
    return lax.ppermute(x, "row", [(i, i ^ k) for i in range(8)])


def column_gather(x):
    by_x = swap(x, 2)
    by_y = swap(x, 4)
    core = swap(x, 1)
    by_x_core = swap(by_x, 1)
    by_y_core = swap(by_y, 1)
    diagonal = swap(by_x, 4)
    return [x, core, by_x, by_x_core, by_y, by_y_core, diagonal, swap(diagonal, 1)]


def rotate(x, step):
    pairs = []
    for row in range(8):
        planes = [c for c in range(4) if c != row // 2]
        for i in range(3):
            pairs.append((row * 4 + planes[i], row * 4 + planes[(i + step) % 3]))
    return lax.ppermute(x, ("row", "col"), pairs)


def in_plane(x, source, target, u):
    pairs = []
    for col in range(4):
        for core in range(2):
            here = (col ^ source) * 2 + core
            there = (col ^ target) * 2 + (core ^ u)
            pairs.append((here * 4 + col, there * 4 + col))
    return lax.ppermute(x, ("row", "col"), pairs)


def to_corner(same, cross):
    by_y = [in_plane(same, 2, 0, 0), in_plane(cross, 2, 0, 1)]
    half_way = in_plane(cross, 3, 1, 0)
    by_x = [in_plane(same, 1, 0, 0), in_plane(cross, 1, 0, 1)]
    direct = in_plane(same, 3, 0, 0)
    return [*by_x, *by_y, direct, in_plane(half_way, 1, 0, 1)]


def local(density, pattern):
    masked = filtered(density.astype(jnp.float32), pattern).astype(jnp.bfloat16)
    rows, columns = masked.shape
    row, col = lax.axis_index("row"), lax.axis_index("col")
    where = jnp.stack([row, col]).astype(jnp.int32)
    kept = jnp.repeat(pattern.astype(jnp.bfloat16), B, axis=1)
    kept = jnp.pad(kept, ((0, EXTRA - kept.shape[0]), (0, 0)))
    own = jnp.concatenate([masked, kept], axis=0)
    half = rows // 2
    near, flip = [(i, i ^ 1) for i in range(4)], [(i, i ^ 3) for i in range(4)]
    cross_a = lax.ppermute(own[:half], "col", flip)
    cross_b = lax.ppermute(own[half:], "col", flip)
    pair = lax.ppermute(own, "col", near)
    far_a = lax.ppermute(cross_a, "col", near)
    far_b = lax.ppermute(cross_b, "col", near)
    rights = column_gather(masked)

    flops = 2 * 2 * rows * rows * columns
    size = 2 * rows * columns
    tile = jax.ShapeDtypeStruct((rows, columns), jnp.bfloat16)
    wide = jax.ShapeDtypeStruct((rows, columns), jnp.float32)
    partial, panel, right = call(
        square_early_kernel,
        [SCALARS] + [ANYWHERE] * 12,
        (where, own, pair, cross_a, cross_b, *rights),
        (
            wide,
            jax.ShapeDtypeStruct((3, rows + EXTRA, columns), jnp.bfloat16),
            jax.ShapeDtypeStruct((8, rows, columns), jnp.bfloat16),
        ),
        [DMA((3,)), DMA((8,))],
        3 * flops,
        24 * size,
    )
    other = swap(panel, 1)
    half_tile = jax.ShapeDtypeStruct((half, columns), jnp.bfloat16)
    sums_shape = jax.ShapeDtypeStruct((8, B), jnp.float32)
    squared_a, sums = call(
        square_a_kernel,
        [SCALARS] + [WHOLE] * 4,
        (where, own, partial, right, far_a),
        (half_tile, sums_shape),
        [],
        flops // 2,
        6 * size,
    )
    turns_a = [rotate(squared_a, i) for i in (1, 2)]
    sums = call(tick_kernel, [WHOLE], (sums,), sums_shape, [], 0, 8 * sums.size, 1)
    squared_b, sums = call(
        square_b_kernel,
        [SCALARS] + [WHOLE] * 5,
        (where, own, partial, right, far_b, sums),
        (half_tile, sums_shape),
        [],
        flops // 2,
        6 * size,
    )
    turns_b = [rotate(squared_b, i) for i in (1, 2)]
    total = sums

    def add(left, right):
        return call(
            add_kernel,
            [WHOLE] * 2,
            (left, right),
            jax.ShapeDtypeStruct(left.shape, left.dtype),
            [],
            left.size,
            12 * left.size,
            1,
        )

    for k in (1, 2, 4):
        total = add(total, swap(total, k))
    quarter = jax.ShapeDtypeStruct((rows, rows), jnp.bfloat16)
    turned = call(
        turn_kernel,
        [SCALARS, WHOLE, WHOLE],
        (where, squared_a, squared_b),
        (quarter, quarter),
        [],
        0,
        2 * size,
    )
    sides = to_corner(*turned)
    local_square = call(
        own_square_kernel,
        [SCALARS] + [WHOLE] * 6,
        (where, panel, other, far_a, far_b, swap(far_a, 1), swap(far_b, 1)),
        tile,
        [pltpu.VMEM((rows + EXTRA, columns), jnp.bfloat16)] * 2,
        4 * flops,
        9 * size,
        16,
    )
    cubic = call(
        cubic_early_kernel,
        [SCALARS] + [WHOLE] * 4,
        (where, squared_a, squared_b, local_square, right),
        wide,
        [],
        2 * flops,
        8 * size,
        16,
    )
    cubic = call(
        cubic_middle_kernel,
        [SCALARS] + [WHOLE] * 6,
        (where, cubic, *turns_a, right, *sides[:2]),
        wide,
        [],
        flops,
        9 * size,
    )
    planes = [lax.ppermute(total, "col", [(i, i ^ k) for i in range(4)]) for k in (1, 2, 3)]
    total = call(
        add_planes_kernel,
        [WHOLE] * 4,
        (total, *planes),
        jax.ShapeDtypeStruct(total.shape, total.dtype),
        [],
        3 * total.size,
        20 * total.size,
        1,
    )
    purified = call(
        cubic_late_kernel,
        [SCALARS] + [WHOLE] * 11,
        (where, own, squared_a, squared_b, cubic, *turns_b, right, *sides[2:]),
        wide,
        [pltpu.VMEM((rows, columns), jnp.float32)],
        2 * flops,
        16 * size,
    )
    return (purified, total[0, 0] / (rows * lax.axis_size("row")))


def solution(mesh):
    placed = (P("row", "col"), P("row", "col"))
    body = local if (mesh.shape["row"], mesh.shape["col"]) == (8, 4) else general
    return jax.shard_map(
        body, mesh=mesh, in_specs=placed, out_specs=(P("row", "col"), P()), check_vma=False
    )
```

```python
import functools

import jax
import jax.numpy as jnp
from jax import lax
from jax.experimental import pallas as pl
from jax.experimental.pallas import tpu as pltpu
from jax.sharding import PartitionSpec as P


B = 128


def filtered(values, pattern):
    block_rows, block_cols = pattern.shape
    blocked = (
        values.reshape(block_rows, B, block_cols, B) * pattern.astype(jnp.float32)[:, None, :, None]
    )
    return blocked.reshape(block_rows * B, block_cols * B)


def general(density, pattern):
    masked = filtered(density.astype(jnp.float32), pattern).astype(jnp.bfloat16)
    row_count = masked.shape[0]
    col_count = masked.shape[1]
    column = lax.all_gather(masked, "row", axis=0, tiled=True)

    def multiply(factor):
        return jnp.dot(
            lax.all_gather(factor, "col", axis=1, tiled=True),
            column,
            preferred_element_type=jnp.float32,
        )

    squared = filtered(multiply(masked), pattern).astype(jnp.bfloat16)
    cubic_term = filtered(multiply(squared), pattern)
    purified = 3.0 * squared.astype(jnp.float32) - 2.0 * cubic_term
    row_index = lax.axis_index("row") * row_count + jnp.arange(row_count, dtype=jnp.int32)
    col_index = lax.axis_index("col") * col_count + jnp.arange(col_count, dtype=jnp.int32)
    diagonal_sum = jnp.sum(jnp.where(row_index[:, None] == col_index[None, :], purified, 0.0))
    total_trace = lax.psum(diagonal_sum, ("row", "col"))
    occupation = total_trace / (row_count * lax.axis_size("row"))
    return (purified, occupation)


NEAR = (0, 1, 3)
LAST = 2


def piece(left, right):
    rows = right.shape[1]
    return jnp.dot(left[:rows, :rows], right[0], preferred_element_type=jnp.float32) + jnp.dot(
        left[:rows, rows:], right[1], preferred_element_type=jnp.float32
    )


def multiply(acc, left, right, fresh):
    if fresh:
        acc[...] = piece(left, right)
    else:
        acc[...] += piece(left, right)


def blocks(rows, columns, body):
    @pl.loop(0, (rows // B) * (columns // B))
    def _(block):
        a = block // (columns // B)
        b = block % (columns // B)
        body(
            a,
            b,
            (pl.ds(pl.multiple_of(a * B, B), B), pl.ds(pl.multiple_of(b * B, B), B)),
        )


def mask_kernel(pattern, density, out, kept_ref):
    rows, columns = out.shape
    for a in range(rows // B):
        for b in range(columns // B):
            part = (slice(a * B, (a + 1) * B), slice(b * B, (b + 1) * B))
            kept = pattern[a, b].astype(jnp.float32)
            kept_ref[a : a + 1, part[1]] = jnp.full((1, B), kept, jnp.float32)
            out[part] = (density[part].astype(jnp.float32) * kept).astype(jnp.bfloat16)


def square_early_kernel(where, own, pair, cross, *refs):
    rights = refs[:8]
    acc, panel, right, left_sem, right_sem = refs[8:]
    row, col = where[0], where[1]
    for i, ref in enumerate((own, pair, cross)):
        pltpu.make_async_copy(ref, panel.at[i], left_sem.at[i]).start()

    for k in range(8):
        slot = row ^ k
        pltpu.make_async_copy(rights[k], right.at[slot], right_sem.at[slot]).start()
    for i, d in enumerate(NEAR):
        slot = 2 * (col ^ d)
        pltpu.make_async_copy(panel.at[i], panel.at[i], left_sem.at[i]).wait()
        for t in range(2):
            there = right.at[slot + t]
            pltpu.make_async_copy(there, there, right_sem.at[slot + t]).wait()
        multiply(acc, panel.at[i], right.at[pl.ds(slot, 2)], i == 0)
    slot = 2 * (col ^ LAST)
    for t in range(2):
        there = right.at[slot + t]
        pltpu.make_async_copy(there, there, right_sem.at[slot + t]).wait()


def square_late_kernel(where, kept_ref, own, acc_in, right, far, squared_ref, sum_ref):
    row, col = where[0], where[1]
    rows, columns = squared_ref.shape
    total = acc_in[...] + piece(far, right.at[pl.ds(2 * (col ^ LAST), 2)])
    kept = kept_ref[...]
    sums = jnp.zeros((8, columns), jnp.float32)
    for a in range(rows // B):
        part = slice(a * B, (a + 1) * B)
        squared = (total[part] * kept[a : a + 1]).astype(jnp.bfloat16)
        squared_ref[part, :] = squared
        term = squared.astype(jnp.float32) * own[part, :].astype(jnp.float32)
        sums -= 2.0 * jnp.sum(term.reshape(B // 8, 8, columns), axis=0)
    sum_ref[...] = sums[:, :B]
    for n in range(1, columns // B):
        sum_ref[...] += sums[:, n * B : (n + 1) * B]

    @pl.when(row // 2 == col)
    def _():
        same = lax.broadcasted_iota(jnp.int32, (B, B), 0) == lax.broadcasted_iota(
            jnp.int32, (B, B), 1
        )
        for a in range(rows // B):
            lanes = pl.ds(pl.multiple_of(row * rows - col * columns + a * B, B), B)
            squared = squared_ref[a * B : (a + 1) * B, lanes].astype(jnp.float32)
            term = jnp.where(same, 3.0 * squared, 0.0)
            sum_ref[...] += jnp.sum(term.reshape(B // 8, 8, B), axis=0)

    sum_ref[...] = jnp.broadcast_to(jnp.sum(sum_ref[...], keepdims=True), sum_ref.shape)


def add_kernel(left, right, out):
    out[...] = left[...] + right[...]


def add_planes_kernel(order, own, first, second, third, out):
    total = (own[...] + first[...]) + (second[...] + third[...])
    out[0, 0] = total[0, 0] / order


def turn_kernel(where, squared, same_ref, cross_ref):
    core = where[0] % 2
    half = same_ref.shape[0]

    def body(a, b, part):
        for out, h in ((same_ref, core), (cross_ref, 1 - core)):
            lanes = pl.ds(pl.multiple_of(h * half + b * B, B), B)
            out[part[1], part[0]] = squared[part[0], lanes].T

    blocks(half, half, body)


def own_square_kernel(where, own_pattern, *refs):
    patterns, (panel, other, far, far_other, out) = (own_pattern, *refs[:3]), refs[3:]
    row, col = where[0], where[1]
    core, chip = row % 2, row // 2
    rows = out.shape[0]
    d = col ^ chip
    for source, last, h in ((panel, far, core), (other, far_other, 1 - core)):
        total = None
        for left, right in [(panel.at[i], source.at[i]) for i in range(3)] + [(far, last)]:
            part = lax.dot_general(
                left[:rows, :],
                right[:rows, :],
                (((1,), (1,)), ((), ())),
                preferred_element_type=jnp.float32,
            )
            total = part if total is None else total + part
        for a in range(rows // B):
            for b in range(rows // B):
                place = h * (rows // B) + b
                kept = jnp.int32(0)
                for i, pattern in enumerate(patterns):
                    kept = jnp.where(d == i, pattern[a, place], kept)
                lanes = pl.ds(pl.multiple_of(h * rows + b * B, B), B)
                out[a * B : (a + 1) * B, lanes] = (
                    total[a * B : (a + 1) * B, b * B : (b + 1) * B] * kept.astype(jnp.float32)
                ).astype(jnp.bfloat16)


def late_sources(row, col):
    chip = row // 2
    place = col - (col > chip).astype(jnp.int32)
    sources = []
    for i in range(3):
        index = (place + 2 - i) % 3
        other = index + (index >= chip).astype(jnp.int32)
        sources.append(jnp.where(chip == col, col ^ (i + 1), other))
    return sources


def cubic_early_kernel(where, squared, local_square, right, acc):
    row, col = where[0], where[1]
    chip = row // 2
    multiply(acc, squared, right.at[pl.ds(2 * col, 2)], True)

    @pl.when(chip != col)
    def _():
        multiply(acc, local_square, right.at[pl.ds(2 * chip, 2)], False)


def side_piece(sides, right_all, source, core):
    return sum(
        jnp.dot(ref[...], right_all[2 * source + (core ^ u)], preferred_element_type=jnp.float32)
        for u, ref in enumerate(sides)
    )


def cubic_middle_kernel(where, acc_in, right_all, same, cross, acc):
    row, col = where[0], where[1]

    @pl.when(row // 2 == col)
    def _():
        acc[...] = acc_in[...] + side_piece((same, cross), right_all, col ^ 1, row % 2)

    @pl.when(row // 2 != col)
    def _():
        acc[...] = acc_in[...]


def cubic_late_kernel(where, kept_ref, squared, acc, turn1, turn2, right_all, *refs):
    sides, purified_ref, scratch = refs[:4], refs[4], refs[5]
    row, col = where[0], where[1]
    core, chip = row % 2, row // 2
    rows, _ = squared.shape
    sources = late_sources(row, col)

    def finish(first, second):
        scratch[...] = acc[...] + first
        total = scratch[...] + second()
        kept = kept_ref[...]
        for a in range(rows // B):
            part = slice(a * B, (a + 1) * B)
            wide = squared[part, :].astype(jnp.float32)
            purified_ref[part, :] = 3.0 * wide - 2.0 * (total[part] * kept[a : a + 1])

    @pl.when(chip != col)
    def _():
        finish(
            piece(turn1, right_all.at[pl.ds(2 * sources[0], 2)]),
            lambda: piece(turn2, right_all.at[pl.ds(2 * sources[1], 2)]),
        )

    @pl.when(chip == col)
    def _():
        finish(
            side_piece(sides[:2], right_all, col ^ 2, core),
            lambda: side_piece(sides[2:], right_all, col ^ 3, core),
        )


ANYWHERE = pl.BlockSpec(memory_space=pl.ANY)
SCALARS = pl.BlockSpec(memory_space=pltpu.SMEM)
WHOLE = pl.BlockSpec(memory_space=pltpu.VMEM)
DMA = pltpu.SemaphoreType.DMA


def call(kernel, specs, args, outs, scratch, flops, moved, grant=16, out_spec=WHOLE):
    return pl.pallas_call(
        kernel,
        out_shape=outs,
        in_specs=specs,
        out_specs=jax.tree.map(lambda _: out_spec, outs),
        scratch_shapes=scratch,
        compiler_params=pltpu.CompilerParams(vmem_limit_bytes=grant << 20),
        cost_estimate=pl.CostEstimate(flops=flops, bytes_accessed=moved, transcendentals=0),
    )(*args)


def swap(x, k):
    return lax.ppermute(x, "row", [(i, i ^ k) for i in range(8)])


def column_gather(x):
    by_x = swap(x, 2)
    by_y = swap(x, 4)
    core = swap(x, 1)
    by_x_core = swap(by_x, 1)
    by_y_core = swap(by_y, 1)
    diagonal = swap(by_x, 4)
    return [x, core, by_x, by_x_core, by_y, by_y_core, diagonal, swap(diagonal, 1)]


def rotate(x, step):
    pairs = []
    for row in range(8):
        planes = [c for c in range(4) if c != row // 2]
        for i in range(3):
            pairs.append((row * 4 + planes[i], row * 4 + planes[(i + step) % 3]))
    return lax.ppermute(x, ("row", "col"), pairs)


def in_plane(x, source, target, u):
    pairs = []
    for col in range(4):
        for core in range(2):
            here = (col ^ source) * 2 + core
            there = (col ^ target) * 2 + (core ^ u)
            pairs.append((here * 4 + col, there * 4 + col))
    return lax.ppermute(x, ("row", "col"), pairs)


def to_corner(same, cross):
    by_y = [in_plane(same, 2, 0, 0), in_plane(cross, 2, 0, 1)]
    half_way = in_plane(cross, 3, 1, 0)
    by_x = [in_plane(same, 1, 0, 0), in_plane(cross, 1, 0, 1)]
    direct = in_plane(same, 3, 0, 0)
    return [*by_x, *by_y, direct, in_plane(half_way, 1, 0, 1)]


def local(density, pattern):
    rows, columns = density.shape
    row, col = lax.axis_index("row"), lax.axis_index("col")
    where = jnp.stack([row, col]).astype(jnp.int32)
    tile = jax.ShapeDtypeStruct((rows, columns), jnp.bfloat16)
    own, kept = call(
        mask_kernel,
        [SCALARS, WHOLE],
        (pattern, density),
        (tile, jax.ShapeDtypeStruct((8, columns), jnp.float32)),
        [],
        rows * columns,
        4 * rows * columns,
    )
    cross = lax.ppermute(own, "col", [(i, i ^ 3) for i in range(4)])
    pair = lax.ppermute(own, "col", [(i, i ^ 1) for i in range(4)])
    far = lax.ppermute(cross, "col", [(i, i ^ 1) for i in range(4)])
    patterns = [lax.ppermute(pattern, "col", [(i, i ^ k) for i in range(4)]) for k in (1, 2, 3)]
    rights = column_gather(own)

    flops = 2 * 2 * rows * rows * columns
    size = 2 * rows * columns
    wide = jax.ShapeDtypeStruct((rows, columns), jnp.float32)
    partial, panel, right = call(
        square_early_kernel,
        [SCALARS] + [ANYWHERE] * 11,
        (where, own, pair, cross, *rights),
        (
            wide,
            jax.ShapeDtypeStruct((3, rows, columns), jnp.bfloat16),
            jax.ShapeDtypeStruct((8, rows, columns), jnp.bfloat16),
        ),
        [DMA((3,)), DMA((8,))],
        3 * flops,
        24 * size,
    )
    other = swap(panel, 1)
    squared, sums = call(
        square_late_kernel,
        [SCALARS] + [WHOLE] * 5,
        (where, kept, own, partial, right, far),
        (tile, jax.ShapeDtypeStruct((8, B), jnp.float32)),
        [],
        flops,
        8 * size,
    )
    turns = [rotate(squared, 1), rotate(squared, 2)]
    total = sums

    def add(left, right):
        return call(
            add_kernel,
            [WHOLE] * 2,
            (left, right),
            jax.ShapeDtypeStruct(left.shape, left.dtype),
            [],
            left.size,
            12 * left.size,
            1,
        )

    for k in (1, 2, 4):
        total = add(total, swap(total, k))
    quarter = jax.ShapeDtypeStruct((rows, rows), jnp.bfloat16)
    turned = call(
        turn_kernel,
        [SCALARS, WHOLE],
        (where, squared),
        (quarter, quarter),
        [],
        0,
        2 * size,
    )
    sides = to_corner(*turned)
    local_square = call(
        own_square_kernel,
        [SCALARS] * 5 + [WHOLE] * 4,
        (where, pattern, *patterns, panel, other, far, swap(far, 1)),
        tile,
        [],
        4 * flops,
        9 * size,
        16,
    )
    cubic = call(
        cubic_early_kernel,
        [SCALARS] + [WHOLE] * 3,
        (where, squared, local_square, right),
        wide,
        [],
        2 * flops,
        8 * size,
        16,
    )
    cubic = call(
        cubic_middle_kernel,
        [SCALARS] + [WHOLE] * 4,
        (where, cubic, right, *sides[:2]),
        wide,
        [],
        flops,
        9 * size,
    )
    planes = [lax.ppermute(total, "col", [(i, i ^ k) for i in range(4)]) for k in (1, 2, 3)]
    occupation = call(
        functools.partial(add_planes_kernel, rows * lax.axis_size("row")),
        [WHOLE] * 4,
        (total, *planes),
        jax.ShapeDtypeStruct((1, 1), jnp.float32),
        [],
        3 * total.size,
        20 * total.size,
        1,
        SCALARS,
    )
    purified = call(
        cubic_late_kernel,
        [SCALARS] + [WHOLE] * 10,
        (where, kept, squared, cubic, *turns, right, *sides[2:]),
        wide,
        [pltpu.VMEM((rows, columns), jnp.float32)],
        2 * flops,
        16 * size,
    )
    return (purified, occupation.reshape(()))


def solution(mesh):
    placed = (P("row", "col"), P("row", "col"))
    body = local if (mesh.shape["row"], mesh.shape["col"]) == (8, 4) else general
    return jax.shard_map(
        body, mesh=mesh, in_specs=placed, out_specs=(P("row", "col"), P()), check_vma=False
    )
```

```python
import functools

import jax
import jax.numpy as jnp
from jax import lax
from jax.experimental import pallas as pl
from jax.experimental.pallas import tpu as pltpu
from jax.sharding import PartitionSpec as P


B = 128


def filtered(values, pattern):
    block_rows, block_cols = pattern.shape
    blocked = (
        values.reshape(block_rows, B, block_cols, B) * pattern.astype(jnp.float32)[:, None, :, None]
    )
    return blocked.reshape(block_rows * B, block_cols * B)


def general(density, pattern):
    masked = filtered(density.astype(jnp.float32), pattern).astype(jnp.bfloat16)
    row_count = masked.shape[0]
    col_count = masked.shape[1]
    column = lax.all_gather(masked, "row", axis=0, tiled=True)

    def multiply(factor):
        return jnp.dot(
            lax.all_gather(factor, "col", axis=1, tiled=True),
            column,
            preferred_element_type=jnp.float32,
        )

    squared = filtered(multiply(masked), pattern).astype(jnp.bfloat16)
    cubic_term = filtered(multiply(squared), pattern)
    purified = 3.0 * squared.astype(jnp.float32) - 2.0 * cubic_term
    row_index = lax.axis_index("row") * row_count + jnp.arange(row_count, dtype=jnp.int32)
    col_index = lax.axis_index("col") * col_count + jnp.arange(col_count, dtype=jnp.int32)
    diagonal_sum = jnp.sum(jnp.where(row_index[:, None] == col_index[None, :], purified, 0.0))
    total_trace = lax.psum(diagonal_sum, ("row", "col"))
    occupation = total_trace / (row_count * lax.axis_size("row"))
    return (purified, occupation)


NEAR = (0, 1, 3)
LAST = 2


def piece(left, right):
    rows = right.shape[1]
    return jnp.dot(left[:rows, :rows], right[0], preferred_element_type=jnp.float32) + jnp.dot(
        left[:rows, rows:], right[1], preferred_element_type=jnp.float32
    )


def multiply(acc, left, right, fresh):
    if fresh:
        acc[...] = piece(left, right)
    else:
        acc[...] += piece(left, right)


def blocks(rows, columns, body):
    @pl.loop(0, (rows // B) * (columns // B))
    def _(block):
        a = block // (columns // B)
        b = block % (columns // B)
        body(
            a,
            b,
            (pl.ds(pl.multiple_of(a * B, B), B), pl.ds(pl.multiple_of(b * B, B), B)),
        )


def mask_kernel(pattern, density, out, kept_ref):
    rows, columns = out.shape
    for a in range(rows // B):
        for b in range(columns // B):
            part = (slice(a * B, (a + 1) * B), slice(b * B, (b + 1) * B))
            kept = pattern[a, b].astype(jnp.float32)
            kept_ref[a : a + 1, part[1]] = jnp.full((1, B), kept, jnp.float32)
            out[part] = (density[part].astype(jnp.float32) * kept).astype(jnp.bfloat16)


def square_early_kernel(where, own, pair, cross, *refs):
    rights = refs[:8]
    acc, panel, right, left_sem, right_sem = refs[8:]
    row, col = where[0], where[1]
    for i, ref in enumerate((own, pair, cross)):
        pltpu.make_async_copy(ref, panel.at[i], left_sem.at[i]).start()

    for k in range(8):
        slot = row ^ k
        pltpu.make_async_copy(rights[k], right.at[slot], right_sem.at[slot]).start()
    for i, d in enumerate(NEAR):
        slot = 2 * (col ^ d)
        pltpu.make_async_copy(panel.at[i], panel.at[i], left_sem.at[i]).wait()
        for t in range(2):
            there = right.at[slot + t]
            pltpu.make_async_copy(there, there, right_sem.at[slot + t]).wait()
        multiply(acc, panel.at[i], right.at[pl.ds(slot, 2)], i == 0)
    slot = 2 * (col ^ LAST)
    for t in range(2):
        there = right.at[slot + t]
        pltpu.make_async_copy(there, there, right_sem.at[slot + t]).wait()


def square_late_kernel(where, kept_ref, own, acc_in, right, far, squared_ref, sum_ref):
    row, col = where[0], where[1]
    rows, columns = squared_ref.shape
    total = acc_in[...] + piece(far, right.at[pl.ds(2 * (col ^ LAST), 2)])
    kept = kept_ref[...]
    sums = jnp.zeros((8, columns), jnp.float32)
    for a in range(rows // B):
        part = slice(a * B, (a + 1) * B)
        squared = (total[part] * kept[a : a + 1]).astype(jnp.bfloat16)
        squared_ref[part, :] = squared
        term = squared.astype(jnp.float32) * own[part, :].astype(jnp.float32)
        sums -= 2.0 * jnp.sum(term.reshape(B // 8, 8, columns), axis=0)
    sum_ref[...] = sums[:, :B]
    for n in range(1, columns // B):
        sum_ref[...] += sums[:, n * B : (n + 1) * B]

    @pl.when(row // 2 == col)
    def _():
        same = lax.broadcasted_iota(jnp.int32, (B, B), 0) == lax.broadcasted_iota(
            jnp.int32, (B, B), 1
        )
        for a in range(rows // B):
            lanes = pl.ds(pl.multiple_of(row * rows - col * columns + a * B, B), B)
            squared = squared_ref[a * B : (a + 1) * B, lanes].astype(jnp.float32)
            term = jnp.where(same, 3.0 * squared, 0.0)
            sum_ref[...] += jnp.sum(term.reshape(B // 8, 8, B), axis=0)

    sum_ref[...] = jnp.broadcast_to(jnp.sum(sum_ref[...], keepdims=True), sum_ref.shape)


def add_kernel(left, right, out):
    out[...] = left[...] + right[...]


def add_planes_kernel(order, own, first, second, third, out):
    total = (own[...] + first[...]) + (second[...] + third[...])
    out[0, 0] = total[0, 0] / order


def turn_kernel(where, squared, same_ref, cross_ref):
    core = where[0] % 2
    half = same_ref.shape[0]

    def body(a, b, part):
        for out, h in ((same_ref, core), (cross_ref, 1 - core)):
            lanes = pl.ds(pl.multiple_of(h * half + b * B, B), B)
            out[part[1], part[0]] = squared[part[0], lanes].T

    blocks(half, half, body)


def own_square_kernel(where, own_pattern, *refs):
    patterns, (panel, other, far, far_other, out) = (own_pattern, *refs[:3]), refs[3:]
    row, col = where[0], where[1]
    core, chip = row % 2, row // 2
    rows = out.shape[0]
    d = col ^ chip
    for source, last, h in ((panel, far, core), (other, far_other, 1 - core)):
        total = None
        for left, right in [(panel.at[i], source.at[i]) for i in range(3)] + [(far, last)]:
            part = lax.dot_general(
                left[:rows, :],
                right[:rows, :],
                (((1,), (1,)), ((), ())),
                preferred_element_type=jnp.float32,
            )
            total = part if total is None else total + part
        for a in range(rows // B):
            for b in range(rows // B):
                place = h * (rows // B) + b
                kept = jnp.int32(0)
                for i, pattern in enumerate(patterns):
                    kept = jnp.where(d == i, pattern[a, place], kept)
                lanes = pl.ds(pl.multiple_of(h * rows + b * B, B), B)
                out[a * B : (a + 1) * B, lanes] = (
                    total[a * B : (a + 1) * B, b * B : (b + 1) * B] * kept.astype(jnp.float32)
                ).astype(jnp.bfloat16)


def late_sources(row, col):
    chip = row // 2
    place = col - (col > chip).astype(jnp.int32)
    sources = []
    for i in range(3):
        index = (place + 2 - i) % 3
        other = index + (index >= chip).astype(jnp.int32)
        sources.append(jnp.where(chip == col, col ^ (i + 1), other))
    return sources


def cubic_early_kernel(where, squared, local_square, right, acc):
    row, col = where[0], where[1]
    chip = row // 2
    multiply(acc, squared, right.at[pl.ds(2 * col, 2)], True)

    @pl.when(chip != col)
    def _():
        multiply(acc, local_square, right.at[pl.ds(2 * chip, 2)], False)


def side_piece(sides, right_all, source, core):
    return sum(
        jnp.dot(ref[...], right_all[2 * source + (core ^ u)], preferred_element_type=jnp.float32)
        for u, ref in enumerate(sides)
    )


def cubic_middle_kernel(where, acc_in, turn, right_all, same, cross, acc):
    row, col = where[0], where[1]
    source = late_sources(row, col)[0]

    @pl.when(row // 2 == col)
    def _():
        acc[...] = acc_in[...] + side_piece((same, cross), right_all, col ^ 1, row % 2)

    @pl.when(row // 2 != col)
    def _():
        acc[...] = acc_in[...] + piece(turn, right_all.at[pl.ds(2 * source, 2)])


def cubic_corner_kernel(where, acc_in, right_all, *refs):
    sides, acc, scratch = refs[:4], refs[4], refs[5]
    row, col = where[0], where[1]
    core = row % 2

    @pl.when(row // 2 == col)
    def _():
        scratch[...] = acc_in[...] + side_piece(sides[2:], right_all, col ^ 3, core)
        acc[...] = scratch[...] + side_piece(sides[:2], right_all, col ^ 2, core)

    @pl.when(row // 2 != col)
    def _():
        acc[...] = acc_in[...]


def cubic_late_kernel(where, kept_ref, squared, acc, turn, right_all, purified_ref):
    row, col = where[0], where[1]
    rows, _ = squared.shape
    source = late_sources(row, col)[1]

    def finish(total):
        kept = kept_ref[...]
        for a in range(rows // B):
            part = slice(a * B, (a + 1) * B)
            wide = squared[part, :].astype(jnp.float32)
            purified_ref[part, :] = 3.0 * wide - 2.0 * (total[part] * kept[a : a + 1])

    @pl.when(row // 2 != col)
    def _():
        finish(acc[...] + piece(turn, right_all.at[pl.ds(2 * source, 2)]))

    @pl.when(row // 2 == col)
    def _():
        finish(acc)


ANYWHERE = pl.BlockSpec(memory_space=pl.ANY)
SCALARS = pl.BlockSpec(memory_space=pltpu.SMEM)
WHOLE = pl.BlockSpec(memory_space=pltpu.VMEM)
DMA = pltpu.SemaphoreType.DMA


def call(kernel, specs, args, outs, scratch, flops, moved, grant=16, out_spec=WHOLE):
    return pl.pallas_call(
        kernel,
        out_shape=outs,
        in_specs=specs,
        out_specs=jax.tree.map(lambda _: out_spec, outs),
        scratch_shapes=scratch,
        compiler_params=pltpu.CompilerParams(vmem_limit_bytes=grant << 20),
        cost_estimate=pl.CostEstimate(flops=flops, bytes_accessed=moved, transcendentals=0),
    )(*args)


def swap(x, k):
    return lax.ppermute(x, "row", [(i, i ^ k) for i in range(8)])


def column_gather(x):
    by_x = swap(x, 2)
    by_y = swap(x, 4)
    core = swap(x, 1)
    by_x_core = swap(by_x, 1)
    by_y_core = swap(by_y, 1)
    diagonal = swap(by_x, 4)
    return [x, core, by_x, by_x_core, by_y, by_y_core, diagonal, swap(diagonal, 1)]


def rotate(x, step):
    pairs = []
    for row in range(8):
        planes = [c for c in range(4) if c != row // 2]
        for i in range(3):
            pairs.append((row * 4 + planes[i], row * 4 + planes[(i + step) % 3]))
    return lax.ppermute(x, ("row", "col"), pairs)


def in_plane(x, source, target, u):
    pairs = []
    for col in range(4):
        for core in range(2):
            here = (col ^ source) * 2 + core
            there = (col ^ target) * 2 + (core ^ u)
            pairs.append((here * 4 + col, there * 4 + col))
    return lax.ppermute(x, ("row", "col"), pairs)


def to_corner(same, cross):
    by_y = [in_plane(same, 2, 0, 0), in_plane(cross, 2, 0, 1)]
    half_way = in_plane(cross, 3, 1, 0)
    by_x = [in_plane(same, 1, 0, 0), in_plane(cross, 1, 0, 1)]
    direct = in_plane(same, 3, 0, 0)
    return [*by_x, *by_y, direct, in_plane(half_way, 1, 0, 1)]


def local(density, pattern):
    rows, columns = density.shape
    row, col = lax.axis_index("row"), lax.axis_index("col")
    where = jnp.stack([row, col]).astype(jnp.int32)
    tile = jax.ShapeDtypeStruct((rows, columns), jnp.bfloat16)
    own, kept = call(
        mask_kernel,
        [SCALARS, WHOLE],
        (pattern, density),
        (tile, jax.ShapeDtypeStruct((8, columns), jnp.float32)),
        [],
        rows * columns,
        4 * rows * columns,
    )
    cross = lax.ppermute(own, "col", [(i, i ^ 3) for i in range(4)])
    pair = lax.ppermute(own, "col", [(i, i ^ 1) for i in range(4)])
    far = lax.ppermute(cross, "col", [(i, i ^ 1) for i in range(4)])
    patterns = [lax.ppermute(pattern, "col", [(i, i ^ k) for i in range(4)]) for k in (1, 2, 3)]
    rights = column_gather(own)

    flops = 2 * 2 * rows * rows * columns
    size = 2 * rows * columns
    wide = jax.ShapeDtypeStruct((rows, columns), jnp.float32)
    partial, panel, right = call(
        square_early_kernel,
        [SCALARS] + [ANYWHERE] * 11,
        (where, own, pair, cross, *rights),
        (
            wide,
            jax.ShapeDtypeStruct((3, rows, columns), jnp.bfloat16),
            jax.ShapeDtypeStruct((8, rows, columns), jnp.bfloat16),
        ),
        [DMA((3,)), DMA((8,))],
        3 * flops,
        24 * size,
    )
    other = swap(panel, 1)
    squared, sums = call(
        square_late_kernel,
        [SCALARS] + [WHOLE] * 5,
        (where, kept, own, partial, right, far),
        (tile, jax.ShapeDtypeStruct((8, B), jnp.float32)),
        [],
        flops,
        8 * size,
    )
    turns = [rotate(squared, 1), rotate(squared, 2)]
    total = sums

    def add(left, right):
        return call(
            add_kernel,
            [WHOLE] * 2,
            (left, right),
            jax.ShapeDtypeStruct(left.shape, left.dtype),
            [],
            left.size,
            12 * left.size,
            1,
        )

    for k in (1, 2, 4):
        total = add(total, swap(total, k))
    quarter = jax.ShapeDtypeStruct((rows, rows), jnp.bfloat16)
    turned = call(
        turn_kernel,
        [SCALARS, WHOLE],
        (where, squared),
        (quarter, quarter),
        [],
        0,
        2 * size,
    )
    sides = to_corner(*turned)
    local_square = call(
        own_square_kernel,
        [SCALARS] * 5 + [WHOLE] * 4,
        (where, pattern, *patterns, panel, other, far, swap(far, 1)),
        tile,
        [],
        4 * flops,
        9 * size,
        16,
    )
    cubic = call(
        cubic_early_kernel,
        [SCALARS] + [WHOLE] * 3,
        (where, squared, local_square, right),
        wide,
        [],
        2 * flops,
        8 * size,
        16,
    )
    cubic = call(
        cubic_middle_kernel,
        [SCALARS] + [WHOLE] * 5,
        (where, cubic, turns[0], right, *sides[:2]),
        wide,
        [],
        flops,
        9 * size,
    )
    planes = [lax.ppermute(total, "col", [(i, i ^ k) for i in range(4)]) for k in (1, 2, 3)]
    occupation = call(
        functools.partial(add_planes_kernel, rows * lax.axis_size("row")),
        [WHOLE] * 4,
        (total, *planes),
        jax.ShapeDtypeStruct((1, 1), jnp.float32),
        [],
        3 * total.size,
        20 * total.size,
        1,
        SCALARS,
    )
    cubic = call(
        cubic_corner_kernel,
        [SCALARS] + [WHOLE] * 6,
        (where, cubic, right, *sides[2:]),
        wide,
        [pltpu.VMEM((rows, columns), jnp.float32)],
        2 * flops,
        12 * size,
    )
    purified = call(
        cubic_late_kernel,
        [SCALARS] + [WHOLE] * 5,
        (where, kept, squared, cubic, turns[1], right),
        wide,
        [],
        flops,
        12 * size,
    )
    return (purified, occupation.reshape(()))


def solution(mesh):
    placed = (P("row", "col"), P("row", "col"))
    body = local if (mesh.shape["row"], mesh.shape["col"]) == (8, 4) else general
    return jax.shard_map(
        body, mesh=mesh, in_specs=placed, out_specs=(P("row", "col"), P()), check_vma=False
    )
```

```python
import functools

import jax
import jax.numpy as jnp
from jax import lax
from jax.experimental import pallas as pl
from jax.experimental.pallas import tpu as pltpu
from jax.sharding import PartitionSpec as P


B = 128


def filtered(values, pattern):
    block_rows, block_cols = pattern.shape
    blocked = (
        values.reshape(block_rows, B, block_cols, B) * pattern.astype(jnp.float32)[:, None, :, None]
    )
    return blocked.reshape(block_rows * B, block_cols * B)


def general(density, pattern):
    masked = filtered(density.astype(jnp.float32), pattern).astype(jnp.bfloat16)
    row_count = masked.shape[0]
    col_count = masked.shape[1]
    column = lax.all_gather(masked, "row", axis=0, tiled=True)

    def multiply(factor):
        return jnp.dot(
            lax.all_gather(factor, "col", axis=1, tiled=True),
            column,
            preferred_element_type=jnp.float32,
        )

    squared = filtered(multiply(masked), pattern).astype(jnp.bfloat16)
    cubic_term = filtered(multiply(squared), pattern)
    purified = 3.0 * squared.astype(jnp.float32) - 2.0 * cubic_term
    row_index = lax.axis_index("row") * row_count + jnp.arange(row_count, dtype=jnp.int32)
    col_index = lax.axis_index("col") * col_count + jnp.arange(col_count, dtype=jnp.int32)
    diagonal_sum = jnp.sum(jnp.where(row_index[:, None] == col_index[None, :], purified, 0.0))
    total_trace = lax.psum(diagonal_sum, ("row", "col"))
    occupation = total_trace / (row_count * lax.axis_size("row"))
    return (purified, occupation)


NEAR = (0, 1, 3)
LAST = 2


def piece(left, right):
    rows = right.shape[1]
    return jnp.dot(left[:, :rows], right[0], preferred_element_type=jnp.float32) + jnp.dot(
        left[:, rows:], right[1], preferred_element_type=jnp.float32
    )


def multiply(acc, left, right, fresh):
    if fresh:
        acc[...] = piece(left, right)
    else:
        acc[...] += piece(left, right)


def blocks(rows, columns, body):
    @pl.loop(0, (rows // B) * (columns // B))
    def _(block):
        a = block // (columns // B)
        b = block % (columns // B)
        body(
            a,
            b,
            (pl.ds(pl.multiple_of(a * B, B), B), pl.ds(pl.multiple_of(b * B, B), B)),
        )


def mask_kernel(pattern, density, out, kept_ref):
    rows, columns = out.shape
    for a in range(rows // B):
        for b in range(columns // B):
            part = (slice(a * B, (a + 1) * B), slice(b * B, (b + 1) * B))
            kept = pattern[a, b].astype(jnp.float32)
            kept_ref[a : a + 1, part[1]] = jnp.full((1, B), kept, jnp.float32)
            out[part] = (density[part].astype(jnp.float32) * kept).astype(jnp.bfloat16)


def square_early_kernel(where, own, pair, cross, *refs):
    rights = refs[:8]
    acc, panel, right, left_sem, right_sem = refs[8:]
    row, col = where[0], where[1]
    for i, ref in enumerate((own, pair, cross)):
        pltpu.make_async_copy(ref, panel.at[i], left_sem.at[i]).start()

    for k in range(8):
        slot = row ^ k
        pltpu.make_async_copy(rights[k], right.at[slot], right_sem.at[slot]).start()
    for i, d in enumerate(NEAR):
        slot = 2 * (col ^ d)
        pltpu.make_async_copy(panel.at[i], panel.at[i], left_sem.at[i]).wait()
        for t in range(2):
            there = right.at[slot + t]
            pltpu.make_async_copy(there, there, right_sem.at[slot + t]).wait()
        multiply(acc, panel.at[i], right.at[pl.ds(slot, 2)], i == 0)
    slot = 2 * (col ^ LAST)
    for t in range(2):
        there = right.at[slot + t]
        pltpu.make_async_copy(there, there, right_sem.at[slot + t]).wait()


def square_late_kernel(where, kept_ref, own, acc_in, right, far, *outs):
    squared_ref, upper, lower, sum_ref = outs
    row, col = where[0], where[1]
    rows, columns = squared_ref.shape
    total = acc_in[...] + piece(far, right.at[pl.ds(2 * (col ^ LAST), 2)])
    kept = kept_ref[...]
    sums = jnp.zeros((8, columns), jnp.float32)
    for a in range(rows // B):
        part = slice(a * B, (a + 1) * B)
        squared = (total[part] * kept[a : a + 1]).astype(jnp.bfloat16)
        squared_ref[part, :] = squared
        half, place = (upper, a * B) if a * B < rows // 2 else (lower, a * B - rows // 2)
        half[place : place + B, :] = squared
        term = squared.astype(jnp.float32) * own[part, :].astype(jnp.float32)
        sums -= 2.0 * jnp.sum(term.reshape(B // 8, 8, columns), axis=0)
    sum_ref[...] = sums[:, :B]
    for n in range(1, columns // B):
        sum_ref[...] += sums[:, n * B : (n + 1) * B]

    @pl.when(row // 2 == col)
    def _():
        same = lax.broadcasted_iota(jnp.int32, (B, B), 0) == lax.broadcasted_iota(
            jnp.int32, (B, B), 1
        )
        for a in range(rows // B):
            lanes = pl.ds(pl.multiple_of(row * rows - col * columns + a * B, B), B)
            squared = squared_ref[a * B : (a + 1) * B, lanes].astype(jnp.float32)
            term = jnp.where(same, 3.0 * squared, 0.0)
            sum_ref[...] += jnp.sum(term.reshape(B // 8, 8, B), axis=0)

    sum_ref[...] = jnp.broadcast_to(jnp.sum(sum_ref[...], keepdims=True), sum_ref.shape)


def add_kernel(left, right, out):
    out[...] = left[...] + right[...]


def add_planes_kernel(order, own, first, second, third, out):
    total = (own[...] + first[...]) + (second[...] + third[...])
    out[0, 0] = total[0, 0] / order


def turn_kernel(where, squared, same_ref, cross_ref):
    core = where[0] % 2
    half = same_ref.shape[0]

    def body(a, b, part):
        for out, h in ((same_ref, core), (cross_ref, 1 - core)):
            lanes = pl.ds(pl.multiple_of(h * half + b * B, B), B)
            out[part[1], part[0]] = squared[part[0], lanes].T

    blocks(half, half, body)


def own_square_kernel(where, own_pattern, *refs):
    patterns, (panel, other, far, far_other, out) = (own_pattern, *refs[:3]), refs[3:]
    row, col = where[0], where[1]
    core, chip = row % 2, row // 2
    rows = out.shape[0]
    d = col ^ chip
    for source, last, h in ((panel, far, core), (other, far_other, 1 - core)):
        total = None
        for left, right in [(panel.at[i], source.at[i]) for i in range(3)] + [(far, last)]:
            part = lax.dot_general(
                left[:rows, :],
                right[:rows, :],
                (((1,), (1,)), ((), ())),
                preferred_element_type=jnp.float32,
            )
            total = part if total is None else total + part
        for a in range(rows // B):
            for b in range(rows // B):
                place = h * (rows // B) + b
                kept = jnp.int32(0)
                for i, pattern in enumerate(patterns):
                    kept = jnp.where(d == i, pattern[a, place], kept)
                lanes = pl.ds(pl.multiple_of(h * rows + b * B, B), B)
                out[a * B : (a + 1) * B, lanes] = (
                    total[a * B : (a + 1) * B, b * B : (b + 1) * B] * kept.astype(jnp.float32)
                ).astype(jnp.bfloat16)


def late_sources(row, col):
    chip = row // 2
    place = col - (col > chip).astype(jnp.int32)
    sources = []
    for i in range(3):
        index = (place + 2 - i) % 3
        other = index + (index >= chip).astype(jnp.int32)
        sources.append(jnp.where(chip == col, col ^ (i + 1), other))
    return sources


def cubic_early_kernel(where, squared, local_square, right, acc):
    row, col = where[0], where[1]
    chip = row // 2
    multiply(acc, squared, right.at[pl.ds(2 * col, 2)], True)

    @pl.when(chip != col)
    def _():
        multiply(acc, local_square, right.at[pl.ds(2 * chip, 2)], False)


def side_piece(sides, right_all, source, core):
    return sum(
        jnp.dot(ref[...], right_all[2 * source + (core ^ u)], preferred_element_type=jnp.float32)
        for u, ref in enumerate(sides)
    )


def cubic_middle_kernel(where, acc_in, turn, right_all, same, cross, acc):
    row, col = where[0], where[1]
    source = late_sources(row, col)[0]

    @pl.when(row // 2 == col)
    def _():
        acc[...] = acc_in[...] + side_piece((same, cross), right_all, col ^ 1, row % 2)

    @pl.when(row // 2 != col)
    def _():
        acc[...] = acc_in[...] + piece(turn, right_all.at[pl.ds(2 * source, 2)])


def cubic_corner_kernel(away, where, acc_in, right_all, same, cross, acc):
    row, col = where[0], where[1]

    @pl.when(row // 2 == col)
    def _():
        acc[...] = acc_in[...] + side_piece((same, cross), right_all, col ^ away, row % 2)

    @pl.when(row // 2 != col)
    def _():
        acc[...] = acc_in[...]


def finish_rows(first, count, total, kept_ref, squared, out, block, sem):
    copies = []
    for a in range(count // B):
        part = slice(a * B, (a + 1) * B)
        whole = slice(first + a * B, first + (a + 1) * B)
        line = first // B + a
        wide = squared[whole, :].astype(jnp.float32)
        block[part, :] = 3.0 * wide - 2.0 * (total[part] * kept_ref[line : line + 1, :])
        copies.append(pltpu.make_async_copy(block.at[part], out.at[whole], sem.at[a]))
        copies[-1].start()
    for copy in copies:
        copy.wait()


def cubic_upper_kernel(where, kept_ref, squared, acc, turn, right_all, out, block, sem):
    row, col = where[0], where[1]
    count = turn.shape[0]
    source = late_sources(row, col)[1]

    @pl.when(row // 2 != col)
    def _():
        total = acc[:count] + piece(turn, right_all.at[pl.ds(2 * source, 2)])
        finish_rows(0, count, total, kept_ref, squared, out, block, sem)


def cubic_late_kernel(where, kept_ref, squared, acc, turn, right_all, upper, out, block, sem):
    del upper
    row, col = where[0], where[1]
    rows = acc.shape[0]
    count = turn.shape[0]
    source = late_sources(row, col)[1]

    @pl.when(row // 2 != col)
    def _():
        total = acc[count:] + piece(turn, right_all.at[pl.ds(2 * source, 2)])
        finish_rows(rows - count, count, total, kept_ref, squared, out, block, sem)

    @pl.when(row // 2 == col)
    def _():
        finish_rows(0, rows, acc, kept_ref, squared, out, block, sem)


ANYWHERE = pl.BlockSpec(memory_space=pl.ANY)
SCALARS = pl.BlockSpec(memory_space=pltpu.SMEM)
WHOLE = pl.BlockSpec(memory_space=pltpu.VMEM)
DMA = pltpu.SemaphoreType.DMA


def call(kernel, specs, args, outs, scratch, flops, moved, grant=16, out_spec=WHOLE, aliases=None):
    return pl.pallas_call(
        kernel,
        out_shape=outs,
        in_specs=specs,
        out_specs=jax.tree.map(lambda _: out_spec, outs),
        input_output_aliases=aliases or {},
        scratch_shapes=scratch,
        compiler_params=pltpu.CompilerParams(vmem_limit_bytes=grant << 20),
        cost_estimate=pl.CostEstimate(flops=flops, bytes_accessed=moved, transcendentals=0),
    )(*args)


def swap(x, k):
    return lax.ppermute(x, "row", [(i, i ^ k) for i in range(8)])


def column_gather(x):
    by_x = swap(x, 2)
    by_y = swap(x, 4)
    core = swap(x, 1)
    by_x_core = swap(by_x, 1)
    by_y_core = swap(by_y, 1)
    diagonal = swap(by_x, 4)
    return [x, core, by_x, by_x_core, by_y, by_y_core, diagonal, swap(diagonal, 1)]


def rotate(x, step):
    pairs = []
    for row in range(8):
        planes = [c for c in range(4) if c != row // 2]
        for i in range(3):
            pairs.append((row * 4 + planes[i], row * 4 + planes[(i + step) % 3]))
    return lax.ppermute(x, ("row", "col"), pairs)


def in_plane(x, source, target, u):
    pairs = []
    for col in range(4):
        for core in range(2):
            here = (col ^ source) * 2 + core
            there = (col ^ target) * 2 + (core ^ u)
            pairs.append((here * 4 + col, there * 4 + col))
    return lax.ppermute(x, ("row", "col"), pairs)


def to_corner(same, cross):
    by_y = [in_plane(same, 2, 0, 0), in_plane(cross, 2, 0, 1)]
    half_way = in_plane(cross, 3, 1, 0)
    by_x = [in_plane(same, 1, 0, 0), in_plane(cross, 1, 0, 1)]
    direct = in_plane(same, 3, 0, 0)
    return [*by_x, *by_y, direct, in_plane(half_way, 1, 0, 1)]


def local(density, pattern):
    rows, columns = density.shape
    row, col = lax.axis_index("row"), lax.axis_index("col")
    where = jnp.stack([row, col]).astype(jnp.int32)
    tile = jax.ShapeDtypeStruct((rows, columns), jnp.bfloat16)
    own, kept = call(
        mask_kernel,
        [SCALARS, WHOLE],
        (pattern, density),
        (tile, jax.ShapeDtypeStruct((8, columns), jnp.float32)),
        [],
        rows * columns,
        4 * rows * columns,
    )
    cross = lax.ppermute(own, "col", [(i, i ^ 3) for i in range(4)])
    pair = lax.ppermute(own, "col", [(i, i ^ 1) for i in range(4)])
    far = lax.ppermute(cross, "col", [(i, i ^ 1) for i in range(4)])
    patterns = [lax.ppermute(pattern, "col", [(i, i ^ k) for i in range(4)]) for k in (1, 2, 3)]
    rights = column_gather(own)

    flops = 2 * 2 * rows * rows * columns
    size = 2 * rows * columns
    wide = jax.ShapeDtypeStruct((rows, columns), jnp.float32)
    partial, panel, right = call(
        square_early_kernel,
        [SCALARS] + [ANYWHERE] * 11,
        (where, own, pair, cross, *rights),
        (
            wide,
            jax.ShapeDtypeStruct((3, rows, columns), jnp.bfloat16),
            jax.ShapeDtypeStruct((8, rows, columns), jnp.bfloat16),
        ),
        [DMA((3,)), DMA((8,))],
        3 * flops,
        24 * size,
    )
    other = swap(panel, 1)
    half = rows // 2
    half_tile = jax.ShapeDtypeStruct((half, columns), jnp.bfloat16)
    squared, upper, lower, sums = call(
        square_late_kernel,
        [SCALARS] + [WHOLE] * 5,
        (where, kept, own, partial, right, far),
        (tile, half_tile, half_tile, jax.ShapeDtypeStruct((8, B), jnp.float32)),
        [],
        flops,
        8 * size,
    )
    turn1 = rotate(squared, 1)
    turn2a = rotate(upper, 2)
    turn2b = rotate(lower, 2)
    total = sums

    def add(left, right):
        return call(
            add_kernel,
            [WHOLE] * 2,
            (left, right),
            jax.ShapeDtypeStruct(left.shape, left.dtype),
            [],
            left.size,
            12 * left.size,
            1,
        )

    for k in (1, 2, 4):
        total = add(total, swap(total, k))
    quarter = jax.ShapeDtypeStruct((rows, rows), jnp.bfloat16)
    turned = call(
        turn_kernel,
        [SCALARS, WHOLE],
        (where, squared),
        (quarter, quarter),
        [],
        0,
        2 * size,
    )
    sides = to_corner(*turned)
    local_square = call(
        own_square_kernel,
        [SCALARS] * 5 + [WHOLE] * 4,
        (where, pattern, *patterns, panel, other, far, swap(far, 1)),
        tile,
        [],
        4 * flops,
        9 * size,
        16,
    )
    cubic = call(
        cubic_early_kernel,
        [SCALARS] + [WHOLE] * 3,
        (where, squared, local_square, right),
        wide,
        [],
        2 * flops,
        8 * size,
        16,
    )
    cubic = call(
        cubic_middle_kernel,
        [SCALARS] + [WHOLE] * 5,
        (where, cubic, turn1, right, *sides[:2]),
        wide,
        [],
        flops,
        9 * size,
    )
    planes = [lax.ppermute(total, "col", [(i, i ^ k) for i in range(4)]) for k in (1, 2, 3)]
    occupation = call(
        functools.partial(add_planes_kernel, rows * lax.axis_size("row")),
        [WHOLE] * 4,
        (total, *planes),
        jax.ShapeDtypeStruct((1, 1), jnp.float32),
        [],
        3 * total.size,
        20 * total.size,
        1,
        SCALARS,
    )
    for away, quarters in ((3, sides[4:]), (2, sides[2:4])):
        cubic = call(
            functools.partial(cubic_corner_kernel, away),
            [SCALARS] + [WHOLE] * 4,
            (where, cubic, right, *quarters),
            wide,
            [],
            flops,
            8 * size,
        )
    blocks_out = [pltpu.VMEM((rows, columns), jnp.float32), DMA((rows // B,))]
    purified = call(
        cubic_upper_kernel,
        [SCALARS] + [WHOLE] * 5,
        (where, kept, squared, cubic, turn2a, right),
        wide,
        blocks_out,
        flops // 2,
        6 * size,
        out_spec=ANYWHERE,
    )
    purified = call(
        cubic_late_kernel,
        [SCALARS] + [WHOLE] * 5 + [ANYWHERE],
        (where, kept, squared, cubic, turn2b, right, purified),
        wide,
        blocks_out,
        flops // 2,
        6 * size,
        out_spec=ANYWHERE,
        aliases={6: 0},
    )
    return (purified, occupation.reshape(()))


def solution(mesh):
    placed = (P("row", "col"), P("row", "col"))
    body = local if (mesh.shape["row"], mesh.shape["col"]) == (8, 4) else general
    return jax.shard_map(
        body, mesh=mesh, in_specs=placed, out_specs=(P("row", "col"), P()), check_vma=False
    )
```
